32 devices in a mesh: dp: 8 (over z, core), blk: 4 (over y, x).
Axes of the slice: x: 2, y: 2, z: 4, core: 2. Of those that a mesh axis runs over, the one named last changes fastest.
Arguments:
- tokens: bfloat16 [16, 1024, 768], P('dp', 'blk'), may hold values from -6 to 6
- cotangent: bfloat16 [16, 1024, 768], P('dp', 'blk'), may hold values from -6 to 6
- lengths: int32 [16], P('dp'), may hold values from 256 to 1024, as said below
- w_query: bfloat16 [768, 768], replicated, may hold values from -0.21875 to 0.21875
- w_key: bfloat16 [768, 768], replicated, may hold values from -0.21875 to 0.21875
- w_value: bfloat16 [768, 768], replicated, may hold values from -0.21875 to 0.21875
- w_output: bfloat16 [768, 768], replicated, may hold values from -0.875 to 0.875
- w_gate: bfloat16 [768, 2048], replicated, may hold values from -0.21875 to 0.21875
- w_up: bfloat16 [768, 2048], replicated, may hold values from -0.21875 to 0.21875
- w_down: bfloat16 [2048, 768], replicated, may hold values from -0.125 to 0.125
- gain_attn: float32 [768], replicated, may hold values from 0.5 to 1.5
- gain_ffn: float32 [768], replicated, may hold values from 0.5 to 1.5
Outputs:
- output: bfloat16 [16, 1024, 768], P('dp', 'blk')
- grad_tokens: bfloat16 [16, 1024, 768], P('dp', 'blk')
- grad_query: float32 [768, 768], P('blk')
- grad_key: float32 [768, 768], P('blk')
- grad_value: float32 [768, 768], P('blk')
- grad_output: float32 [768, 768], P('blk')
- grad_gate: float32 [768, 2048], P('blk')
- grad_up: float32 [768, 2048], P('blk')
- grad_down: float32 [2048, 768], P('blk')
- grad_gain_attn: float32 [768], P('blk')
- grad_gain_ffn: float32 [768], P('blk')
The draws below stay inside these ranges and needn't reach their ends.
Inputs may be any that keep to these rules, and one draw needn't show every extreme that they name: `lengths`: each item holds 1024 or 256 valid tokens; among the 2 items on each index of dp at least one holds 1024.
All inputs are finite; a program needn't handle non-finite values.
Results may differ from the reference program's by a relative error of at most 0.02.
Values may be sent and summed in bfloat16 or wider, within the bound.
A program may use at most 256 MiB of HBM per device.

```python
import math
import jax
import jax.numpy as jnp
from jax import lax

D = 768
HEADS = 12
HD = 64
FF = 2048
SEQ = 1024
SHORT = 256
ITEMS = 2
ITEMS_ALL = 16


def draw_lengths(key, part):
    groups = ITEMS_ALL // ITEMS
    coins = jax.random.randint(jax.random.fold_in(key, 11), (groups, ITEMS), 0, 5)
    chosen = jax.random.randint(jax.random.fold_in(key, 12), (groups,), 0, ITEMS)
    forced = jnp.arange(ITEMS, dtype=jnp.int32)[None, :] == chosen[:, None]
    is_long = (coins < 3) | forced
    return jnp.where(is_long, SEQ, SHORT).astype(jnp.int32).reshape(groups * ITEMS)


def with_spikes(array, stream_key, source, target, blocks, factor):
    owner, partner = [(jnp.arange(array.shape[position]) // (array.shape[position] // blocks)).reshape([-1 if axis == position else 1 for axis in range(array.ndim)]) for position in (source, target)]
    chosen = jax.random.permutation(stream_key, blocks)[partner]
    strong = (owner == chosen) | (owner == (partner + blocks // 2) % blocks)
    return jnp.where(strong, factor * array, array)


def levels(rng, extent, pieces, smallest, largest):
    factor_of = 1.0
    for position, blocks in pieces:
        steps = jax.random.uniform(jax.random.fold_in(jax.random.fold_in(rng, 6), position), (blocks,), jnp.float32, smallest / len(pieces), largest / len(pieces))
        factor_of = factor_of * jnp.repeat(jnp.exp(steps), extent[position] // blocks).reshape((-1,) + (1,) * (len(extent) - 1 - position))
    return factor_of


def noise(key, extent, scale, reach, shards=(), kind=jnp.bfloat16):
    values = jax.random.normal(key, extent, jnp.float32) * scale
    if len(shards) > 0:
        values = levels(key, extent, shards, -0.22, 0.18) * values
    return jnp.clip(values, min=-reach, max=reach).astype(kind)


def bell_draw_with(own_key, dims, spread, bound, split, heavy, held_as=jnp.bfloat16):
    entries = spread * jax.random.normal(own_key, dims, jnp.float32)
    if split:
        entries = entries * levels(own_key, dims, split, -0.22, 0.18)
    return jnp.clip(with_spikes(entries, jax.random.fold_in(own_key, 3), *heavy), -bound, bound).astype(held_as)


def setup_inputs(seed: int = 0) -> dict:
    splits = jax.random.split(jax.random.key(seed), 13)
    tokens = noise(splits[0], (ITEMS_ALL, SEQ, D), 1.0, 6.0, ((0, 8), (1, 4)))
    cotangent = bell_draw_with(splits[1], (ITEMS_ALL, SEQ, D), 1.0, 6.0, ((0, 8), (1, 4)), (0, 2, 8, 2.0))
    lengths = draw_lengths(jax.random.fold_in(splits[12], 71), 0)
    w_query = noise(splits[3], (D, D), D ** -0.5, 0.21875)
    w_key = noise(splits[4], (D, D), D ** -0.5, 0.21875)
    w_value = noise(splits[5], (D, D), D ** -0.5, 0.21875)
    w_output = noise(splits[6], (D, D), (D // 16) ** -0.5, 0.875)
    w_gate = noise(splits[7], (D, FF), D ** -0.5, 0.21875)
    w_up = noise(splits[8], (D, FF), D ** -0.5, 0.21875)
    w_down = noise(splits[9], (FF, D), FF ** -0.5, 0.125)
    gain_attn = jnp.clip(1.0 + 0.1 * jax.random.normal(splits[10], (D,), jnp.float32), 0.5, 1.5)
    gain_ffn = jnp.clip(1.0 + 0.1 * jax.random.normal(splits[11], (D,), jnp.float32), 0.5, 1.5)
    return dict(tokens=tokens, cotangent=cotangent, lengths=lengths, w_query=w_query, w_key=w_key, w_value=w_value, w_output=w_output, w_gate=w_gate, w_up=w_up, w_down=w_down, gain_attn=gain_attn, gain_ffn=gain_ffn)


epsilon = 1e-05
masked_value = -1e+30
highest = lax.Precision.HIGHEST

@jax.custom_vjp
def low(v):
    return lax.optimization_barrier(v.astype(jnp.bfloat16)).astype(jnp.float32)

@jax.custom_vjp
def low_back(v):
    return v

def low_keep(v):
    return (low(v), None)

def low_pass(kept, grad):
    return (grad,)

def back_keep(v):
    return (v, None)

def back_low(kept, grad):
    return (low(grad),)
low.defvjp(low_keep, low_pass)
low_back.defvjp(back_keep, back_low)

def matmul_hi(left, right):
    return jnp.dot(left, right, precision=highest)

def rms_scale(values, gain):
    return values * lax.rsqrt(lax.optimization_barrier(jnp.mean(values * values, axis=-1, keepdims=True)) + epsilon) * gain

def tables(positions, head_dim):
    half_dim = head_dim // 2
    frequency = jnp.exp(jnp.arange(half_dim, dtype=jnp.float32) * (-2.0 * math.log(10000.0) / head_dim))
    angles = positions[:, None] * frequency[None, :]
    return (jnp.cos(angles), jnp.sin(angles))

def rotate(tensor, cosine_table, sine_table):
    half_dim = tensor.shape[-1] // 2
    first = tensor[..., :half_dim]
    second = tensor[..., half_dim:]
    cosine_b = cosine_table[:, None, :]
    sine_b = sine_table[:, None, :]
    return jnp.concatenate([first * cosine_b - second * sine_b, first * sine_b + second * cosine_b], axis=-1)

def block_forward(incoming, weights, valid_rows, cosine_table, sine_table, allowed):
    w_query, w_key, w_value, w_output, w_gate, w_up, w_down, gain_attn, gain_ffn = weights
    normed_one = low(rms_scale(incoming, gain_attn))
    query = low(rotate(low_back(matmul_hi(normed_one, w_query)).reshape(SEQ, HEADS, HD), cosine_table, sine_table))
    keys_all = low(rotate(low_back(matmul_hi(normed_one, w_key)).reshape(SEQ, HEADS, HD), cosine_table, sine_table))
    values_all = low_back(low(matmul_hi(normed_one, w_value))).reshape(SEQ, HEADS, HD)
    scores = low_back(jnp.einsum('qhd,khd->hqk', query, keys_all, precision=highest) * HD ** (-0.5))
    scores = jnp.where(allowed[None], scores, masked_value)
    softmax_w = low(jax.nn.softmax(scores, axis=-1))
    attended = jnp.einsum('hqk,khd->qhd', softmax_w, values_all, precision=highest).reshape(SEQ, D)
    attended = low_back(low(attended))
    middle = incoming + low_back(matmul_hi(attended, w_output))
    normed_two = low(rms_scale(middle, gain_ffn))
    gate_pre = low_back(matmul_hi(normed_two, w_gate))
    up_pre = low_back(matmul_hi(normed_two, w_up))
    hidden = low(jax.nn.silu(gate_pre) * up_pre)
    return (middle + low_back(matmul_hi(hidden, w_down))) * valid_rows

def reference(tokens, cotangent, lengths, w_query, w_key, w_value, w_output, w_gate, w_up, w_down, gain_attn, gain_ffn):
    weights = tuple((weight.astype(jnp.float32) for weight in (w_query, w_key, w_value, w_output, w_gate, w_up, w_down, gain_attn, gain_ffn)))
    positions = jnp.arange(SEQ, dtype=jnp.int32)
    cosine_table, sine_table = tables(positions.astype(jnp.float32), HD)
    allowed = positions[None, :] <= positions[:, None]

    def one_item(running, item_data):
        item_tokens, item_cot, item_length = item_data
        valid_rows = (positions < item_length).astype(jnp.float32)[:, None]

        def forward(incoming, *params):
            return block_forward(incoming, params, valid_rows, cosine_table, sine_table, allowed)
        result, pullback = jax.vjp(forward, item_tokens.astype(jnp.float32), *weights)
        gradients = pullback(item_cot.astype(jnp.float32))
        running = tuple((running_sum + gradient for running_sum, gradient in zip(running, gradients[1:])))
        return (running, (result.astype(jnp.bfloat16), gradients[0].astype(jnp.bfloat16)))
    zero_sums = tuple((jnp.zeros(weight.shape, jnp.float32) for weight in weights))
    running, (outputs, input_grads) = lax.scan(one_item, zero_sums, (tokens, cotangent, lengths))
    return (outputs, input_grads, running[0], running[1], running[2], running[3], running[4], running[5], running[6], running[7], running[8])
```

```python
import functools
import math

import jax
import jax.numpy as jnp
from jax import lax
from jax.experimental import pallas as pl
from jax.experimental.pallas import tpu as pltpu
from jax.sharding import PartitionSpec as P

HEADS = 12


epsilon = 1e-05
masked_value = -1e30


def shifted(value, axis, by):
    size = lax.axis_size(axis)
    pairs = [(i, i + by) for i in range(size) if 0 <= i + by < size]
    return lax.ppermute(value, axis, pairs)


def tables(positions, head_dim):
    half_dim = head_dim // 2
    frequency = jnp.exp(
        jnp.arange(half_dim, dtype=jnp.float32) * (-2.0 * math.log(10000.0) / head_dim)
    )
    angles = positions[:, None] * frequency[None, :]
    return (jnp.cos(angles), jnp.sin(angles))


def rotate(tensor, cosine_table, sine_table):
    half_dim = tensor.shape[-1] // 2
    first = tensor[..., :half_dim]
    second = tensor[..., half_dim:]
    cosine_b = cosine_table[:, None, :]
    sine_b = sine_table[:, None, :]
    return jnp.concatenate(
        [first * cosine_b - second * sine_b, first * sine_b + second * cosine_b], axis=-1
    )


def contract_rows(left, right):
    return lax.dot_general(
        left, right, (((0,), (0,)), ((), ())), preferred_element_type=jnp.float32
    )


def times_transposed(left, right):
    return lax.dot_general(
        left, right, (((1,), (1,)), ((), ())), preferred_element_type=jnp.float32
    )


def band_layer(
    tokens,
    cotangent,
    lengths,
    w_query,
    w_key,
    w_value,
    w_output,
    w_gate,
    w_up,
    w_down,
    gain_attn,
    gain_ffn,
):
    item_count, band_len, model_width = tokens.shape
    head_count = HEADS
    head_dim = model_width // head_count
    band_count = lax.axis_size("blk")
    band_index = lax.axis_index("blk")
    seq_len = band_len * band_count
    row_count = item_count * band_len
    score_scale = head_dim ** (-0.5)
    positions = band_index * band_len + jnp.arange(band_len, dtype=jnp.int32)
    valid_rows = (positions[None, :] < lengths[:, None]).astype(jnp.float32).reshape(row_count, 1)
    cosine_table, sine_table = tables(positions.astype(jnp.float32), head_dim)
    key_positions = jnp.arange(seq_len, dtype=jnp.int32)
    allowed = key_positions[None, :] <= positions[:, None]
    incoming = tokens.astype(jnp.float32).reshape(row_count, model_width)
    inv_one = lax.rsqrt(jnp.mean(incoming * incoming, axis=-1, keepdims=True) + epsilon)
    normed_one = (incoming * inv_one * gain_attn).astype(jnp.bfloat16)
    query = rotate(
        jnp.dot(normed_one, w_query, preferred_element_type=jnp.float32).reshape(
            item_count, band_len, head_count, head_dim
        ),
        cosine_table,
        sine_table,
    ).astype(jnp.bfloat16)
    key_own = rotate(
        jnp.dot(normed_one, w_key, preferred_element_type=jnp.float32).reshape(
            item_count, band_len, head_count, head_dim
        ),
        cosine_table,
        sine_table,
    ).astype(jnp.bfloat16)
    value_own = jnp.dot(normed_one, w_value, preferred_element_type=jnp.float32).astype(
        jnp.bfloat16
    )
    pair = jnp.concatenate(
        [
            key_own.reshape(item_count, band_len, model_width),
            value_own.reshape(item_count, band_len, model_width),
        ],
        axis=-1,
    )
    buffer = jnp.zeros((item_count, band_count, band_len, 2 * model_width), jnp.bfloat16)
    buffer = lax.dynamic_update_slice_in_dim(buffer, pair[:, None], band_index, 1)

    def cycle_step(turn_index, state):
        carried, buffer = state
        carried = shifted(carried, "blk", 1)
        source = band_index - turn_index
        placed = lax.dynamic_update_slice_in_dim(
            buffer, carried[:, None], jnp.maximum(source, 0), 1
        )
        buffer = jnp.where(source >= 0, placed, buffer)
        return (carried, buffer)

    _, buffer = lax.fori_loop(1, band_count, cycle_step, (pair, buffer))
    whole = buffer.reshape(item_count, seq_len, 2 * model_width)
    keys_all = whole[..., :model_width].reshape(item_count, seq_len, head_count, head_dim)
    values_all = whole[..., model_width:].reshape(item_count, seq_len, head_count, head_dim)
    scores = (
        jnp.einsum("iqhd,ikhd->ihqk", query, keys_all, preferred_element_type=jnp.float32)
        * score_scale
    )
    scores = jnp.where(allowed[None, None], scores, masked_value)
    highest_s = jnp.max(scores, axis=-1, keepdims=True)
    expo = jnp.exp(scores - highest_s)
    totals = jnp.sum(expo, axis=-1, keepdims=True)
    softmax_w = expo / totals
    attended = jnp.einsum(
        "ihqk,ikhd->iqhd",
        softmax_w.astype(jnp.bfloat16),
        values_all,
        preferred_element_type=jnp.float32,
    )
    attended = attended.astype(jnp.bfloat16).reshape(row_count, model_width)
    middle = incoming + jnp.dot(attended, w_output, preferred_element_type=jnp.float32)
    inv_two = lax.rsqrt(jnp.mean(middle * middle, axis=-1, keepdims=True) + epsilon)
    normed_two = (middle * inv_two * gain_ffn).astype(jnp.bfloat16)
    gate_pre = jnp.dot(normed_two, w_gate, preferred_element_type=jnp.float32)
    up_pre = jnp.dot(normed_two, w_up, preferred_element_type=jnp.float32)
    sigmoid_g = jax.nn.sigmoid(gate_pre)
    silu_g = gate_pre * sigmoid_g
    hidden = (silu_g * up_pre).astype(jnp.bfloat16)
    ffn_out = jnp.dot(hidden, w_down, preferred_element_type=jnp.float32)
    result = (middle + ffn_out) * valid_rows
    output = result.astype(jnp.bfloat16).reshape(item_count, band_len, model_width)
    grad_res = cotangent.astype(jnp.float32).reshape(row_count, model_width) * valid_rows
    grad_ffn = grad_res.astype(jnp.bfloat16)
    grad_down = contract_rows(hidden, grad_ffn)
    grad_hidden = times_transposed(grad_ffn, w_down)
    grad_gate_pre = (
        grad_hidden * up_pre * (sigmoid_g * (1.0 + gate_pre * (1.0 - sigmoid_g)))
    ).astype(jnp.bfloat16)
    grad_up_pre = (grad_hidden * silu_g).astype(jnp.bfloat16)
    grad_gate = contract_rows(normed_two, grad_gate_pre)
    grad_up = contract_rows(normed_two, grad_up_pre)
    grad_normed_two = times_transposed(grad_gate_pre, w_gate) + times_transposed(grad_up_pre, w_up)
    grad_gain_ffn = jnp.sum(grad_normed_two * middle * inv_two, axis=0)
    scaled_two = grad_normed_two * gain_ffn
    grad_middle = grad_res + inv_two * (
        scaled_two
        - middle * inv_two * inv_two * jnp.mean(scaled_two * middle, axis=-1, keepdims=True)
    )
    grad_branch = grad_middle.astype(jnp.bfloat16)
    grad_output = contract_rows(attended, grad_branch)
    grad_attended = (
        times_transposed(grad_branch, w_output)
        .astype(jnp.bfloat16)
        .reshape(item_count, band_len, head_count, head_dim)
    )
    again = (
        jnp.einsum("iqhd,ikhd->ihqk", query, keys_all, preferred_element_type=jnp.float32)
        * score_scale
    )
    again = jnp.where(allowed[None, None], again, masked_value)
    probable = jnp.exp(again - highest_s) / totals
    grad_probs = jnp.einsum(
        "iqhd,ikhd->ihqk", grad_attended, values_all, preferred_element_type=jnp.float32
    )
    row_delta = jnp.sum(probable * grad_probs, axis=-1, keepdims=True)
    grad_scores = (probable * (grad_probs - row_delta)).astype(jnp.bfloat16)
    grad_query = (
        jnp.einsum("ihqk,ikhd->iqhd", grad_scores, keys_all, preferred_element_type=jnp.float32)
        * score_scale
    )
    grad_values = jnp.einsum(
        "ihqk,iqhd->ikhd",
        probable.astype(jnp.bfloat16),
        grad_attended,
        preferred_element_type=jnp.float32,
    )
    grad_keys = (
        jnp.einsum("ihqk,iqhd->ikhd", grad_scores, query, preferred_element_type=jnp.float32)
        * score_scale
    )
    grad_pair = jnp.concatenate(
        [
            grad_keys.reshape(item_count, seq_len, model_width),
            grad_values.reshape(item_count, seq_len, model_width),
        ],
        axis=-1,
    )
    blocks = grad_pair.reshape(item_count, band_count, band_len, 2 * model_width)
    empty_block = jnp.zeros((item_count, band_len, 2 * model_width), jnp.float32)

    def block_of(index):
        picked = lax.dynamic_index_in_dim(blocks, jnp.maximum(index, 0), 1, keepdims=False)
        return jnp.where(index >= 0, picked, empty_block)

    def cycle_back(turn_index, carried):
        carried = shifted(carried.astype(jnp.bfloat16), "blk", -1).astype(carried.dtype)
        return carried + block_of(band_index - (band_count - 1) + turn_index)

    own_grads = lax.fori_loop(1, band_count, cycle_back, block_of(band_index - (band_count - 1)))
    grad_key_own = own_grads[..., :model_width].reshape(item_count, band_len, head_count, head_dim)
    grad_value_raw = (
        own_grads[..., model_width:].astype(jnp.bfloat16).reshape(row_count, model_width)
    )
    grad_key_raw = (
        rotate(grad_key_own, cosine_table, -sine_table)
        .astype(jnp.bfloat16)
        .reshape(row_count, model_width)
    )
    grad_query_raw = (
        rotate(grad_query, cosine_table, -sine_table)
        .astype(jnp.bfloat16)
        .reshape(row_count, model_width)
    )
    grad_wquery = contract_rows(normed_one, grad_query_raw)
    grad_wkey = contract_rows(normed_one, grad_key_raw)
    grad_wvalue = contract_rows(normed_one, grad_value_raw)
    grad_normed_one = (
        times_transposed(grad_query_raw, w_query)
        + times_transposed(grad_key_raw, w_key)
        + times_transposed(grad_value_raw, w_value)
    )
    grad_gain_attn = jnp.sum(grad_normed_one * incoming * inv_one, axis=0)
    scaled_one = grad_normed_one * gain_attn
    grad_incoming = grad_middle + inv_one * (
        scaled_one
        - incoming * inv_one * inv_one * jnp.mean(scaled_one * incoming, axis=-1, keepdims=True)
    )
    grad_tokens = grad_incoming.astype(jnp.bfloat16).reshape(item_count, band_len, model_width)
    summed = (
        lax.psum_scatter(
            grad_wquery.astype(jnp.bfloat16), "blk", scatter_dimension=0, tiled=True
        ).astype(jnp.float32),
        lax.psum_scatter(
            grad_wkey.astype(jnp.bfloat16), "blk", scatter_dimension=0, tiled=True
        ).astype(jnp.float32),
        lax.psum_scatter(
            grad_wvalue.astype(jnp.bfloat16), "blk", scatter_dimension=0, tiled=True
        ).astype(jnp.float32),
        lax.psum_scatter(
            grad_output.astype(jnp.bfloat16), "blk", scatter_dimension=0, tiled=True
        ).astype(jnp.float32),
        lax.psum_scatter(
            grad_gate.astype(jnp.bfloat16), "blk", scatter_dimension=0, tiled=True
        ).astype(jnp.float32),
        lax.psum_scatter(
            grad_up.astype(jnp.bfloat16), "blk", scatter_dimension=0, tiled=True
        ).astype(jnp.float32),
        lax.psum_scatter(
            grad_down.astype(jnp.bfloat16), "blk", scatter_dimension=0, tiled=True
        ).astype(jnp.float32),
        lax.psum_scatter(
            grad_gain_attn.astype(jnp.bfloat16), "blk", scatter_dimension=0, tiled=True
        ).astype(jnp.float32),
        lax.psum_scatter(
            grad_gain_ffn.astype(jnp.bfloat16), "blk", scatter_dimension=0, tiled=True
        ).astype(jnp.float32),
    )
    summed = (
        lax.psum(summed[0].astype(jnp.bfloat16), "dp").astype(jnp.float32),
        lax.psum(summed[1].astype(jnp.bfloat16), "dp").astype(jnp.float32),
        lax.psum(summed[2].astype(jnp.bfloat16), "dp").astype(jnp.float32),
        lax.psum(summed[3].astype(jnp.bfloat16), "dp").astype(jnp.float32),
        lax.psum(summed[4].astype(jnp.bfloat16), "dp").astype(jnp.float32),
        lax.psum(summed[5].astype(jnp.bfloat16), "dp").astype(jnp.float32),
        lax.psum(summed[6].astype(jnp.bfloat16), "dp").astype(jnp.float32),
        lax.psum(summed[7].astype(jnp.bfloat16), "dp").astype(jnp.float32),
        lax.psum(summed[8].astype(jnp.bfloat16), "dp").astype(jnp.float32),
    )
    return (
        output,
        grad_tokens,
        summed[0],
        summed[1],
        summed[2],
        summed[3],
        summed[4],
        summed[5],
        summed[6],
        summed[7],
        summed[8],
    )


MESH = pl.DeviceIdType.MESH
CORES = 2
CHIPS = 4


def place():
    dp = lax.axis_index("dp")
    return dp, lax.axis_index("blk"), lax.rem(dp, CORES)


def near(dp, blk, core=0, chip=0, line=0):
    flip = core + CORES * line
    return {"dp": dp ^ flip if flip else dp, "blk": blk ^ chip if chip else blk}


def greet(dp, blk, flips):
    barrier = pltpu.get_barrier_semaphore()
    for flip in flips:
        pl.semaphore_signal(barrier, inc=1, device_id=near(dp, blk, *flip), device_id_type=MESH)
    pl.semaphore_wait(barrier, len(flips))


def remote(src, dst, send, recv, where):
    return pltpu.make_async_remote_copy(
        src_ref=src, dst_ref=dst, send_sem=send, recv_sem=recv, device_id=where, device_id_type=MESH
    )


def part(start, size):
    return pl.ds(pl.multiple_of(start, size), size)


PLANE = [(core, chip, 0) for chip in range(CHIPS) for core in range(CORES) if core or chip]


class Gather:
    SEMS = [(2,), (4, 2), (4,), (4,), (4,)]

    def __init__(self, band, buf, sems):
        self.band, self.buf = band, buf
        self.own, self.send, self.recv, self.fsend, self.frecv = sems
        self.dp, self.blk, self.core = place()
        self.rows = band.shape[1]
        self.half = self.rows // 2
        self.mine = (self.blk // 2) == self.core

    def out(self, r, h):
        target = self.blk ^ r
        return remote(
            self.band.at[lax.rem(target, 2), pl.ds(h * self.half, self.half)],
            self.buf.at[part(self.blk * self.rows + h * self.half, self.half)],
            self.send.at[r, h],
            self.recv.at[r],
            {"dp": self.dp - self.core + h, "blk": target},
        )

    def across(self, r):
        rows = self.buf.at[part((self.blk ^ r) * self.rows + self.core * self.half, self.half)]
        return remote(rows, rows, self.fsend.at[r], self.frecv.at[r], near(self.dp, self.blk, 1))

    def keep(self):
        rows = self.buf.at[part(self.blk * self.rows, self.rows)]
        src = self.band.at[lax.rem(self.blk, 2)]
        return (
            pltpu.make_async_copy(src, rows, self.own.at[0]),
            remote(src, rows, self.fsend.at[0], self.frecv.at[0], near(self.dp, self.blk, 1)),
        )

    def sends(self, r):
        return ((self.blk ^ r) // 2) == self.core

    def start(self):
        for r in (3, 1, 2):

            @pl.when(self.sends(r))
            def _():
                for h in range(2):
                    self.out(r, h).start()

        @pl.when(self.mine)
        def _():
            for copy in self.keep():
                copy.start()

    def forward(self):
        for r in (1, 2, 3):
            self.out(r, 0).wait_recv()
            self.across(r).start()

    def finish(self):
        @pl.when(self.mine)
        def _():
            here, there = self.keep()
            here.wait()
            there.wait_send()

        @pl.when(jnp.logical_not(self.mine))
        def _():
            self.keep()[1].wait_recv()

        for r in (1, 2, 3):
            self.across(r).wait()

    def drain(self):
        for r in (1, 2, 3):

            @pl.when(self.sends(r))
            def _():
                for h in range(2):
                    self.out(r, h).wait_send()


class Return:
    SEMS = [(1,), (4,), (2, 2)]

    def __init__(self, src, buf, sems):
        self.src, self.buf = src, buf
        self.own, self.send, self.recv = sems
        self.dp, self.blk, self.core = place()
        self.half = src.shape[1]
        self.home = self.blk // 2

    def out(self, r):
        chip = self.blk ^ r
        return remote(
            self.src.at[chip],
            self.buf.at[lax.rem(self.blk, 2), part(self.core * self.half, self.half)],
            self.send.at[r],
            self.recv.at[lax.rem(self.blk, 2), self.core],
            {"dp": self.dp - self.core + self.home, "blk": chip},
        )

    def keep(self):
        return pltpu.make_async_copy(
            self.src.at[self.blk],
            self.buf.at[lax.rem(self.blk, 2), part(self.core * self.half, self.half)],
            self.own.at[0],
        )

    def start(self):
        for r in (3, 1, 2):
            self.out(r).start()

        @pl.when(self.home == self.core)
        def _():
            self.keep().start()

        @pl.when(self.home != self.core)
        def _():
            self.out(0).start()

    def finish(self):
        for i in range(2):
            for h in range(2):
                local = (self.core * 2 + i == self.blk) & (self.core == h)

                @pl.when(jnp.logical_not(local))
                def _():
                    remote(
                        self.src.at[0],
                        self.buf.at[i, pl.ds(h * self.half, self.half)],
                        self.send.at[0],
                        self.recv.at[i, h],
                        near(self.dp, self.blk, 1),
                    ).wait_recv()

        @pl.when(self.home == self.core)
        def _():
            self.keep().wait()

        @pl.when(self.home != self.core)
        def _():
            self.out(0).wait_send()

        for r in (1, 2, 3):
            self.out(r).wait_send()


def dma_sems(shapes):
    return [pltpu.SemaphoreType.DMA(shape) for shape in shapes]


def vmem_specs(count):
    return [pl.BlockSpec(memory_space=pltpu.VMEM)] * count


def link_params(ident):
    return pltpu.CompilerParams(
        collective_id=ident, has_side_effects=True, vmem_limit_bytes=56 << 20
    )


def gather_kernel(tokens, cotangent, tokens_out, cotangent_out, tbuf, cbuf, *sems):
    dp, blk, core = place()
    greet(dp, blk, PLANE)
    count = len(Gather.SEMS)
    moves = [Gather(tokens, tbuf, sems[:count]), Gather(cotangent, cbuf, sems[count:])]
    for step in ("start", "forward", "finish", "drain"):
        for move in moves:
            getattr(move, step)()
    tokens_out[...] = tbuf[...]
    cotangent_out[...] = cbuf[...]


def gathered(tokens, cotangent):
    items, band, width = tokens.shape
    whole = jax.ShapeDtypeStruct((band * CHIPS, width), tokens.dtype)
    return pl.pallas_call(
        gather_kernel,
        out_shape=(whole, whole),
        in_specs=vmem_specs(2),
        out_specs=tuple(vmem_specs(2)),
        scratch_shapes=[pltpu.VMEM(whole.shape, whole.dtype)] * 2 + dma_sems(Gather.SEMS * 2),
        compiler_params=link_params(0),
    )(tokens, cotangent)


def swap_kernel(src, dst, out, buf, sems):
    dp, blk, core = place()
    greet(dp, blk, [(1, 0, 0)])
    out[...] = src[...]
    copy = remote(out, buf, sems.at[0], sems.at[1], near(dp, blk, 1))
    copy.start()
    copy.wait()
    dst[...] = buf[...]


def swapped(value, ident):
    return pl.pallas_call(
        swap_kernel,
        out_shape=jax.ShapeDtypeStruct(value.shape, value.dtype),
        in_specs=vmem_specs(1),
        out_specs=pl.BlockSpec(memory_space=pltpu.VMEM),
        scratch_shapes=[pltpu.VMEM(value.shape, value.dtype)] * 2 + dma_sems([(2,)]),
        compiler_params=link_params(ident),
    )(value)


class Chunk:
    SEMS = [(2, 2, 2), (2, 2), (3, 2), (2,)]

    def __init__(self, src, first, second, total, line, fin, sems, turned=False):
        self.src, self.first, self.second, self.total, self.line, self.fin = (
            src, first, second, total, line, fin,
        )
        self.s1, self.s2, self.sz, self.sc = sems
        self.turned = turned
        self.dp, self.blk, self.core = place()
        self.z = self.dp // CORES
        self.outer = (self.z == 0) | (self.z == 3)

    def piece(self, chip, h):
        if self.turned:
            rows, cols = self.src.shape[0] // 2, self.src.shape[1] // CHIPS
            return self.src.at[pl.ds(h * rows, rows), part(chip * cols, cols)]
        rows = self.src.shape[0] // CHIPS // 2
        return self.src.at[part(chip * 2 * rows + h * rows, rows)]

    def ways(self, h):
        return (1, 2) if h == 0 else (2, 1)

    def step1(self, h, n):
        near_way, far_way = self.ways(h)
        chip = self.blk ^ near_way ^ (far_way if n else 0)
        return remote(
            self.piece(chip, h), self.first.at[h, n], self.s1.at[0, h, n], self.s1.at[1, h, n],
            near(self.dp, self.blk, 0, near_way),
        )

    def step2(self, h):
        return remote(
            self.first.at[h, 1], self.second.at[h], self.s2.at[0, h], self.s2.at[1, h],
            near(self.dp, self.blk, 0, self.ways(h)[1]),
        )

    def hop(self, n):
        src = (self.total, self.line.at[0], self.fin.at[self.core])[n]
        dst = (self.line.at[0], self.line.at[1], self.fin.at[self.core])[n]
        return remote(
            src, dst, self.sz.at[n, 0], self.sz.at[n, 1],
            near(self.dp, self.blk, 0, 0, 3 if n == 1 else 1),
        )

    def cross(self):
        half = self.fin.at[self.core]
        return remote(half, half, self.sc.at[0], self.sc.at[1], near(self.dp, self.blk, 1))

    def stage0(self):
        for n in (1, 0):
            for h in range(2):
                self.step1(h, n).start()

    def stage1(self):
        for h in range(2):
            self.step1(h, 1).wait_recv()
            chip = self.blk ^ self.ways(h)[1]
            self.first[h, 1] = plus(self.first[h, 1], self.piece(chip, h)[...])
            self.step2(h).start()
        for h in range(2):
            self.step1(h, 0).wait_recv()

    def stage2(self):
        rows = self.second.shape[1]
        for h in range(2):
            self.step2(h).wait_recv()
            self.total[pl.ds(h * rows, rows)] = plus(
                plus(self.first[h, 0], self.piece(self.blk, h)[...], jnp.float32), self.second[h]
            )

        @pl.when(self.outer)
        def _():
            self.hop(0).start()

    def stage3(self):
        @pl.when(jnp.logical_not(self.outer))
        def _():
            self.hop(0).wait_recv()
            self.line[0] = plus(self.line[0], self.total[...])
            self.hop(1).start()

    def stage4(self):
        @pl.when(jnp.logical_not(self.outer))
        def _():
            self.hop(1).wait_recv()
            self.fin[self.core] = plus(self.line[0], self.line[1])
            self.hop(2).start()
            self.cross().start()

    def stage5(self):
        @pl.when(self.outer)
        def _():
            self.hop(2).wait_recv()
            self.cross().start()

    def stage6(self):
        self.cross().wait()
        for h in range(2):
            for n in range(2):
                self.step1(h, n).wait_send()
            self.step2(h).wait_send()

        @pl.when(self.outer)
        def _():
            self.hop(0).wait_send()

        @pl.when(jnp.logical_not(self.outer))
        def _():
            self.hop(1).wait_send()
            self.hop(2).wait_send()

    STAGES = 7

    def stage(self, n):
        getattr(self, "stage" + str(n))()


def plus(one, other, kind=jnp.bfloat16):
    return (one.astype(jnp.float32) + other.astype(jnp.float32)).astype(kind)


class Small:
    SEMS = [(2, 2), (3, 2)]

    def __init__(self, src, hold, sems):
        self.src, self.hold = src, hold
        self.sp, self.sz = sems
        self.dp, self.blk, self.core = place()
        self.z = self.dp // CORES
        self.outer = (self.z == 0) | (self.z == 3)

    def go(self, n):
        src = self.src if n == 0 else self.hold.at[2 * n - 1]
        flips = ((0, 1, 0), (0, 2, 0), (0, 0, 1), (0, 0, 3), (0, 0, 1))
        send, recv = (self.sp.at[n, 0], self.sp.at[n, 1]) if n < 2 else (self.sz.at[n - 2, 0], self.sz.at[n - 2, 1])
        if n == 4:
            src = self.hold.at[8]
        return remote(src, self.hold.at[8 if n == 4 else 2 * n], send, recv, near(self.dp, self.blk, *flips[n]))

    def stage0(self):
        self.go(0).start()

    def stage1(self):
        self.go(0).wait_recv()
        self.hold[1] = self.src[...] + self.hold[0]
        self.go(1).start()

    def stage2(self):
        self.go(1).wait_recv()
        self.hold[3] = self.hold[1] + self.hold[2]

        @pl.when(self.outer)
        def _():
            self.go(2).start()

    def stage3(self):
        @pl.when(jnp.logical_not(self.outer))
        def _():
            self.go(2).wait_recv()
            self.hold[5] = self.hold[3] + self.hold[4]
            self.go(3).start()

    def stage4(self):
        @pl.when(jnp.logical_not(self.outer))
        def _():
            self.go(3).wait_recv()
            self.hold[8] = self.hold[5] + self.hold[6]
            self.go(4).start()

    def stage5(self):
        @pl.when(self.outer)
        def _():
            self.go(4).wait_recv()

    def stage6(self):
        for n in range(2):
            self.go(n).wait_send()

        @pl.when(self.outer)
        def _():
            self.go(2).wait_send()

        @pl.when(jnp.logical_not(self.outer))
        def _():
            self.go(3).wait_send()
            self.go(4).wait_send()

    def stage(self, n):
        getattr(self, "stage" + str(n))()


REACH = PLANE + [(0, 0, 1), (0, 0, 3)]


def chunk_buffers(shape, turned):
    rows, cols = shape
    quarter = (rows, cols // CHIPS) if turned else (rows // CHIPS, cols)
    half = (quarter[0] // 2, quarter[1])
    return [(2, 2) + half, (2,) + half, quarter, (2,) + quarter, (2,) + quarter]


def sum_kernel(shapes, *refs):
    count = len(shapes)
    refs = list(refs)

    def take(n):
        got, refs[:] = refs[:n], refs[n:]
        return got

    srcs, (small, outs, backs) = take(count), take(3)
    fin_out, (small_out, out_band, back_band) = take(count), take(3)
    dp, blk, core = place()
    greet(dp, blk, REACH)
    chunks = []
    fins = []
    for src, turned in zip(srcs, shapes):
        first, second, total, line, fin = take(5)
        chunks.append(Chunk(src, first, second, total, line, fin, take(4), turned))
        fins.append(fin)
    (hold,) = take(1)
    chunks.append(Small(small, hold, take(2)))
    obuf, bbuf = take(2)
    moves = [Return(outs, obuf, take(3)), Return(backs, bbuf, take(3))]
    for move in moves:
        move.start()
    for tick in range(len(chunks) + Chunk.STAGES - 1):
        for n, chunk in enumerate(chunks):
            if 0 <= tick - n < Chunk.STAGES:
                chunk.stage(tick - n)
    for move in moves:
        move.finish()
    for fin, out in zip(fins, fin_out):
        out[...] = fin[...]
    small_out[...] = hold[8]
    out_band[...] = obuf[...]
    back_band[...] = bbuf[...]


def all_summed(grads, turned, small, outs, backs):
    buffers = [chunk_buffers(g.shape, t) for g, t in zip(grads, turned)]
    half = outs.shape[1]
    band = jax.ShapeDtypeStruct((2, 2 * half, outs.shape[2]), jnp.bfloat16)
    scratch = []
    for shapes in buffers:
        scratch += [pltpu.VMEM(s, jnp.bfloat16) for s in shapes] + dma_sems(Chunk.SEMS)
    scratch += [pltpu.VMEM((9,) + small.shape, jnp.float32)] + dma_sems(Small.SEMS)
    scratch += [pltpu.VMEM(band.shape, band.dtype)] * 2 + dma_sems(Return.SEMS * 2)
    return pl.pallas_call(
        functools.partial(sum_kernel, turned),
        out_shape=tuple(jax.ShapeDtypeStruct(s[4], jnp.bfloat16) for s in buffers)
        + (jax.ShapeDtypeStruct(small.shape, jnp.float32), band, band),
        in_specs=vmem_specs(len(grads) + 3),
        out_specs=tuple(vmem_specs(len(grads) + 3)),
        scratch_shapes=scratch,
        compiler_params=link_params(1),
    )(*grads, small, outs, backs)


def item_layer(
    tokens, cotangent, lengths, w_query, w_key, w_value, w_output, w_gate, w_up, w_down, gain_attn, gain_ffn
):
    dp, blk, core = place()
    item_count, band_len, width = tokens.shape
    seq_len = band_len * CHIPS
    heads = HEADS // CORES
    head_dim = width // HEADS
    half = heads * head_dim
    ff = w_gate.shape[1] // CORES
    low = jnp.bfloat16
    positions = blk * band_len + jnp.arange(band_len, dtype=jnp.int32)
    valid = (positions[None, :] < lengths[:, None])[:, :, None]
    x_low, g_ffn = gathered(tokens, jnp.where(valid, cotangent, jnp.zeros_like(cotangent)))
    cos_t, sin_t = tables(jnp.arange(seq_len).astype(jnp.float32), head_dim)
    scale = head_dim ** (-0.5)

    def cols(w):
        return lax.dynamic_slice_in_dim(w, core * half, half, 1)

    def ff_cols(w):
        w = w.reshape(width, CHIPS, CORES, ff // CHIPS)
        return lax.dynamic_index_in_dim(w, core, 2, keepdims=False).reshape(width, ff)

    def join(own, other, axis):
        return jnp.where(
            core == 0, jnp.concatenate([own, other], axis), jnp.concatenate([other, own], axis)
        )

    wq, wk, wv = cols(w_query), cols(w_key), cols(w_value)
    wg, wu = ff_cols(w_gate), ff_cols(w_up)
    wd = lax.dynamic_index_in_dim(
        w_down.reshape(CHIPS, CORES, ff // CHIPS, width), core, 1, keepdims=False
    ).reshape(ff, width)
    wo_rows = lax.dynamic_slice_in_dim(w_output, core * half, half, 0)
    x = x_low.astype(jnp.float32)
    inv_one = lax.rsqrt(jnp.mean(x * x, axis=-1, keepdims=True) + epsilon)
    n1 = (x * inv_one * gain_attn).astype(low)

    def dot(a, b):
        return jnp.dot(a, b, preferred_element_type=jnp.float32)

    q = rotate(dot(n1, wq).reshape(seq_len, heads, head_dim), cos_t, sin_t).astype(low)
    k = rotate(dot(n1, wk).reshape(seq_len, heads, head_dim), cos_t, sin_t).astype(low)
    v = dot(n1, wv).astype(low).reshape(seq_len, heads, head_dim)
    order = jnp.arange(seq_len)
    allowed = (order[None, :] <= order[:, None])[None]
    s = jnp.einsum("qhd,khd->hqk", q, k, preferred_element_type=jnp.float32) * scale
    s = jnp.where(allowed, s, masked_value)
    top = jnp.max(s, axis=-1, keepdims=True)
    e = jnp.exp(s - top)
    p = e / jnp.sum(e, axis=-1, keepdims=True)
    p_low = p.astype(low)
    att = jnp.einsum("hqk,khd->qhd", p_low, v, preferred_element_type=jnp.float32)
    att = att.astype(low).reshape(seq_len, half)
    att_all = join(att, swapped(att, 2), 1)
    middle = x + dot(att_all, w_output)
    inv_two = lax.rsqrt(jnp.mean(middle * middle, axis=-1, keepdims=True) + epsilon)
    n2 = (middle * inv_two * gain_ffn).astype(low)
    gate, up = dot(n2, wg), dot(n2, wu)
    sig = jax.nn.sigmoid(gate)
    silu = gate * sig
    hidden = (silu * up).astype(low)
    g_hidden = times_transposed(g_ffn, wd)
    g_gate = (g_hidden * up * (sig * (1.0 + gate * (1.0 - sig)))).astype(low)
    g_up = (g_hidden * silu).astype(low)
    grad_down = contract_rows(g_ffn, hidden).astype(low)
    grad_gate = contract_rows(n2, g_gate).astype(low)
    grad_up = contract_rows(n2, g_up).astype(low)
    out_part = dot(hidden, wd).astype(low)
    gn2_part = (times_transposed(g_gate, wg) + times_transposed(g_up, wu)).astype(low)
    out_sum = out_part.astype(jnp.float32) + swapped(out_part, 3).astype(jnp.float32)
    g_n2 = gn2_part.astype(jnp.float32) + swapped(gn2_part, 4).astype(jnp.float32)
    result = (middle + out_sum).astype(low)
    gain2 = jnp.sum(g_n2 * middle * inv_two, axis=0)
    a2 = g_n2 * gain_ffn
    g_mid = g_ffn.astype(jnp.float32) + inv_two * (
        a2 - middle * inv_two * inv_two * jnp.mean(a2 * middle, axis=-1, keepdims=True)
    )
    g_branch = g_mid.astype(low)
    grad_o = contract_rows(att_all, cols(g_branch)).astype(low)
    g_att = times_transposed(g_branch, wo_rows).astype(low).reshape(seq_len, heads, head_dim)
    g_p = jnp.einsum("qhd,khd->hqk", g_att, v, preferred_element_type=jnp.float32)
    delta = jnp.sum(p * g_p, axis=-1, keepdims=True)
    g_s = (p * (g_p - delta)).astype(low)
    g_q = jnp.einsum("hqk,khd->qhd", g_s, k, preferred_element_type=jnp.float32) * scale
    g_k = jnp.einsum("hqk,qhd->khd", g_s, q, preferred_element_type=jnp.float32) * scale
    g_v = jnp.einsum("hqk,qhd->khd", p_low, g_att, preferred_element_type=jnp.float32)
    g_v = g_v.astype(low).reshape(seq_len, half)
    g_k = rotate(g_k, cos_t, -sin_t).astype(low).reshape(seq_len, half)
    g_q = rotate(g_q, cos_t, -sin_t).astype(low).reshape(seq_len, half)
    grad_q = contract_rows(n1, g_q).astype(low)
    grad_k = contract_rows(n1, g_k).astype(low)
    grad_v = contract_rows(n1, g_v).astype(low)
    gn1_part = (times_transposed(g_q, wq) + times_transposed(g_k, wk) + times_transposed(g_v, wv)).astype(low)
    g_n1 = gn1_part.astype(jnp.float32) + swapped(gn1_part, 5).astype(jnp.float32)
    gain1 = jnp.sum(g_n1 * x * inv_one, axis=0)
    a1 = g_n1 * gain_attn
    g_x = g_mid + inv_one * (a1 - x * inv_one * inv_one * jnp.mean(a1 * x, axis=-1, keepdims=True))
    small = jnp.concatenate([gain1[None], gain2[None], jnp.zeros((6, width), jnp.float32)])

    def halves(t):
        t = t.astype(low).reshape(CHIPS, 2, band_len // 2, width)
        return lax.dynamic_index_in_dim(t, core, 1, keepdims=False)

    fins = all_summed(
        [grad_down, grad_gate, grad_up, grad_o, grad_q, grad_k, grad_v],
        [True] + [False] * 6,
        small, halves(result), halves(g_x),
    )
    down, gate_w, up_w, o_w, q_w, k_w, v_w, small, output, g_tokens = fins
    output = jnp.where(valid, output, jnp.zeros_like(output))

    def wide(t):
        return jnp.concatenate([t[0], t[1]], axis=1).astype(jnp.float32)

    def wide_ff(t):
        rows = t.shape[1]
        t = t.reshape(2, rows, CHIPS, ff // CHIPS).transpose(1, 2, 0, 3)
        return t.reshape(rows, 2 * ff).astype(jnp.float32)

    down = down.transpose(0, 2, 1).reshape(-1, width).astype(jnp.float32)
    gains = lax.dynamic_slice_in_dim(small, blk * (width // CHIPS), width // CHIPS, 1)
    return (
        output, g_tokens, wide(q_w), wide(k_w), wide(v_w), wide(o_w), wide_ff(gate_w), wide_ff(up_w),
        down, gains[0], gains[1],
    )


def solution(mesh):
    layer = item_layer if dict(mesh.shape) == {'dp': 8, 'blk': 4} else band_layer
    placed = (
        P("dp", "blk", None),
        P("dp", "blk", None),
        P("dp"),
        P(),
        P(),
        P(),
        P(),
        P(),
        P(),
        P(),
        P(),
        P(),
    )
    return jax.shard_map(
        layer,
        mesh=mesh,
        in_specs=placed,
        out_specs=(
            P("dp", "blk", None),
            P("dp", "blk", None),
            P("blk", None),
            P("blk", None),
            P("blk", None),
            P("blk", None),
            P("blk", None),
            P("blk", None),
            P("blk", None),
            P("blk"),
            P("blk"),
        ),
        check_vma=False,
    )
```

```python
import functools
import math

import jax
import jax.numpy as jnp
import numpy as np
from jax import lax
from jax.experimental import pallas as pl
from jax.experimental.pallas import tpu as pltpu
from jax.sharding import PartitionSpec as P

HEADS = 12


epsilon = 1e-05
masked_value = -1e30


def shifted(value, axis, by):
    size = lax.axis_size(axis)
    pairs = [(i, i + by) for i in range(size) if 0 <= i + by < size]
    return lax.ppermute(value, axis, pairs)


def tables(positions, head_dim):
    half_dim = head_dim // 2
    frequency = jnp.exp(
        jnp.arange(half_dim, dtype=jnp.float32) * (-2.0 * math.log(10000.0) / head_dim)
    )
    angles = positions[:, None] * frequency[None, :]
    return (jnp.cos(angles), jnp.sin(angles))


def rotate(tensor, cosine_table, sine_table):
    half_dim = tensor.shape[-1] // 2
    first = tensor[..., :half_dim]
    second = tensor[..., half_dim:]
    cosine_b = cosine_table[:, None, :]
    sine_b = sine_table[:, None, :]
    return jnp.concatenate(
        [first * cosine_b - second * sine_b, first * sine_b + second * cosine_b], axis=-1
    )


def contract_rows(left, right):
    return lax.dot_general(
        left, right, (((0,), (0,)), ((), ())), preferred_element_type=jnp.float32
    )


def times_transposed(left, right):
    return lax.dot_general(
        left, right, (((1,), (1,)), ((), ())), preferred_element_type=jnp.float32
    )


def band_layer(
    tokens,
    cotangent,
    lengths,
    w_query,
    w_key,
    w_value,
    w_output,
    w_gate,
    w_up,
    w_down,
    gain_attn,
    gain_ffn,
):
    item_count, band_len, model_width = tokens.shape
    head_count = HEADS
    head_dim = model_width // head_count
    band_count = lax.axis_size("blk")
    band_index = lax.axis_index("blk")
    seq_len = band_len * band_count
    row_count = item_count * band_len
    score_scale = head_dim ** (-0.5)
    positions = band_index * band_len + jnp.arange(band_len, dtype=jnp.int32)
    valid_rows = (positions[None, :] < lengths[:, None]).astype(jnp.float32).reshape(row_count, 1)
    cosine_table, sine_table = tables(positions.astype(jnp.float32), head_dim)
    key_positions = jnp.arange(seq_len, dtype=jnp.int32)
    allowed = key_positions[None, :] <= positions[:, None]
    incoming = tokens.astype(jnp.float32).reshape(row_count, model_width)
    inv_one = lax.rsqrt(jnp.mean(incoming * incoming, axis=-1, keepdims=True) + epsilon)
    normed_one = (incoming * inv_one * gain_attn).astype(jnp.bfloat16)
    query = rotate(
        jnp.dot(normed_one, w_query, preferred_element_type=jnp.float32).reshape(
            item_count, band_len, head_count, head_dim
        ),
        cosine_table,
        sine_table,
    ).astype(jnp.bfloat16)
    key_own = rotate(
        jnp.dot(normed_one, w_key, preferred_element_type=jnp.float32).reshape(
            item_count, band_len, head_count, head_dim
        ),
        cosine_table,
        sine_table,
    ).astype(jnp.bfloat16)
    value_own = jnp.dot(normed_one, w_value, preferred_element_type=jnp.float32).astype(
        jnp.bfloat16
    )
    pair = jnp.concatenate(
        [
            key_own.reshape(item_count, band_len, model_width),
            value_own.reshape(item_count, band_len, model_width),
        ],
        axis=-1,
    )
    buffer = jnp.zeros((item_count, band_count, band_len, 2 * model_width), jnp.bfloat16)
    buffer = lax.dynamic_update_slice_in_dim(buffer, pair[:, None], band_index, 1)

    def cycle_step(turn_index, state):
        carried, buffer = state
        carried = shifted(carried, "blk", 1)
        source = band_index - turn_index
        placed = lax.dynamic_update_slice_in_dim(
            buffer, carried[:, None], jnp.maximum(source, 0), 1
        )
        buffer = jnp.where(source >= 0, placed, buffer)
        return (carried, buffer)

    _, buffer = lax.fori_loop(1, band_count, cycle_step, (pair, buffer))
    whole = buffer.reshape(item_count, seq_len, 2 * model_width)
    keys_all = whole[..., :model_width].reshape(item_count, seq_len, head_count, head_dim)
    values_all = whole[..., model_width:].reshape(item_count, seq_len, head_count, head_dim)
    scores = (
        jnp.einsum("iqhd,ikhd->ihqk", query, keys_all, preferred_element_type=jnp.float32)
        * score_scale
    )
    scores = jnp.where(allowed[None, None], scores, masked_value)
    highest_s = jnp.max(scores, axis=-1, keepdims=True)
    expo = jnp.exp(scores - highest_s)
    totals = jnp.sum(expo, axis=-1, keepdims=True)
    softmax_w = expo / totals
    attended = jnp.einsum(
        "ihqk,ikhd->iqhd",
        softmax_w.astype(jnp.bfloat16),
        values_all,
        preferred_element_type=jnp.float32,
    )
    attended = attended.astype(jnp.bfloat16).reshape(row_count, model_width)
    middle = incoming + jnp.dot(attended, w_output, preferred_element_type=jnp.float32)
    inv_two = lax.rsqrt(jnp.mean(middle * middle, axis=-1, keepdims=True) + epsilon)
    normed_two = (middle * inv_two * gain_ffn).astype(jnp.bfloat16)
    gate_pre = jnp.dot(normed_two, w_gate, preferred_element_type=jnp.float32)
    up_pre = jnp.dot(normed_two, w_up, preferred_element_type=jnp.float32)
    sigmoid_g = jax.nn.sigmoid(gate_pre)
    silu_g = gate_pre * sigmoid_g
    hidden = (silu_g * up_pre).astype(jnp.bfloat16)
    ffn_out = jnp.dot(hidden, w_down, preferred_element_type=jnp.float32)
    result = (middle + ffn_out) * valid_rows
    output = result.astype(jnp.bfloat16).reshape(item_count, band_len, model_width)
    grad_res = cotangent.astype(jnp.float32).reshape(row_count, model_width) * valid_rows
    grad_ffn = grad_res.astype(jnp.bfloat16)
    grad_down = contract_rows(hidden, grad_ffn)
    grad_hidden = times_transposed(grad_ffn, w_down)
    grad_gate_pre = (
        grad_hidden * up_pre * (sigmoid_g * (1.0 + gate_pre * (1.0 - sigmoid_g)))
    ).astype(jnp.bfloat16)
    grad_up_pre = (grad_hidden * silu_g).astype(jnp.bfloat16)
    grad_gate = contract_rows(normed_two, grad_gate_pre)
    grad_up = contract_rows(normed_two, grad_up_pre)
    grad_normed_two = times_transposed(grad_gate_pre, w_gate) + times_transposed(grad_up_pre, w_up)
    grad_gain_ffn = jnp.sum(grad_normed_two * middle * inv_two, axis=0)
    scaled_two = grad_normed_two * gain_ffn
    grad_middle = grad_res + inv_two * (
        scaled_two
        - middle * inv_two * inv_two * jnp.mean(scaled_two * middle, axis=-1, keepdims=True)
    )
    grad_branch = grad_middle.astype(jnp.bfloat16)
    grad_output = contract_rows(attended, grad_branch)
    grad_attended = (
        times_transposed(grad_branch, w_output)
        .astype(jnp.bfloat16)
        .reshape(item_count, band_len, head_count, head_dim)
    )
    again = (
        jnp.einsum("iqhd,ikhd->ihqk", query, keys_all, preferred_element_type=jnp.float32)
        * score_scale
    )
    again = jnp.where(allowed[None, None], again, masked_value)
    probable = jnp.exp(again - highest_s) / totals
    grad_probs = jnp.einsum(
        "iqhd,ikhd->ihqk", grad_attended, values_all, preferred_element_type=jnp.float32
    )
    row_delta = jnp.sum(probable * grad_probs, axis=-1, keepdims=True)
    grad_scores = (probable * (grad_probs - row_delta)).astype(jnp.bfloat16)
    grad_query = (
        jnp.einsum("ihqk,ikhd->iqhd", grad_scores, keys_all, preferred_element_type=jnp.float32)
        * score_scale
    )
    grad_values = jnp.einsum(
        "ihqk,iqhd->ikhd",
        probable.astype(jnp.bfloat16),
        grad_attended,
        preferred_element_type=jnp.float32,
    )
    grad_keys = (
        jnp.einsum("ihqk,iqhd->ikhd", grad_scores, query, preferred_element_type=jnp.float32)
        * score_scale
    )
    grad_pair = jnp.concatenate(
        [
            grad_keys.reshape(item_count, seq_len, model_width),
            grad_values.reshape(item_count, seq_len, model_width),
        ],
        axis=-1,
    )
    blocks = grad_pair.reshape(item_count, band_count, band_len, 2 * model_width)
    empty_block = jnp.zeros((item_count, band_len, 2 * model_width), jnp.float32)

    def block_of(index):
        picked = lax.dynamic_index_in_dim(blocks, jnp.maximum(index, 0), 1, keepdims=False)
        return jnp.where(index >= 0, picked, empty_block)

    def cycle_back(turn_index, carried):
        carried = shifted(carried.astype(jnp.bfloat16), "blk", -1).astype(carried.dtype)
        return carried + block_of(band_index - (band_count - 1) + turn_index)

    own_grads = lax.fori_loop(1, band_count, cycle_back, block_of(band_index - (band_count - 1)))
    grad_key_own = own_grads[..., :model_width].reshape(item_count, band_len, head_count, head_dim)
    grad_value_raw = (
        own_grads[..., model_width:].astype(jnp.bfloat16).reshape(row_count, model_width)
    )
    grad_key_raw = (
        rotate(grad_key_own, cosine_table, -sine_table)
        .astype(jnp.bfloat16)
        .reshape(row_count, model_width)
    )
    grad_query_raw = (
        rotate(grad_query, cosine_table, -sine_table)
        .astype(jnp.bfloat16)
        .reshape(row_count, model_width)
    )
    grad_wquery = contract_rows(normed_one, grad_query_raw)
    grad_wkey = contract_rows(normed_one, grad_key_raw)
    grad_wvalue = contract_rows(normed_one, grad_value_raw)
    grad_normed_one = (
        times_transposed(grad_query_raw, w_query)
        + times_transposed(grad_key_raw, w_key)
        + times_transposed(grad_value_raw, w_value)
    )
    grad_gain_attn = jnp.sum(grad_normed_one * incoming * inv_one, axis=0)
    scaled_one = grad_normed_one * gain_attn
    grad_incoming = grad_middle + inv_one * (
        scaled_one
        - incoming * inv_one * inv_one * jnp.mean(scaled_one * incoming, axis=-1, keepdims=True)
    )
    grad_tokens = grad_incoming.astype(jnp.bfloat16).reshape(item_count, band_len, model_width)
    summed = (
        lax.psum_scatter(
            grad_wquery.astype(jnp.bfloat16), "blk", scatter_dimension=0, tiled=True
        ).astype(jnp.float32),
        lax.psum_scatter(
            grad_wkey.astype(jnp.bfloat16), "blk", scatter_dimension=0, tiled=True
        ).astype(jnp.float32),
        lax.psum_scatter(
            grad_wvalue.astype(jnp.bfloat16), "blk", scatter_dimension=0, tiled=True
        ).astype(jnp.float32),
        lax.psum_scatter(
            grad_output.astype(jnp.bfloat16), "blk", scatter_dimension=0, tiled=True
        ).astype(jnp.float32),
        lax.psum_scatter(
            grad_gate.astype(jnp.bfloat16), "blk", scatter_dimension=0, tiled=True
        ).astype(jnp.float32),
        lax.psum_scatter(
            grad_up.astype(jnp.bfloat16), "blk", scatter_dimension=0, tiled=True
        ).astype(jnp.float32),
        lax.psum_scatter(
            grad_down.astype(jnp.bfloat16), "blk", scatter_dimension=0, tiled=True
        ).astype(jnp.float32),
        lax.psum_scatter(
            grad_gain_attn.astype(jnp.bfloat16), "blk", scatter_dimension=0, tiled=True
        ).astype(jnp.float32),
        lax.psum_scatter(
            grad_gain_ffn.astype(jnp.bfloat16), "blk", scatter_dimension=0, tiled=True
        ).astype(jnp.float32),
    )
    summed = (
        lax.psum(summed[0].astype(jnp.bfloat16), "dp").astype(jnp.float32),
        lax.psum(summed[1].astype(jnp.bfloat16), "dp").astype(jnp.float32),
        lax.psum(summed[2].astype(jnp.bfloat16), "dp").astype(jnp.float32),
        lax.psum(summed[3].astype(jnp.bfloat16), "dp").astype(jnp.float32),
        lax.psum(summed[4].astype(jnp.bfloat16), "dp").astype(jnp.float32),
        lax.psum(summed[5].astype(jnp.bfloat16), "dp").astype(jnp.float32),
        lax.psum(summed[6].astype(jnp.bfloat16), "dp").astype(jnp.float32),
        lax.psum(summed[7].astype(jnp.bfloat16), "dp").astype(jnp.float32),
        lax.psum(summed[8].astype(jnp.bfloat16), "dp").astype(jnp.float32),
    )
    return (
        output,
        grad_tokens,
        summed[0],
        summed[1],
        summed[2],
        summed[3],
        summed[4],
        summed[5],
        summed[6],
        summed[7],
        summed[8],
    )


MESH = pl.DeviceIdType.MESH
CORES = 2
CHIPS = 4
BLOCK = 256
PAIR = 128
LOW = jnp.bfloat16
F32 = jnp.float32


def place():
    dp = lax.axis_index("dp")
    return dp, lax.axis_index("blk"), lax.rem(dp, CORES)


def near(dp, blk, core=0, chip=0, line=0):
    flip = core + CORES * line
    return {"dp": dp ^ flip if flip else dp, "blk": blk ^ chip if chip else blk}


def greet(dp, blk, flips):
    barrier = pltpu.get_barrier_semaphore()
    for flip in flips:
        pl.semaphore_signal(barrier, inc=1, device_id=near(dp, blk, *flip), device_id_type=MESH)
    pl.semaphore_wait(barrier, len(flips))


def remote(src, dst, send, recv, where):
    return pltpu.make_async_remote_copy(
        src_ref=src, dst_ref=dst, send_sem=send, recv_sem=recv, device_id=where, device_id_type=MESH
    )


def part(start, size):
    return pl.ds(pl.multiple_of(start, size), size)


PLANE = [(core, chip, 0) for chip in range(CHIPS) for core in range(CORES) if core or chip]
REACH = PLANE + [(0, 0, 1), (0, 0, 3)]


def plus(one, other, kind=LOW):
    return (one.astype(F32) + other.astype(F32)).astype(kind)


class Gather:
    SEMS = [(2,), (4, 2), (4,), (4,), (4,)]

    def __init__(self, band, buf, sems):
        self.band, self.buf = band, buf
        self.own, self.send, self.recv, self.fsend, self.frecv = sems
        self.dp, self.blk, self.core = place()
        self.rows = band.shape[1]
        self.half = self.rows // 2
        self.mine = (self.blk // 2) == self.core

    def out(self, r, h):
        target = self.blk ^ r
        return remote(
            self.band.at[lax.rem(target, 2), pl.ds(h * self.half, self.half)],
            self.buf.at[part(self.blk * self.rows + h * self.half, self.half)],
            self.send.at[r, h],
            self.recv.at[r],
            {"dp": self.dp - self.core + h, "blk": target},
        )

    def across(self, r):
        rows = self.buf.at[part((self.blk ^ r) * self.rows + self.core * self.half, self.half)]
        return remote(rows, rows, self.fsend.at[r], self.frecv.at[r], near(self.dp, self.blk, 1))

    def here(self):
        rows = self.buf.at[part(self.blk * self.rows, self.rows)]
        return pltpu.make_async_copy(self.band.at[lax.rem(self.blk, 2)], rows, self.own.at[0])

    def there(self):
        rows = self.buf.at[part(self.blk * self.rows, self.rows)]
        src = self.band.at[lax.rem(self.blk, 2)]
        return remote(src, rows, self.fsend.at[0], self.frecv.at[0], near(self.dp, self.blk, 1))

    def sends(self, r):
        return ((self.blk ^ r) // 2) == self.core

    def start(self):
        for r in (1, 2, 3):

            @pl.when(self.sends(r))
            def _():
                for h in range(2):
                    self.out(r, h).start()

        @pl.when(self.mine)
        def _():
            self.here().start()
            self.there().start()

    def forward(self, r):
        self.out(r, 0).wait_recv()
        self.across(r).start()

    def ready(self, r):
        if r:
            self.across(r).wait_recv()
            return

        @pl.when(self.mine)
        def _():
            self.here().wait()

        @pl.when(jnp.logical_not(self.mine))
        def _():
            self.there().wait_recv()

    def drain(self):
        @pl.when(self.mine)
        def _():
            self.there().wait_send()

        for r in (1, 2, 3):
            self.across(r).wait_send()

            @pl.when(self.sends(r))
            def _():
                for h in range(2):
                    self.out(r, h).wait_send()


class Return:
    SEMS = [(1,), (4,), (2, 2)]

    def __init__(self, src, band, sems):
        self.src, self.band = src, band
        self.own, self.send, self.recv = sems
        self.dp, self.blk, self.core = place()
        self.half = src.shape[1]
        self.home = self.blk // 2

    def slot(self):
        return self.band.at[lax.rem(self.blk, 2), part(self.core * self.half, self.half)]

    def out(self, r):
        chip = self.blk ^ r
        return remote(
            self.src.at[chip],
            self.slot(),
            self.send.at[r],
            self.recv.at[lax.rem(self.blk, 2), self.core],
            {"dp": self.dp - self.core + self.home, "blk": chip},
        )

    def keep(self):
        return pltpu.make_async_copy(self.src.at[self.blk], self.slot(), self.own.at[0])

    def start(self):
        for r in (3, 1, 2):
            self.out(r).start()

        @pl.when(self.home == self.core)
        def _():
            self.keep().start()

        @pl.when(self.home != self.core)
        def _():
            self.out(0).start()

    def drain(self):
        @pl.when(self.home == self.core)
        def _():
            self.keep().wait()

        @pl.when(self.home != self.core)
        def _():
            self.out(0).wait_send()

        for r in (1, 2, 3):
            self.out(r).wait_send()

    def arrived(self):
        for i in range(2):
            for h in range(2):
                local = (self.core * 2 + i == self.blk) & (self.core == h)

                @pl.when(jnp.logical_not(local))
                def _():
                    remote(
                        self.src.at[0],
                        self.band.at[i, pl.ds(h * self.half, self.half)],
                        self.send.at[0],
                        self.recv.at[i, h],
                        near(self.dp, self.blk, 1),
                    ).wait_recv()


class Line:
    def locate(self):
        self.dp, self.blk, self.core = place()
        z = self.dp // CORES
        self.outer = (z == 0) | (z == 3)
        self.inner = jnp.logical_not(self.outer)

    def stage(self, n):
        getattr(self, "stage" + str(n))()


class Chunk(Line):
    SEMS = [(2, 2, 2), (2, 2), (3, 2), (3,)]

    def __init__(self, src, first, second, line, result, sems, turned=False):
        self.src, self.first, self.second, self.line, self.result = src, first, second, line, result
        self.s1, self.s2, self.sz, self.sc = sems
        self.turned = turned
        self.locate()

    @staticmethod
    def shapes(rows, cols, turned):
        half = (rows // 2, cols // CHIPS) if turned else (rows // CHIPS // 2, cols)
        return [(2, 2) + half, (2,) + half, (2, 2) + half], (CORES, 2) + half

    def piece(self, chip, h):
        if self.turned:
            rows, cols = self.src.shape[0] // 2, self.src.shape[1] // CHIPS
            return self.src.at[pl.ds(h * rows, rows), part(chip * cols, cols)]
        rows = self.src.shape[0] // CHIPS // 2
        return self.src.at[part(chip * 2 * rows + h * rows, rows)]

    def ways(self, h):
        return (1, 2) if h == 0 else (2, 1)

    def step1(self, h, n):
        near_way, far_way = self.ways(h)
        chip = self.blk ^ near_way ^ (far_way if n else 0)
        return remote(
            self.piece(chip, h), self.first.at[h, n], self.s1.at[0, h, n], self.s1.at[1, h, n],
            near(self.dp, self.blk, 0, near_way),
        )

    def step2(self, h):
        return remote(
            self.first.at[h, 1], self.second.at[h], self.s2.at[0, h], self.s2.at[1, h],
            near(self.dp, self.blk, 0, self.ways(h)[1]),
        )

    def hop(self, n):
        src = (self.second, self.line.at[0], self.second)[n]
        dst = (self.line.at[0], self.line.at[1], self.line.at[0])[n]
        return remote(
            src, dst, self.sz.at[n, 0], self.sz.at[n, 1],
            near(self.dp, self.blk, 0, 0, 3 if n == 1 else 1),
        )

    def share(self, total):
        slot = self.result.at[self.core]
        return (
            remote(total, slot, self.sc.at[0], self.sc.at[1], near(self.dp, self.blk, 1)),
            pltpu.make_async_copy(total, slot, self.sc.at[2]),
        )

    def stage0(self):
        for n in (1, 0):
            for h in range(2):
                self.step1(h, n).start()

    def stage1(self):
        for h in range(2):
            self.step1(h, 1).wait_recv()
            chip = self.blk ^ self.ways(h)[1]
            self.first[h, 1] = plus(self.first[h, 1], self.piece(chip, h)[...])
            self.step2(h).start()

    def stage2(self):
        for h in range(2):
            self.step1(h, 0).wait_recv()
            self.step2(h).wait_recv()
            own = plus(self.first[h, 0], self.piece(self.blk, h)[...], F32)
            self.second[h] = plus(own, self.second[h])

        @pl.when(self.outer)
        def _():
            self.hop(0).start()

    def stage3(self):
        @pl.when(self.inner)
        def _():
            self.hop(0).wait_recv()
            for h in range(2):
                self.line[0, h] = plus(self.line[0, h], self.second[h])
            self.hop(1).start()

    def stage4(self):
        @pl.when(self.inner)
        def _():
            self.hop(1).wait_recv()
            for h in range(2):
                self.second[h] = plus(self.line[0, h], self.line[1, h])
            self.hop(2).start()
            for copy in self.share(self.second):
                copy.start()

    def stage5(self):
        @pl.when(self.outer)
        def _():
            self.hop(2).wait_recv()
            for copy in self.share(self.line.at[0]):
                copy.start()

    def stage6(self):
        across, keep = self.share(self.second)
        across.wait()
        keep.wait()
        for h in range(2):
            for n in range(2):
                self.step1(h, n).wait_send()
            self.step2(h).wait_send()

        @pl.when(self.outer)
        def _():
            self.hop(0).wait_send()

        @pl.when(self.inner)
        def _():
            self.hop(1).wait_send()
            self.hop(2).wait_send()


class Small(Line):
    SEMS = [(6, 2)]
    SLOTS = 11

    def __init__(self, hold, result, sems):
        self.hold, self.result = hold, result
        (self.sem,) = sems
        self.locate()

    def go(self, n):
        flips = ((1, 0, 0), (0, 1, 0), (0, 2, 0), (0, 0, 1), (0, 0, 3), (0, 0, 1))
        src, dst = (10, 10) if n == 5 else (2 * n, 2 * n + 1)
        return remote(
            self.hold.at[src], self.hold.at[dst], self.sem.at[n, 0], self.sem.at[n, 1],
            near(self.dp, self.blk, *flips[n]),
        )

    def add(self, n, to):
        self.go(n).wait_recv()
        self.hold[to] = self.hold[2 * n] + self.hold[2 * n + 1]

    def stage0(self):
        self.go(0).start()

    def stage1(self):
        for n in range(2):
            self.add(n, 2 * n + 2)
            self.go(n + 1).start()

    def stage2(self):
        self.add(2, 6)

        @pl.when(self.outer)
        def _():
            self.go(3).start()

    def stage3(self):
        @pl.when(self.inner)
        def _():
            self.add(3, 8)
            self.go(4).start()

    def stage4(self):
        @pl.when(self.inner)
        def _():
            self.add(4, 10)
            self.go(5).start()

    def stage5(self):
        @pl.when(self.outer)
        def _():
            self.go(5).wait_recv()

        self.result[...] = self.hold[10]

    def stage6(self):
        for n in range(3):
            self.go(n).wait_send()

        @pl.when(self.outer)
        def _():
            self.go(3).wait_send()

        @pl.when(self.inner)
        def _():
            self.go(4).wait_send()
            self.go(5).wait_send()


def dot(left, right):
    return jnp.dot(left, right, preferred_element_type=F32)


def dot_rows(left, right):
    return lax.dot_general(left, right, (((0,), (0,)), ((), ())), preferred_element_type=F32)


def dot_cols(left, right):
    return lax.dot_general(left, right, (((1,), (1,)), ((), ())), preferred_element_type=F32)


def inverse_rms(values):
    return lax.rsqrt(jnp.mean(values * values, axis=-1, keepdims=True) + epsilon)


def turn(t, cosine, sine, sign):
    quarter = PAIR // 4
    lane = lax.broadcasted_iota(jnp.int32, t.shape, 1)
    other = jnp.where(
        lane % (2 * quarter) < quarter,
        pltpu.roll(t, PAIR - quarter, 1),
        pltpu.roll(t, quarter, 1),
    )
    return t * cosine + (sign * sine) * other


def both_heads(t):
    lane = lax.broadcasted_iota(jnp.int32, t.shape, 1)
    zero = jnp.zeros_like(t)
    return jnp.concatenate(
        [jnp.where(lane < PAIR // 2, t, zero), jnp.where(lane < PAIR // 2, zero, t)], axis=0
    )


def one_pair(t):
    rows = t.shape[0] // 2
    lane = lax.broadcasted_iota(jnp.int32, (rows, PAIR), 1)
    return jnp.where(lane < PAIR // 2, t[:rows], t[rows:])


BIG = ("down", "gate", "up")
NAMES = BIG + ("output", "query", "key", "value")


def layout(width, ff):
    seq = CHIPS * BLOCK
    half = width // 2
    pairs = half // PAIR
    low = lambda *shape: pltpu.VMEM(shape, LOW)
    keep = dict(
        w_qkv=low(width, 3 * half), w_out=low(width, width), w_gate=low(width, ff), w_up=low(width, ff),
        w_down=low(ff, width), turns=pltpu.VMEM((2, seq, PAIR), F32),
        x=low(seq, width), g_ffn=low(seq, width), n1=low(seq, width),
        q=low(seq, half), k=low(seq, half), v=low(seq, half),
        prob0=low(pairs, 2 * BLOCK, BLOCK), prob1=low(pairs, 2 * BLOCK, 2 * BLOCK),
        prob2=low(pairs, 2 * BLOCK, 3 * BLOCK), prob3=low(pairs, 2 * BLOCK, 4 * BLOCK),
        att=low(seq, width), middle=pltpu.VMEM((seq, width), F32), n2=low(seq, width),
        hidden=low(seq, ff), g_gate=low(seq, ff), g_up=low(seq, ff),
        gn2=low(seq, width),
        swap_out=low(CHIPS, BLOCK // 2, width), swap_in=low(CHIPS, BLOCK // 2, width),
        band=low(CHIPS, BLOCK // 2, width),
        dk=pltpu.VMEM((seq, PAIR), F32), dv=pltpu.VMEM((seq, PAIR), F32),
        hold=pltpu.VMEM((Small.SLOTS, 8, width), F32),
    )
    sems = dict(
        load=[(17,)], gather_x=Gather.SEMS, gather_g=Gather.SEMS, att=[(2, pairs)], swap=[(2, 2)], gn2=[(2, CHIPS)],
        back_out=Return.SEMS, back_x=Return.SEMS, small=Small.SEMS,
    )
    results = {}
    for name in NAMES:
        cols = ff if name in BIG else half
        shapes, results[name] = Chunk.shapes(width, cols, name == "down")
        keep["grad_" + name] = low(width, cols)
        for label, shape in zip(("first_", "second_", "line_"), shapes):
            keep[label + name] = low(*shape)
        sems["sum_" + name] = Chunk.SEMS
    return keep, sems, results


INPUTS = (
    "tokens", "cotangent", "lengths", "turns", "gain_attn", "gain_ffn",
    "w_query", "w_key", "w_value", "w_output", "w_gate", "w_up", "w_down",
)


def layer_kernel(width, ff, *refs):
    refs = list(refs)
    keep, sem_shapes, results = layout(width, ff)

    def take(names):
        got = dict(zip(names, refs))
        del refs[: len(names)]
        return got

    arg = take(INPUTS)
    result = take(NAMES + ("small", "out_band", "x_band"))
    m = take(list(keep))
    sem = {}
    for name, shapes in sem_shapes.items():
        sem[name] = refs[: len(shapes)]
        del refs[: len(shapes)]

    dp, blk, core = place()
    partner = near(dp, blk, 1)
    half = width // 2
    pairs = half // PAIR
    scale = (width // HEADS) ** (-0.5)
    mine = pl.multiple_of(core * half, half)

    def block(r):
        return part(r * BLOCK, BLOCK)

    def half_block(chip, c):
        return part(chip * BLOCK + c * (BLOCK // 2), BLOCK // 2)

    def lanes(p):
        return part(p * PAIR, PAIR)

    loads = []

    def load(src, dst):
        copy = pltpu.make_async_copy(src, dst, sem["load"][0].at[len(loads)])
        copy.start()
        loads.append(copy)

    load(arg["turns"], m["turns"])
    for n, name in enumerate(("w_query", "w_key", "w_value")):
        load(arg[name].at[:, pl.ds(mine, half)], m["w_qkv"].at[:, pl.ds(n * half, half)])

    gather_x = Gather(arg["tokens"], m["x"], sem["gather_x"])
    gather_g = Gather(m["band"].reshape(2, BLOCK, width), m["g_ffn"], sem["gather_g"])
    greet(dp, blk, REACH)
    gather_x.start()
    load(arg["w_output"], m["w_out"])
    unit = ff // CHIPS
    for chip in range(CHIPS):
        there = part(chip * CORES * unit + core * unit, unit)
        here = pl.ds(chip * unit, unit)
        load(arg["w_gate"].at[:, there], m["w_gate"].at[:, here])
        load(arg["w_up"].at[:, there], m["w_up"].at[:, here])
        load(arg["w_down"].at[there], m["w_down"].at[here])
    for i in range(2):
        row = blk * BLOCK + lax.broadcasted_iota(jnp.int32, (BLOCK, width), 0)
        masked = jnp.where(row < arg["lengths"][i], arg["cotangent"][i].astype(F32), 0.0)
        for h in range(2):
            m["band"][2 * i + h] = masked[h * (BLOCK // 2) : (h + 1) * (BLOCK // 2)].astype(LOW)
    gather_g.start()
    for copy in loads[:4]:
        copy.wait()

    def project(r):
        rows = block(blk ^ r)
        x = m["x"][rows].astype(F32)
        n1 = (x * inverse_rms(x) * arg["gain_attn"][...]).astype(LOW)
        m["n1"][rows] = n1
        cosine, sine = m["turns"][0, rows], m["turns"][1, rows]
        for n, name in enumerate("qkv"):
            full = dot(n1, m["w_qkv"][:, n * half : (n + 1) * half])
            for p in range(pairs):
                t = full[:, p * PAIR : (p + 1) * PAIR]
                if name != "v":
                    t = turn(t, cosine, sine, 1.0)
                if name == "q":
                    t = t.astype(LOW).astype(F32) * scale
                m[name][rows, p * PAIR : (p + 1) * PAIR] = t.astype(LOW)

    gather_x.ready(0)
    project(0)
    gather_x.forward(1)
    gather_x.forward(2)
    gather_x.ready(1)
    project(1)
    gather_x.forward(3)
    gather_x.ready(2)
    project(2)
    gather_x.ready(3)
    project(3)
    for r in (1, 2, 3):
        gather_g.forward(r)

    row = lax.broadcasted_iota(jnp.int32, (2 * BLOCK, BLOCK), 0) % BLOCK
    seen = lax.broadcasted_iota(jnp.int32, (2 * BLOCK, BLOCK), 1) <= row

    def att_cols(p):
        return part(core * half + p * PAIR, PAIR)

    def att_copy(p):
        cols = m["att"].at[:, att_cols(p)]
        return remote(cols, cols, sem["att"][0].at[0, p], sem["att"][0].at[1, p], partner)

    @pl.loop(0, pairs)
    def _(p):
        for i in range(CHIPS):
            size = BLOCK * i
            q = both_heads(m["q"][pl.ds(size, BLOCK), lanes(p)])
            own = dot_cols(q, m["k"][pl.ds(size, BLOCK), lanes(p)])
            own = jnp.where(seen, own, masked_value)
            top = jnp.max(own, axis=-1, keepdims=True)
            if i:
                past = dot_cols(q, m["k"][pl.ds(0, size), lanes(p)])
                top = jnp.maximum(top, jnp.max(past, axis=-1, keepdims=True))
                past = jnp.exp(past - top)
            own = jnp.exp(own - top)
            total = jnp.sum(own, axis=-1, keepdims=True)
            if i:
                total = total + jnp.sum(past, axis=-1, keepdims=True)
            share = 1.0 / total
            prob = m["prob" + str(i)]
            own = (own * share).astype(LOW)
            prob[p, :, pl.ds(size, BLOCK)] = own
            att = dot(own, m["v"][pl.ds(size, BLOCK), lanes(p)])
            if i:
                past = (past * share).astype(LOW)
                prob[p, :, pl.ds(0, size)] = past
                att = att + dot(past, m["v"][pl.ds(0, size), lanes(p)])
            m["att"][pl.ds(size, BLOCK), att_cols(p)] = one_pair(att).astype(LOW)
        att_copy(p).start()

    for r in range(CHIPS):
        gather_g.ready(r)
    for copy in loads[4:]:
        copy.wait()
    for p in range(pairs):
        att_copy(p).wait_recv()

    @pl.loop(0, CHIPS)
    def _(r):
        rows = block(r)
        middle = m["x"][rows].astype(F32) + dot(m["att"][rows], m["w_out"][...])
        m["middle"][rows] = middle
        n2 = (middle * inverse_rms(middle) * arg["gain_ffn"][...]).astype(LOW)
        m["n2"][rows] = n2
        for t in range(ff // BLOCK):
            cols = pl.ds(t * BLOCK, BLOCK)
            gate = dot(n2, m["w_gate"][:, cols])
            up = dot(n2, m["w_up"][:, cols])
            g_hidden = dot_cols(m["g_ffn"][rows], m["w_down"][cols])
            sig = 0.5 * jnp.tanh(0.5 * gate) + 0.5
            silu = gate * sig
            m["hidden"][rows, cols] = (silu * up).astype(LOW)
            m["g_up"][rows, cols] = (g_hidden * silu).astype(LOW)
            m["g_gate"][rows, cols] = (g_hidden * up * (sig * (1.0 + gate * (1.0 - sig)))).astype(LOW)

    sums = {}
    for name in NAMES:
        sums[name] = Chunk(
            m["grad_" + name], m["first_" + name], m["second_" + name], m["line_" + name], result[name],
            sem["sum_" + name], name == "down",
        )
    sums["small"] = Small(m["hold"], result["small"], sem["small"])
    done = {name: 0 for name in sums}

    def advance(*names):
        for name in names:
            sums[name].stage(done[name])
            done[name] += 1

    def swap(n):
        return remote(m["swap_out"], m["swap_in"], sem["swap"][0].at[n, 0], sem["swap"][0].at[n, 1], partner)

    @pl.loop(0, CHIPS)
    def _(chip):
        m["swap_out"][chip] = dot(m["hidden"][half_block(chip, 1 - core)], m["w_down"][...]).astype(LOW)

    swap(0).start()

    @pl.loop(0, width // BLOCK)
    def _(t):
        rows = block(t)
        m["grad_down"][rows] = dot_rows(m["g_ffn"][:, rows], m["hidden"][...]).astype(LOW)

    advance("down")
    swap(0).wait()
    gather_g.drain()
    back_out = Return(m["band"], result["out_band"], sem["back_out"])

    @pl.loop(0, CHIPS)
    def _(chip):
        rows = half_block(chip, core)
        out = dot(m["hidden"][rows], m["w_down"][...]) + m["swap_in"][chip].astype(F32)
        m["band"][chip] = (m["middle"][rows] + out).astype(LOW)

    back_out.start()

    @pl.loop(0, width // BLOCK)
    def _(t):
        rows = block(t)
        n2 = m["n2"][:, rows]
        m["grad_up"][rows] = dot_rows(n2, m["g_up"][...]).astype(LOW)
        m["grad_gate"][rows] = dot_rows(n2, m["g_gate"][...]).astype(LOW)

    advance("up", "gate")

    def gn2_copy(r):
        return remote(
            m["hidden"].at[block(r), pl.ds(0, width)], m["gn2"].at[block(r)],
            sem["gn2"][0].at[0, r], sem["gn2"][0].at[1, r], partner,
        )

    @pl.loop(0, CHIPS)
    def _(r):
        rows = block(r)
        got = dot_cols(m["g_gate"][rows], m["w_gate"][...]) + dot_cols(m["g_up"][rows], m["w_up"][...])
        m["hidden"][rows, pl.ds(0, width)] = got.astype(LOW)
        gn2_copy(r).start()

    advance("down")
    m["hold"][0] = jnp.zeros((8, width), F32)

    @pl.loop(0, CHIPS)
    def _(r):
        rows = block(r)
        gn2_copy(r).wait_recv()
        g_n2 = plus(m["hidden"][rows, pl.ds(0, width)], m["gn2"][rows], F32)
        middle = m["middle"][rows]
        inv = inverse_rms(middle)
        m["hold"][0, 1:2] += 0.5 * jnp.sum(g_n2 * middle * inv, axis=0, keepdims=True)
        a2 = g_n2 * arg["gain_ffn"][...]
        inner = jnp.mean(a2 * middle, axis=-1, keepdims=True)
        g_mid = m["g_ffn"][rows].astype(F32) + inv * (a2 - middle * (inv * inv * inner))
        m["n2"][rows] = g_mid.astype(LOW)
        m["middle"][rows] = g_mid

    g_branch, g_mid = m["n2"], m["middle"]

    @pl.loop(0, width // BLOCK)
    def _(t):
        rows = block(t)
        m["grad_output"][rows] = dot_rows(m["att"][:, rows], g_branch[:, pl.ds(mine, half)]).astype(LOW)

    advance("output")
    for r in range(CHIPS):
        gn2_copy(r).wait_send()
    g_att = m["hidden"]
    g_q, g_k = m["g_gate"].at[:, pl.ds(0, half)], m["g_gate"].at[:, pl.ds(half, half)]
    g_v = m["g_up"].at[:, pl.ds(0, half)]

    @pl.loop(0, CHIPS)
    def _(r):
        g_att[block(r), pl.ds(0, half)] = dot_cols(g_branch[block(r)], m["w_out"][pl.ds(mine, half)]).astype(LOW)

    @pl.loop(0, pairs)
    def _(p):
        for i in range(CHIPS - 1, -1, -1):
            rows, size = pl.ds(BLOCK * i, BLOCK), BLOCK * (i + 1)
            past = pl.ds(0, size)
            g = both_heads(g_att[rows, lanes(p)])
            q = both_heads(m["q"][rows, lanes(p)])
            out = m["att"][rows, att_cols(p)].astype(F32)
            delta = jnp.sum(g.astype(F32) * jnp.concatenate([out, out], axis=0), axis=-1, keepdims=True)
            prob = m["prob" + str(i)][p]
            g_prob = dot_cols(g, m["v"][past, lanes(p)])
            g_score = (prob.astype(F32) * (g_prob - delta)).astype(LOW)
            got_q = one_pair(dot(g_score, m["k"][past, lanes(p)])) * scale
            g_q[rows, lanes(p)] = turn(got_q, m["turns"][0, rows], m["turns"][1, rows], -1.0).astype(LOW)
            got_k, got_v = dot_rows(g_score, q), dot_rows(prob, g)
            if i == CHIPS - 1:
                m["dk"][...] = got_k
                m["dv"][...] = got_v
            else:
                m["dk"][past] += got_k
                m["dv"][past] += got_v
        for r in range(CHIPS):
            rows = pl.ds(BLOCK * r, BLOCK)
            g_k[rows, lanes(p)] = turn(m["dk"][rows], m["turns"][0, rows], m["turns"][1, rows], -1.0).astype(LOW)
            g_v[rows, lanes(p)] = m["dv"][rows].astype(LOW)

        @pl.when(p == 0)
        def _():
            sums["up"].stage(1)
            sums["down"].stage(2)

        @pl.when(p == 1)
        def _():
            sums["gate"].stage(1)
            sums["up"].stage(2)
            sums["down"].stage(3)

    done.update(down=4, up=3, gate=2)

    @pl.loop(0, width // BLOCK)
    def _(t):
        rows = block(t)
        n1 = m["n1"][:, rows]
        m["grad_query"][rows] = dot_rows(n1, g_q[...]).astype(LOW)
        m["grad_key"][rows] = dot_rows(n1, g_k[...]).astype(LOW)
        m["grad_value"][rows] = dot_rows(n1, g_v[...]).astype(LOW)

    advance("output", "gate", "up", "down")
    advance("query", "key", "value")

    def g_n1(rows):
        got = dot_cols(g_q[rows], m["w_qkv"][:, pl.ds(0, half)])
        got = got + dot_cols(g_k[rows], m["w_qkv"][:, pl.ds(half, half)])
        return got + dot_cols(g_v[rows], m["w_qkv"][:, pl.ds(2 * half, half)])

    @pl.loop(0, CHIPS)
    def _(chip):
        m["swap_out"][chip] = g_n1(half_block(chip, 1 - core)).astype(LOW)

    swap(1).start()
    back_out.drain()
    advance("output", "gate", "up", "down")
    swap(1).wait()
    back_x = Return(m["band"], result["x_band"], sem["back_x"])

    @pl.loop(0, CHIPS)
    def _(chip):
        rows = half_block(chip, core)
        got = g_n1(rows) + m["swap_in"][chip].astype(F32)
        x = m["x"][rows].astype(F32)
        inv = inverse_rms(x)
        m["hold"][0, 0:1] += jnp.sum(got * x * inv, axis=0, keepdims=True)
        a1 = got * arg["gain_attn"][...]
        inner = jnp.mean(a1 * x, axis=-1, keepdims=True)
        m["band"][chip] = (g_mid[rows] + inv * (a1 - x * (inv * inv * inner))).astype(LOW)

    back_x.start()
    advance("small")
    order = ("down", "up", "gate", "output", "query", "key", "value", "small")
    stages = 7
    while any(done[name] < stages for name in order):
        advance(*[name for name in order if done[name] < stages])
    for p in range(pairs):
        att_copy(p).wait_send()
    gather_x.drain()
    back_x.drain()
    back_out.arrived()
    back_x.arrived()


def vmem_specs(count):
    return [pl.BlockSpec(memory_space=pltpu.VMEM)] * count


def any_specs(count):
    return [pl.BlockSpec(memory_space=pl.ANY)] * count


def finish_kernel(lengths, down, gate, up, output, query, key, value, out, *results):
    step = pl.program_id(0)
    blk = lax.axis_index("blk")
    r_out, r_query, r_key, r_value, r_output, r_gate, r_up, r_down = results
    for src, dst in ((query, r_query), (key, r_key), (value, r_value), (output, r_output)):
        cols = src.shape[-1]
        for c in range(CORES):
            dst[:, c * cols : (c + 1) * cols] = src[c, 0].astype(F32)
    for src, dst in ((gate, r_gate), (up, r_up)):
        unit = src.shape[-1] // CHIPS
        for c in range(CORES):
            for chip in range(CHIPS):
                at = (chip * CORES + c) * unit
                dst[:, at : at + unit] = src[c, 0, :, chip * unit : (chip + 1) * unit].astype(F32)
    cols = down.shape[2]
    for h in range(2):
        r_down[:, h * cols : (h + 1) * cols] = down[0, h].astype(F32).T
    rows = out.shape[1]
    for i in range(2):
        place_ = blk * BLOCK + step * rows + lax.broadcasted_iota(jnp.int32, out.shape[1:], 0)
        r_out[i] = jnp.where(place_ < lengths[i], out[i].astype(F32), 0.0).astype(LOW)


def item_layer(
    tokens, cotangent, lengths, w_query, w_key, w_value, w_output, w_gate, w_up, w_down, gain_attn, gain_ffn
):
    width = tokens.shape[2]
    ff = w_gate.shape[1] // CORES
    half = width // 2
    keep, sem_shapes, results = layout(width, ff)
    cosine, sine = turn_tables(CHIPS * BLOCK, width // HEADS)
    band = jax.ShapeDtypeStruct(tokens.shape, LOW)
    fins = pl.pallas_call(
        functools.partial(layer_kernel, width, ff),
        out_shape=[jax.ShapeDtypeStruct(results[n], LOW) for n in NAMES]
        + [jax.ShapeDtypeStruct((8, width), F32), band, band],
        in_specs=any_specs(1) + vmem_specs(1) + [pl.BlockSpec(memory_space=pltpu.SMEM)] + any_specs(1)
        + vmem_specs(2) + any_specs(7),
        out_specs=any_specs(len(NAMES)) + vmem_specs(1) + any_specs(2),
        scratch_shapes=list(keep.values())
        + [pltpu.SemaphoreType.DMA(s) for shapes in sem_shapes.values() for s in shapes],
        compiler_params=pltpu.CompilerParams(
            collective_id=0, has_side_effects=True, vmem_limit_bytes=VMEM_BYTES
        ),
    )(
        tokens, cotangent, lengths, jnp.stack([cosine, sine]), gain_attn[None], gain_ffn[None],
        w_query, w_key, w_value, w_output, w_gate, w_up, w_down,
    )
    *sums, small, out_band, x_band = fins
    steps = 4
    rows = half // 2
    down_shape = results["down"]

    def grad_spec(cols):
        return pl.BlockSpec((CORES, 1, rows // steps, cols), lambda s: (0, s // 2, s % 2, 0))

    def wide_spec(cols):
        return pl.BlockSpec((rows // steps, cols), lambda s: (s, 0))

    band_spec = pl.BlockSpec((2, BLOCK // steps, width), lambda s: (0, s, 0))
    wide = lambda cols: jax.ShapeDtypeStruct((rows, cols), F32)
    output, g_query, g_key, g_value, g_output, g_gate, g_up, g_down = pl.pallas_call(
        finish_kernel,
        grid=(steps,),
        out_shape=[band] + [wide(width)] * 4 + [wide(2 * ff)] * 2
        + [jax.ShapeDtypeStruct((CORES * down_shape[3], width), F32)],
        in_specs=[pl.BlockSpec(memory_space=pltpu.SMEM)]
        + [pl.BlockSpec((1, 2, down_shape[2], down_shape[3] // 2), lambda s: (s // 2, 0, 0, s % 2))]
        + [grad_spec(ff)] * 2 + [grad_spec(half)] * 4 + [band_spec],
        out_specs=[band_spec] + [wide_spec(width)] * 4 + [wide_spec(2 * ff)] * 2
        + [pl.BlockSpec((down_shape[3] // 2, width), lambda s: (s, 0))],
        compiler_params=pltpu.CompilerParams(vmem_limit_bytes=32 << 20),
    )(lengths, *sums, out_band)
    gains = lax.dynamic_slice_in_dim(small, lax.axis_index("blk") * (width // CHIPS), width // CHIPS, 1)
    return (output, x_band, g_query, g_key, g_value, g_output, g_gate, g_up, g_down, gains[0], gains[1])


VMEM_BYTES = 65 << 20


def turn_tables(length, head_dim):
    half_dim = head_dim // 2
    steps = np.arange(half_dim, dtype=np.float32) * np.float32(-2.0 * math.log(10000.0) / head_dim)
    angles = np.arange(length, dtype=np.float32)[:, None] * np.exp(steps)[None, :]
    cosine, sine = np.cos(angles), np.sin(angles)
    return (
        np.concatenate([cosine] * 4, axis=1).astype(np.float32),
        np.concatenate([-sine, sine, -sine, sine], axis=1).astype(np.float32),
    )


def solution(mesh):
    layer = item_layer if dict(mesh.shape) == {'dp': 8, 'blk': 4} else band_layer
    placed = (
        P("dp", "blk", None),
        P("dp", "blk", None),
        P("dp"),
        P(),
        P(),
        P(),
        P(),
        P(),
        P(),
        P(),
        P(),
        P(),
    )
    return jax.shard_map(
        layer,
        mesh=mesh,
        in_specs=placed,
        out_specs=(
            P("dp", "blk", None),
            P("dp", "blk", None),
            P("blk", None),
            P("blk", None),
            P("blk", None),
            P("blk", None),
            P("blk", None),
            P("blk", None),
            P("blk", None),
            P("blk"),
            P("blk"),
        ),
        check_vma=False,
    )
```

```python
import functools
import math
from types import SimpleNamespace

import jax
import jax.numpy as jnp
import numpy as np
from jax import lax
from jax.experimental import pallas as pl
from jax.experimental.pallas import tpu as pltpu
from jax.sharding import PartitionSpec as P

HEADS = 12


epsilon = 1e-05
masked_value = -1e30


def shifted(value, axis, by):
    size = lax.axis_size(axis)
    pairs = [(i, i + by) for i in range(size) if 0 <= i + by < size]
    return lax.ppermute(value, axis, pairs)


def tables(positions, head_dim):
    half_dim = head_dim // 2
    frequency = jnp.exp(
        jnp.arange(half_dim, dtype=jnp.float32) * (-2.0 * math.log(10000.0) / head_dim)
    )
    angles = positions[:, None] * frequency[None, :]
    return (jnp.cos(angles), jnp.sin(angles))


def rotate(tensor, cosine_table, sine_table):
    half_dim = tensor.shape[-1] // 2
    first = tensor[..., :half_dim]
    second = tensor[..., half_dim:]
    cosine_b = cosine_table[:, None, :]
    sine_b = sine_table[:, None, :]
    return jnp.concatenate(
        [first * cosine_b - second * sine_b, first * sine_b + second * cosine_b], axis=-1
    )


def contract_rows(left, right):
    return lax.dot_general(
        left, right, (((0,), (0,)), ((), ())), preferred_element_type=jnp.float32
    )


def times_transposed(left, right):
    return lax.dot_general(
        left, right, (((1,), (1,)), ((), ())), preferred_element_type=jnp.float32
    )


def band_layer(
    tokens,
    cotangent,
    lengths,
    w_query,
    w_key,
    w_value,
    w_output,
    w_gate,
    w_up,
    w_down,
    gain_attn,
    gain_ffn,
):
    item_count, band_len, model_width = tokens.shape
    head_count = HEADS
    head_dim = model_width // head_count
    band_count = lax.axis_size("blk")
    band_index = lax.axis_index("blk")
    seq_len = band_len * band_count
    row_count = item_count * band_len
    score_scale = head_dim ** (-0.5)
    positions = band_index * band_len + jnp.arange(band_len, dtype=jnp.int32)
    valid_rows = (positions[None, :] < lengths[:, None]).astype(jnp.float32).reshape(row_count, 1)
    cosine_table, sine_table = tables(positions.astype(jnp.float32), head_dim)
    key_positions = jnp.arange(seq_len, dtype=jnp.int32)
    allowed = key_positions[None, :] <= positions[:, None]
    incoming = tokens.astype(jnp.float32).reshape(row_count, model_width)
    inv_one = lax.rsqrt(jnp.mean(incoming * incoming, axis=-1, keepdims=True) + epsilon)
    normed_one = (incoming * inv_one * gain_attn).astype(jnp.bfloat16)
    query = rotate(
        jnp.dot(normed_one, w_query, preferred_element_type=jnp.float32).reshape(
            item_count, band_len, head_count, head_dim
        ),
        cosine_table,
        sine_table,
    ).astype(jnp.bfloat16)
    key_own = rotate(
        jnp.dot(normed_one, w_key, preferred_element_type=jnp.float32).reshape(
            item_count, band_len, head_count, head_dim
        ),
        cosine_table,
        sine_table,
    ).astype(jnp.bfloat16)
    value_own = jnp.dot(normed_one, w_value, preferred_element_type=jnp.float32).astype(
        jnp.bfloat16
    )
    pair = jnp.concatenate(
        [
            key_own.reshape(item_count, band_len, model_width),
            value_own.reshape(item_count, band_len, model_width),
        ],
        axis=-1,
    )
    buffer = jnp.zeros((item_count, band_count, band_len, 2 * model_width), jnp.bfloat16)
    buffer = lax.dynamic_update_slice_in_dim(buffer, pair[:, None], band_index, 1)

    def cycle_step(turn_index, state):
        carried, buffer = state
        carried = shifted(carried, "blk", 1)
        source = band_index - turn_index
        placed = lax.dynamic_update_slice_in_dim(
            buffer, carried[:, None], jnp.maximum(source, 0), 1
        )
        buffer = jnp.where(source >= 0, placed, buffer)
        return (carried, buffer)

    _, buffer = lax.fori_loop(1, band_count, cycle_step, (pair, buffer))
    whole = buffer.reshape(item_count, seq_len, 2 * model_width)
    keys_all = whole[..., :model_width].reshape(item_count, seq_len, head_count, head_dim)
    values_all = whole[..., model_width:].reshape(item_count, seq_len, head_count, head_dim)
    scores = (
        jnp.einsum("iqhd,ikhd->ihqk", query, keys_all, preferred_element_type=jnp.float32)
        * score_scale
    )
    scores = jnp.where(allowed[None, None], scores, masked_value)
    highest_s = jnp.max(scores, axis=-1, keepdims=True)
    expo = jnp.exp(scores - highest_s)
    totals = jnp.sum(expo, axis=-1, keepdims=True)
    softmax_w = expo / totals
    attended = jnp.einsum(
        "ihqk,ikhd->iqhd",
        softmax_w.astype(jnp.bfloat16),
        values_all,
        preferred_element_type=jnp.float32,
    )
    attended = attended.astype(jnp.bfloat16).reshape(row_count, model_width)
    middle = incoming + jnp.dot(attended, w_output, preferred_element_type=jnp.float32)
    inv_two = lax.rsqrt(jnp.mean(middle * middle, axis=-1, keepdims=True) + epsilon)
    normed_two = (middle * inv_two * gain_ffn).astype(jnp.bfloat16)
    gate_pre = jnp.dot(normed_two, w_gate, preferred_element_type=jnp.float32)
    up_pre = jnp.dot(normed_two, w_up, preferred_element_type=jnp.float32)
    sigmoid_g = jax.nn.sigmoid(gate_pre)
    silu_g = gate_pre * sigmoid_g
    hidden = (silu_g * up_pre).astype(jnp.bfloat16)
    ffn_out = jnp.dot(hidden, w_down, preferred_element_type=jnp.float32)
    result = (middle + ffn_out) * valid_rows
    output = result.astype(jnp.bfloat16).reshape(item_count, band_len, model_width)
    grad_res = cotangent.astype(jnp.float32).reshape(row_count, model_width) * valid_rows
    grad_ffn = grad_res.astype(jnp.bfloat16)
    grad_down = contract_rows(hidden, grad_ffn)
    grad_hidden = times_transposed(grad_ffn, w_down)
    grad_gate_pre = (
        grad_hidden * up_pre * (sigmoid_g * (1.0 + gate_pre * (1.0 - sigmoid_g)))
    ).astype(jnp.bfloat16)
    grad_up_pre = (grad_hidden * silu_g).astype(jnp.bfloat16)
    grad_gate = contract_rows(normed_two, grad_gate_pre)
    grad_up = contract_rows(normed_two, grad_up_pre)
    grad_normed_two = times_transposed(grad_gate_pre, w_gate) + times_transposed(grad_up_pre, w_up)
    grad_gain_ffn = jnp.sum(grad_normed_two * middle * inv_two, axis=0)
    scaled_two = grad_normed_two * gain_ffn
    grad_middle = grad_res + inv_two * (
        scaled_two
        - middle * inv_two * inv_two * jnp.mean(scaled_two * middle, axis=-1, keepdims=True)
    )
    grad_branch = grad_middle.astype(jnp.bfloat16)
    grad_output = contract_rows(attended, grad_branch)
    grad_attended = (
        times_transposed(grad_branch, w_output)
        .astype(jnp.bfloat16)
        .reshape(item_count, band_len, head_count, head_dim)
    )
    again = (
        jnp.einsum("iqhd,ikhd->ihqk", query, keys_all, preferred_element_type=jnp.float32)
        * score_scale
    )
    again = jnp.where(allowed[None, None], again, masked_value)
    probable = jnp.exp(again - highest_s) / totals
    grad_probs = jnp.einsum(
        "iqhd,ikhd->ihqk", grad_attended, values_all, preferred_element_type=jnp.float32
    )
    row_delta = jnp.sum(probable * grad_probs, axis=-1, keepdims=True)
    grad_scores = (probable * (grad_probs - row_delta)).astype(jnp.bfloat16)
    grad_query = (
        jnp.einsum("ihqk,ikhd->iqhd", grad_scores, keys_all, preferred_element_type=jnp.float32)
        * score_scale
    )
    grad_values = jnp.einsum(
        "ihqk,iqhd->ikhd",
        probable.astype(jnp.bfloat16),
        grad_attended,
        preferred_element_type=jnp.float32,
    )
    grad_keys = (
        jnp.einsum("ihqk,iqhd->ikhd", grad_scores, query, preferred_element_type=jnp.float32)
        * score_scale
    )
    grad_pair = jnp.concatenate(
        [
            grad_keys.reshape(item_count, seq_len, model_width),
            grad_values.reshape(item_count, seq_len, model_width),
        ],
        axis=-1,
    )
    blocks = grad_pair.reshape(item_count, band_count, band_len, 2 * model_width)
    empty_block = jnp.zeros((item_count, band_len, 2 * model_width), jnp.float32)

    def block_of(index):
        picked = lax.dynamic_index_in_dim(blocks, jnp.maximum(index, 0), 1, keepdims=False)
        return jnp.where(index >= 0, picked, empty_block)

    def cycle_back(turn_index, carried):
        carried = shifted(carried.astype(jnp.bfloat16), "blk", -1).astype(carried.dtype)
        return carried + block_of(band_index - (band_count - 1) + turn_index)

    own_grads = lax.fori_loop(1, band_count, cycle_back, block_of(band_index - (band_count - 1)))
    grad_key_own = own_grads[..., :model_width].reshape(item_count, band_len, head_count, head_dim)
    grad_value_raw = (
        own_grads[..., model_width:].astype(jnp.bfloat16).reshape(row_count, model_width)
    )
    grad_key_raw = (
        rotate(grad_key_own, cosine_table, -sine_table)
        .astype(jnp.bfloat16)
        .reshape(row_count, model_width)
    )
    grad_query_raw = (
        rotate(grad_query, cosine_table, -sine_table)
        .astype(jnp.bfloat16)
        .reshape(row_count, model_width)
    )
    grad_wquery = contract_rows(normed_one, grad_query_raw)
    grad_wkey = contract_rows(normed_one, grad_key_raw)
    grad_wvalue = contract_rows(normed_one, grad_value_raw)
    grad_normed_one = (
        times_transposed(grad_query_raw, w_query)
        + times_transposed(grad_key_raw, w_key)
        + times_transposed(grad_value_raw, w_value)
    )
    grad_gain_attn = jnp.sum(grad_normed_one * incoming * inv_one, axis=0)
    scaled_one = grad_normed_one * gain_attn
    grad_incoming = grad_middle + inv_one * (
        scaled_one
        - incoming * inv_one * inv_one * jnp.mean(scaled_one * incoming, axis=-1, keepdims=True)
    )
    grad_tokens = grad_incoming.astype(jnp.bfloat16).reshape(item_count, band_len, model_width)
    summed = (
        lax.psum_scatter(
            grad_wquery.astype(jnp.bfloat16), "blk", scatter_dimension=0, tiled=True
        ).astype(jnp.float32),
        lax.psum_scatter(
            grad_wkey.astype(jnp.bfloat16), "blk", scatter_dimension=0, tiled=True
        ).astype(jnp.float32),
        lax.psum_scatter(
            grad_wvalue.astype(jnp.bfloat16), "blk", scatter_dimension=0, tiled=True
        ).astype(jnp.float32),
        lax.psum_scatter(
            grad_output.astype(jnp.bfloat16), "blk", scatter_dimension=0, tiled=True
        ).astype(jnp.float32),
        lax.psum_scatter(
            grad_gate.astype(jnp.bfloat16), "blk", scatter_dimension=0, tiled=True
        ).astype(jnp.float32),
        lax.psum_scatter(
            grad_up.astype(jnp.bfloat16), "blk", scatter_dimension=0, tiled=True
        ).astype(jnp.float32),
        lax.psum_scatter(
            grad_down.astype(jnp.bfloat16), "blk", scatter_dimension=0, tiled=True
        ).astype(jnp.float32),
        lax.psum_scatter(
            grad_gain_attn.astype(jnp.bfloat16), "blk", scatter_dimension=0, tiled=True
        ).astype(jnp.float32),
        lax.psum_scatter(
            grad_gain_ffn.astype(jnp.bfloat16), "blk", scatter_dimension=0, tiled=True
        ).astype(jnp.float32),
    )
    summed = (
        lax.psum(summed[0].astype(jnp.bfloat16), "dp").astype(jnp.float32),
        lax.psum(summed[1].astype(jnp.bfloat16), "dp").astype(jnp.float32),
        lax.psum(summed[2].astype(jnp.bfloat16), "dp").astype(jnp.float32),
        lax.psum(summed[3].astype(jnp.bfloat16), "dp").astype(jnp.float32),
        lax.psum(summed[4].astype(jnp.bfloat16), "dp").astype(jnp.float32),
        lax.psum(summed[5].astype(jnp.bfloat16), "dp").astype(jnp.float32),
        lax.psum(summed[6].astype(jnp.bfloat16), "dp").astype(jnp.float32),
        lax.psum(summed[7].astype(jnp.bfloat16), "dp").astype(jnp.float32),
        lax.psum(summed[8].astype(jnp.bfloat16), "dp").astype(jnp.float32),
    )
    return (
        output,
        grad_tokens,
        summed[0],
        summed[1],
        summed[2],
        summed[3],
        summed[4],
        summed[5],
        summed[6],
        summed[7],
        summed[8],
    )


MESH = pl.DeviceIdType.MESH
ITEM, BAND = "dp", "blk"
CORES = 2
CHIPS = 4
BLOCK = 256
PAIR = 128
LOW = jnp.bfloat16
F32 = jnp.float32


def place():
    dp = lax.axis_index(ITEM)
    return dp, lax.axis_index(BAND), lax.rem(dp, CORES)


def near(dp, blk, core=0, chip=0, line=0):
    flip = core + CORES * line
    return {ITEM: dp ^ flip if flip else dp, BAND: blk ^ chip if chip else blk}


def greet(dp, blk, flips):
    barrier = pltpu.get_barrier_semaphore()
    for flip in flips:
        pl.semaphore_signal(barrier, inc=1, device_id=near(dp, blk, *flip), device_id_type=MESH)
    pl.semaphore_wait(barrier, len(flips))


def remote(src, dst, send, recv, where):
    return pltpu.make_async_remote_copy(
        src_ref=src, dst_ref=dst, send_sem=send, recv_sem=recv, device_id=where, device_id_type=MESH
    )


def part(start, size):
    return pl.ds(pl.multiple_of(start, size), size)


PLANE = [(core, chip, 0) for chip in range(CHIPS) for core in range(CORES) if core or chip]
REACH = PLANE + [(0, 0, 1), (0, 0, 3)]


def plus(one, other, kind=LOW):
    return (one.astype(F32) + other.astype(F32)).astype(kind)


class Gather:
    SEMS = [(2,), (4, 2), (4,), (4,), (4,)]

    def __init__(self, band, buf, sems):
        self.band, self.buf = band, buf
        self.own, self.send, self.recv, self.fsend, self.frecv = sems
        self.dp, self.blk, self.core = place()
        self.rows = band.shape[1]
        self.half = self.rows // 2
        self.mine = (self.blk // 2) == self.core

    def out(self, r, h):
        target = self.blk ^ r
        return remote(
            self.band.at[lax.rem(target, 2), pl.ds(h * self.half, self.half)],
            self.buf.at[part(self.blk * self.rows + h * self.half, self.half)],
            self.send.at[r, h],
            self.recv.at[r],
            {ITEM: self.dp - self.core + h, BAND: target},
        )

    def across(self, r):
        rows = self.buf.at[part((self.blk ^ r) * self.rows + self.core * self.half, self.half)]
        return remote(rows, rows, self.fsend.at[r], self.frecv.at[r], near(self.dp, self.blk, 1))

    def here(self):
        rows = self.buf.at[part(self.blk * self.rows, self.rows)]
        return pltpu.make_async_copy(self.band.at[lax.rem(self.blk, 2)], rows, self.own.at[0])

    def there(self):
        rows = self.buf.at[part(self.blk * self.rows, self.rows)]
        src = self.band.at[lax.rem(self.blk, 2)]
        return remote(src, rows, self.fsend.at[0], self.frecv.at[0], near(self.dp, self.blk, 1))

    def sends(self, r):
        return ((self.blk ^ r) // 2) == self.core

    def start(self):
        for r in (1, 2, 3):

            @pl.when(self.sends(r))
            def _():
                for h in range(2):
                    self.out(r, h).start()

        @pl.when(self.mine)
        def _():
            self.here().start()
            self.there().start()

    def forward(self, r):
        self.out(r, 0).wait_recv()
        self.across(r).start()

    def ready(self, r):
        if r:
            self.across(r).wait_recv()
            return

        @pl.when(self.mine)
        def _():
            self.here().wait()

        @pl.when(jnp.logical_not(self.mine))
        def _():
            self.there().wait_recv()

    def drain(self):
        @pl.when(self.mine)
        def _():
            self.there().wait_send()

        for r in (1, 2, 3):
            self.across(r).wait_send()

            @pl.when(self.sends(r))
            def _():
                for h in range(2):
                    self.out(r, h).wait_send()


class Return:
    SEMS = [(1,), (4,), (2, 2)]

    def __init__(self, src, band, sems):
        self.src, self.band = src, band
        self.own, self.send, self.recv = sems
        self.dp, self.blk, self.core = place()
        self.half = src.shape[1]
        self.home = self.blk // 2

    def slot(self):
        return self.band.at[lax.rem(self.blk, 2), part(self.core * self.half, self.half)]

    def out(self, r):
        chip = self.blk ^ r
        return remote(
            self.src.at[chip],
            self.slot(),
            self.send.at[r],
            self.recv.at[lax.rem(self.blk, 2), self.core],
            {ITEM: self.dp - self.core + self.home, BAND: chip},
        )

    def keep(self):
        return pltpu.make_async_copy(self.src.at[self.blk], self.slot(), self.own.at[0])

    def start(self):
        for r in (3, 1, 2):
            self.out(r).start()

        @pl.when(self.home == self.core)
        def _():
            self.keep().start()

        @pl.when(self.home != self.core)
        def _():
            self.out(0).start()

    def drain(self):
        @pl.when(self.home == self.core)
        def _():
            self.keep().wait()

        @pl.when(self.home != self.core)
        def _():
            self.out(0).wait_send()

        for r in (1, 2, 3):
            self.out(r).wait_send()

    def arrived(self):
        for i in range(2):
            for h in range(2):
                local = (self.core * 2 + i == self.blk) & (self.core == h)

                @pl.when(jnp.logical_not(local))
                def _():
                    remote(
                        self.src.at[0],
                        self.band.at[i, pl.ds(h * self.half, self.half)],
                        self.send.at[0],
                        self.recv.at[i, h],
                        near(self.dp, self.blk, 1),
                    ).wait_recv()


class Line:
    def locate(self):
        self.dp, self.blk, self.core = place()
        z = self.dp // CORES
        self.outer = (z == 0) | (z == 3)
        self.inner = jnp.logical_not(self.outer)

    def stage(self, n):
        (self.stage0, self.stage1, self.stage2, self.stage3, self.stage4, self.stage5, self.stage6)[n]()


class Chunk(Line):
    SEMS = [(2, 2, 2), (2, 2), (3, 2, 2), (2, 3)]

    def __init__(self, src, buffers, result, sems, turned=False):
        self.src, self.result, self.turned = src, result, turned
        self.first, self.second, self.line = buffers
        self.s1, self.s2, self.sz, self.sc = sems
        self.locate()

    @staticmethod
    def shapes(rows, cols, turned):
        half = (rows // 2, cols // CHIPS) if turned else (rows // CHIPS // 2, cols)
        return [(2, 2) + half, (2,) + half, (2, 2) + half], (CORES, 2) + half

    def piece(self, chip, h):
        rows, cols = self.first.shape[2:]
        if self.turned:
            return self.src.at[pl.ds(h * rows, rows), part(chip * cols, cols)]
        return self.src.at[part(chip * 2 * rows + h * rows, rows)]

    def ways(self, h):
        return (1, 2) if h == 0 else (2, 1)

    def step1(self, h, n):
        near_way, far_way = self.ways(h)
        chip = self.blk ^ near_way ^ (far_way if n else 0)
        return remote(
            self.piece(chip, h), self.first.at[h, n], self.s1.at[0, h, n], self.s1.at[1, h, n],
            near(self.dp, self.blk, 0, near_way),
        )

    def step2(self, h):
        return remote(
            self.first.at[h, 1], self.second.at[h], self.s2.at[0, h], self.s2.at[1, h],
            near(self.dp, self.blk, 0, self.ways(h)[1]),
        )

    def hop(self, n, h):
        src = (self.second.at[h], self.line.at[0, h], self.second.at[h])[n]
        dst = self.line.at[1 if n == 1 else 0, h]
        return remote(
            src, dst, self.sz.at[n, h, 0], self.sz.at[n, h, 1],
            near(self.dp, self.blk, 0, 0, 3 if n == 1 else 1),
        )

    def share(self, total, h):
        slot = self.result.at[self.core, h]
        return (
            remote(total, slot, self.sc.at[h, 0], self.sc.at[h, 1], near(self.dp, self.blk, 1)),
            pltpu.make_async_copy(total, slot, self.sc.at[h, 2]),
        )

    def xy_start(self):
        for n in (1, 0):
            for h in range(2):
                self.step1(h, n).start()

    def xy_turn(self):
        for h in range(2):
            self.step1(h, 1).wait_recv()
            chip = self.blk ^ self.ways(h)[1]
            self.first[h, 1] = plus(self.first[h, 1], self.piece(chip, h)[...])
            self.step2(h).start()

    def xy_end(self, h):
        self.step1(h, 0).wait_recv()
        self.step2(h).wait_recv()
        own = plus(self.first[h, 0], self.piece(self.blk, h)[...], F32)
        self.second[h] = plus(own, self.second[h])

    def xy_drain(self):
        for h in range(2):
            for n in range(2):
                self.step1(h, n).wait_send()
            self.step2(h).wait_send()

    def stage0(self):
        self.xy_start()

    def stage1(self):
        self.xy_turn()

    def stage2(self):
        for h in range(2):
            self.xy_end(h)

            @pl.when(self.outer)
            def _():
                self.hop(0, h).start()

    def stage3(self):
        @pl.when(self.inner)
        def _():
            for h in range(2):
                self.hop(0, h).wait_recv()
                self.line[0, h] = plus(self.line[0, h], self.second[h])
                self.hop(1, h).start()

    def stage4(self):
        @pl.when(self.inner)
        def _():
            for h in range(2):
                self.hop(1, h).wait_recv()
                self.second[h] = plus(self.line[0, h], self.line[1, h])
                self.hop(2, h).start()
                for copy in self.share(self.second.at[h], h):
                    copy.start()

    def stage5(self):
        @pl.when(self.outer)
        def _():
            for h in range(2):
                self.hop(2, h).wait_recv()
                for copy in self.share(self.line.at[0, h], h):
                    copy.start()

    def stage6(self):
        for h in range(2):
            for copy in self.share(self.second.at[h], h):
                copy.wait()
        self.xy_drain()

        @pl.when(self.outer)
        def _():
            for h in range(2):
                self.hop(0, h).wait_send()

        @pl.when(self.inner)
        def _():
            for h in range(2):
                self.hop(1, h).wait_send()
                self.hop(2, h).wait_send()


class PairChunk(Chunk):
    SEMS = [(CHIPS, 2), (2, 2, 2), (2, 2), (2, 2), (3,)]

    def __init__(self, src, buffers, result, sems, turned=False):
        self.src, self.result, self.turned = src, result, turned
        self.pair, self.first, self.second, self.line, self.total = buffers
        self.sp, self.s1, self.s2, self.sz, self.sc = sems
        self.locate()
        self.kept = lax.rem((self.dp // CORES + 1) // 2, 2)

    @staticmethod
    def shapes(rows, cols, turned):
        whole = (rows // 2, cols // CHIPS) if turned else (rows // CHIPS // 2, cols)
        half = (whole[0] // 2, whole[1])
        return [(CHIPS,) + whole, (2, 2) + half, (2,) + half, (2,) + half, (2, 2) + half], (CORES, 2, 2) + half

    def share_of(self, chip, s):
        rows, cols = self.pair.shape[1:]
        if self.turned:
            return self.src.at[part(s * rows, rows), pl.ds(chip * cols, cols)]
        return self.src.at[part(chip * 2 * rows + s * rows, rows)]

    def piece(self, chip, h):
        rows = self.pair.shape[1] // 2
        return self.pair.at[chip, pl.ds(h * rows, rows)]

    def swap(self, chip):
        return remote(
            self.share_of(chip, 1 - self.kept), self.pair.at[chip], self.sp.at[chip, 0], self.sp.at[chip, 1],
            near(self.dp, self.blk, 0, 0, 1),
        )

    def middle(self):
        return remote(
            self.second, self.line, self.sz.at[0, 0], self.sz.at[0, 1], near(self.dp, self.blk, 0, 0, 3)
        )

    def hand(self):
        half = self.total.at[self.kept]
        return remote(half, half, self.sz.at[1, 0], self.sz.at[1, 1], near(self.dp, self.blk, 0, 0, 1))

    def spread(self):
        slot = self.result.at[self.core]
        return (
            remote(self.total, slot, self.sc.at[0], self.sc.at[1], near(self.dp, self.blk, 1)),
            pltpu.make_async_copy(self.total, slot, self.sc.at[2]),
        )

    def stage0(self):
        for chip in range(CHIPS):
            self.swap(chip).start()

    def stage1(self):
        for chip in range(CHIPS):
            self.swap(chip).wait_recv()
            self.pair[chip] = plus(self.pair[chip], self.share_of(chip, self.kept)[...])
        self.xy_start()

    def stage2(self):
        self.xy_turn()

    def stage3(self):
        for h in range(2):
            self.xy_end(h)
        self.middle().start()

    def stage4(self):
        self.middle().wait_recv()
        for h in range(2):
            self.total[self.kept, h] = plus(self.second[h], self.line[h])
        self.hand().start()

    def stage5(self):
        self.hand().wait_recv()
        for copy in self.spread():
            copy.start()

    def stage6(self):
        for copy in self.spread():
            copy.wait()
        for chip in range(CHIPS):
            self.swap(chip).wait_send()
        self.xy_drain()
        self.middle().wait_send()
        self.hand().wait_send()


class Small(Line):
    SEMS = [(6, 2)]
    SLOTS = 11

    def __init__(self, hold, result, sems):
        self.hold, self.result = hold, result
        (self.sem,) = sems
        self.locate()

    def go(self, n):
        flips = ((1, 0, 0), (0, 1, 0), (0, 2, 0), (0, 0, 1), (0, 0, 3), (0, 0, 1))
        src, dst = (10, 10) if n == 5 else (2 * n, 2 * n + 1)
        return remote(
            self.hold.at[src], self.hold.at[dst], self.sem.at[n, 0], self.sem.at[n, 1],
            near(self.dp, self.blk, *flips[n]),
        )

    def add(self, n, to):
        self.go(n).wait_recv()
        self.hold[to] = self.hold[2 * n] + self.hold[2 * n + 1]

    def stage0(self):
        self.go(0).start()

    def stage1(self):
        for n in range(2):
            self.add(n, 2 * n + 2)
            self.go(n + 1).start()

    def stage2(self):
        self.add(2, 6)

        @pl.when(self.outer)
        def _():
            self.go(3).start()

    def stage3(self):
        @pl.when(self.inner)
        def _():
            self.add(3, 8)
            self.go(4).start()

    def stage4(self):
        @pl.when(self.inner)
        def _():
            self.add(4, 10)
            self.go(5).start()

    def stage5(self):
        @pl.when(self.outer)
        def _():
            self.go(5).wait_recv()

        self.result[...] = self.hold[10]

    def stage6(self):
        for n in range(3):
            self.go(n).wait_send()

        @pl.when(self.outer)
        def _():
            self.go(3).wait_send()

        @pl.when(self.inner)
        def _():
            self.go(4).wait_send()
            self.go(5).wait_send()


def dot(left, right):
    return jnp.dot(left, right, preferred_element_type=F32)


def dot_rows(left, right):
    return lax.dot_general(left, right, (((0,), (0,)), ((), ())), preferred_element_type=F32)


def dot_cols(left, right):
    return lax.dot_general(left, right, (((1,), (1,)), ((), ())), preferred_element_type=F32)


def inverse_rms(values):
    return lax.rsqrt(jnp.mean(values * values, axis=-1, keepdims=True) + epsilon)


def turn(t, cosine, sine, sign):
    quarter = PAIR // 4
    lane = lax.broadcasted_iota(jnp.int32, t.shape, 1)
    other = jnp.where(
        lane % (2 * quarter) < quarter,
        pltpu.roll(t, PAIR - quarter, 1),
        pltpu.roll(t, quarter, 1),
    )
    return t * cosine + (sign * sine) * other


def both_heads(t):
    lane = lax.broadcasted_iota(jnp.int32, t.shape, 1)
    zero = jnp.zeros_like(t)
    return jnp.concatenate(
        [jnp.where(lane < PAIR // 2, t, zero), jnp.where(lane < PAIR // 2, zero, t)], axis=0
    )


def one_pair(t):
    rows = t.shape[0] // 2
    lane = lax.broadcasted_iota(jnp.int32, (rows, PAIR), 1)
    return jnp.where(lane < PAIR // 2, t[:rows], t[rows:])


FF0, FF1, FF2, FF3, DOWN, OUT, QUERY, KEY, VALUE, SMALL = range(10)
TILES = (FF0, FF1, FF2, FF3)
PAIRED = (FF0, OUT)
(
    TILE0, TILE1, TILE2, TILE3, GRAD_DOWN, PART_OUT, GRAD_N2, OWN_OUT, GRAD_MID, GRAD_OUT, GRAD_ATT,
    HEADS0, HEADS1, HEADS2, GRAD_QKV, PART_N1, OWN_N1, SEND_OUT, SEND_X,
) = range(100, 119)
ORDER = (
    TILE0, FF0, TILE1, FF1, TILE2, TILE3, FF1, GRAD_DOWN, DOWN, PART_OUT, GRAD_N2, OWN_OUT, FF1, GRAD_MID, FF0,
    GRAD_OUT, GRAD_ATT, FF0, OUT, FF1, DOWN, HEADS0, FF2, FF0, HEADS1, DOWN, FF1, FF3, OUT, HEADS2, FF2, GRAD_QKV,
    FF1, KEY, DOWN, OUT, FF0, FF3, FF2, QUERY, PART_N1, KEY, FF2, DOWN, OUT, FF3, VALUE, OWN_N1, QUERY, FF2, SMALL,
    VALUE, FF3, KEY, FF0, SMALL, KEY, SEND_X, QUERY, OUT, DOWN, FF3, SMALL, VALUE, SEND_OUT, QUERY, FF3, QUERY,
    VALUE, OUT, KEY, VALUE, QUERY, SMALL, VALUE, KEY, FF2, SMALL, SMALL,
)


def layout(width, ff):
    seq = CHIPS * BLOCK
    half = width // 2
    pairs = half // PAIR

    def low(*shape):
        return pltpu.VMEM(shape, LOW)

    def wide(*shape):
        return pltpu.VMEM(shape, F32)

    grads, sums = [], []
    keep = dict(
        w_qkv=low(width, 3 * half), w_out=low(width, width), w_ff=low(width, 2 * ff),
        w_down=low(ff, width), turns=wide(2, seq, PAIR),
        x=low(seq, width), g_ffn=low(seq, width), n1=low(seq, width),
        q=low(seq, half), k=low(seq, half), v=low(seq, half),
        prob=[low(pairs, 2 * BLOCK, (i + 1) * BLOCK) for i in range(CHIPS)],
        att=low(seq, width), middle=wide(seq, width), n2=low(seq, width), n2_turned=low(width, seq),
        hidden=low(seq, ff), g_ff=low(seq, 2 * ff), share=wide(seq, PAIR), gn2=low(seq, width),
        swap_out=low(CHIPS, BLOCK // 2, width), swap_in=low(2, CHIPS, BLOCK // 2, width),
        band=low(CHIPS, BLOCK // 2, width),
        dk=wide(seq, PAIR), dv=wide(seq, PAIR), hold=wide(Small.SLOTS, 8, width),
        grad=grads, sums=sums,
    )
    sems = dict(
        load=[(17,)], gather_x=Gather.SEMS, gather_g=Gather.SEMS, att=[(2, pairs)], swap=[(2, 2)], gn2=[(2, CHIPS)],
        back_out=Return.SEMS, back_x=Return.SEMS, small=Small.SEMS,
        sums=[PairChunk.SEMS if name in PAIRED else Chunk.SEMS for name in range(SMALL)],
    )
    sems = jax.tree.map(pltpu.SemaphoreType.DMA, sems, is_leaf=lambda t: isinstance(t, tuple))
    results = []
    for name in range(SMALL):
        cols = ff if name == DOWN else 2 * (ff // CHIPS) if name in TILES else half
        kind = PairChunk if name in PAIRED else Chunk
        shapes, result = kind.shapes(width, cols, name == DOWN)
        results.append(result)
        grads.append(low(width, cols))
        sums.append([low(*shape) for shape in shapes])
    return keep, sems, results


def layer_kernel(
    scratch, tokens, cotangent, lengths, turns, gain_attn, gain_ffn,
    w_query, w_key, w_value, w_output, w_gate, w_up, w_down, *refs,
):
    width, ff = tokens.shape[2], w_gate.shape[1] // CORES
    results, (small_result, out_band, x_band) = refs[:SMALL], refs[SMALL : SMALL + 3]
    keep, sems = jax.tree.unflatten(scratch, refs[SMALL + 3 :])
    m, sem = SimpleNamespace(**keep), SimpleNamespace(**sems)
    dp, blk, core = place()
    partner = near(dp, blk, 1)
    half = width // 2
    pairs = half // PAIR
    scale = (width // HEADS) ** (-0.5)
    mine = pl.multiple_of(core * half, half)

    def block(r):
        return part(r * BLOCK, BLOCK)

    def half_block(chip, c):
        return part(chip * BLOCK + c * (BLOCK // 2), BLOCK // 2)

    def lanes(p):
        return part(p * PAIR, PAIR)

    loads = []

    def load(src, dst):
        copy = pltpu.make_async_copy(src, dst, sem.load[0].at[len(loads)])
        copy.start()
        loads.append(copy)

    load(turns, m.turns)
    for n, weight in enumerate((w_query, w_key, w_value)):
        load(weight.at[:, pl.ds(mine, half)], m.w_qkv.at[:, pl.ds(n * half, half)])

    gather_x = Gather(tokens, m.x, sem.gather_x)
    gather_g = Gather(m.band.reshape(2, BLOCK, width), m.g_ffn, sem.gather_g)
    greet(dp, blk, REACH)
    gather_x.start()
    load(w_output, m.w_out)
    unit = ff // CHIPS
    for chip in range(CHIPS):
        there = part(chip * CORES * unit + core * unit, unit)
        load(w_up.at[:, there], m.w_ff.at[:, pl.ds(2 * chip * unit, unit)])
        load(w_gate.at[:, there], m.w_ff.at[:, pl.ds((2 * chip + 1) * unit, unit)])
        load(w_down.at[there], m.w_down.at[pl.ds(chip * unit, unit)])
    for i in range(2):
        row = blk * BLOCK + lax.broadcasted_iota(jnp.int32, (BLOCK, width), 0)
        masked = jnp.where(row < lengths[i], cotangent[i].astype(F32), 0.0)
        for h in range(2):
            m.band[2 * i + h] = masked[h * (BLOCK // 2) : (h + 1) * (BLOCK // 2)].astype(LOW)
    for copy in loads[:4]:
        copy.wait()

    def project(r):
        rows = block(blk ^ r)
        x = m.x[rows].astype(F32)
        n1 = (x * inverse_rms(x) * gain_attn[...][None]).astype(LOW)
        m.n1[rows] = n1
        cosine, sine = m.turns[0, rows], m.turns[1, rows]
        for n, store in enumerate((m.q, m.k, m.v)):
            full = dot(n1, m.w_qkv[:, n * half : (n + 1) * half])
            for p in range(pairs):
                t = full[:, p * PAIR : (p + 1) * PAIR]
                if n < 2:
                    t = turn(t, cosine, sine, 1.0)
                if n == 0:
                    t = t.astype(LOW).astype(F32) * scale
                store[rows, p * PAIR : (p + 1) * PAIR] = t.astype(LOW)

    gather_x.ready(0)
    project(0)
    gather_x.forward(1)
    gather_x.forward(2)
    gather_x.ready(1)
    project(1)
    gather_x.forward(3)
    gather_x.ready(2)
    project(2)
    gather_x.ready(3)
    gather_g.start()
    project(3)

    row = lax.broadcasted_iota(jnp.int32, (2 * BLOCK, BLOCK), 0) % BLOCK
    seen = lax.broadcasted_iota(jnp.int32, (2 * BLOCK, BLOCK), 1) <= row

    lane = lax.broadcasted_iota(jnp.int32, (BLOCK, PAIR), 1)

    def att_cols(p):
        return part(core * half + p * PAIR, PAIR)

    def att_copy(p):
        cols = m.att.at[:, att_cols(p)]
        return remote(cols, cols, sem.att[0].at[0, p], sem.att[0].at[1, p], partner)

    @pl.loop(0, pairs)
    def _(p):
        for i in range(CHIPS):
            size = BLOCK * i
            q = both_heads(m.q[pl.ds(size, BLOCK), lanes(p)])
            own = dot_cols(q, m.k[pl.ds(size, BLOCK), lanes(p)])
            own = jnp.where(seen, own, masked_value)
            top = jnp.max(own, axis=-1, keepdims=True)
            if i:
                past = dot_cols(q, m.k[pl.ds(0, size), lanes(p)])
                top = jnp.maximum(top, jnp.max(past, axis=-1, keepdims=True))
                past = jnp.exp(past - top)
            own = jnp.exp(own - top)
            total = jnp.sum(own, axis=-1, keepdims=True)
            if i:
                total = total + jnp.sum(past, axis=-1, keepdims=True)
            share = 1.0 / total
            kept = m.share[pl.ds(size, BLOCK)]
            kept = jnp.where(lane == 2 * p, share[:BLOCK], kept)
            m.share[pl.ds(size, BLOCK)] = jnp.where(lane == 2 * p + 1, share[BLOCK:], kept)
            prob = m.prob[i]
            own = own.astype(LOW)
            prob[p, :, pl.ds(size, BLOCK)] = own
            att = dot(own, m.v[pl.ds(size, BLOCK), lanes(p)])
            if i:
                past = past.astype(LOW)
                prob[p, :, pl.ds(0, size)] = past
                att = att + dot(past, m.v[pl.ds(0, size), lanes(p)])
            m.att[pl.ds(size, BLOCK), att_cols(p)] = one_pair(att * share).astype(LOW)
        att_copy(p).start()

    for r in (1, 2, 3):
        gather_g.forward(r)
    loads[4].wait()
    for p in range(pairs):
        att_copy(p).wait_recv()

    @pl.loop(0, CHIPS)
    def _(r):
        rows = block(r)
        middle = m.x[rows].astype(F32) + dot(m.att[rows], m.w_out[...])
        m.middle[rows] = middle
        n2 = (middle * inverse_rms(middle) * gain_ffn[...][None]).astype(LOW)
        m.n2[rows] = n2
        m.n2_turned[:, rows] = n2.T

    for r in range(CHIPS):
        gather_g.ready(r)
    for copy in loads[5:]:
        copy.wait()

    sums = []
    for name in range(SMALL):
        own = (m.grad[name], m.sums[name], results[name], sem.sums[name])
        sums.append((PairChunk if name in PAIRED else Chunk)(*own, name == DOWN))
    sums.append(Small(m.hold, small_result, sem.small))
    done = [0] * len(sums)

    def advance(*names):
        for name in names:
            sums[name].stage(done[name])
            done[name] += 1

    def tile(t):
        units, both = block(t), part(t * 2 * BLOCK, 2 * BLOCK)

        @pl.loop(0, CHIPS)
        def _(r):
            rows = block(r)
            pre = dot(m.n2[rows], m.w_ff[:, both])
            up, gate = pre[:, :BLOCK], pre[:, BLOCK:]
            g_hidden = dot_cols(m.g_ffn[rows], m.w_down[units])
            sig = 0.5 * jnp.tanh(0.5 * gate) + 0.5
            silu = gate * sig
            m.hidden[rows, units] = (silu * up).astype(LOW)
            m.g_ff[rows, part(t * 2 * BLOCK, BLOCK)] = (g_hidden * silu).astype(LOW)
            g_gate = g_hidden * up * (sig * (1.0 + gate * (1.0 - sig)))
            m.g_ff[rows, part(t * 2 * BLOCK + BLOCK, BLOCK)] = g_gate.astype(LOW)

        for name in TILES:

            @pl.when(t == name)
            def _():
                for r in range(width // BLOCK):
                    rows = pl.ds(r * BLOCK, BLOCK)
                    m.grad[name][rows] = dot(m.n2_turned[rows], m.g_ff[:, both]).astype(LOW)

    def grad_down():
        @pl.loop(0, width // BLOCK)
        def _(t):
            rows = block(t)
            m.grad[DOWN][rows] = dot_rows(m.g_ffn[:, rows], m.hidden[...]).astype(LOW)

    def swap(n):
        return remote(m.swap_out, m.swap_in.at[n], sem.swap[0].at[n, 0], sem.swap[0].at[n, 1], partner)

    def part_out():
        @pl.loop(0, CHIPS)
        def _(chip):
            m.swap_out[chip] = dot(m.hidden[half_block(chip, 1 - core)], m.w_down[...]).astype(LOW)

        swap(0).start()

    back_out = Return(m.band, out_band, sem.back_out)
    back_x = Return(m.swap_out, x_band, sem.back_x)

    def own_out():
        swap(0).wait()
        gather_g.drain()

        @pl.loop(0, CHIPS)
        def _(chip):
            rows = half_block(chip, core)
            out = dot(m.hidden[rows], m.w_down[...]) + m.swap_in[0, chip].astype(F32)
            m.band[chip] = (m.middle[rows] + out).astype(LOW)

    def gn2_copy(r):
        return remote(
            m.n2.at[block(r)], m.gn2.at[block(r)], sem.gn2[0].at[0, r], sem.gn2[0].at[1, r], partner,
        )

    def grad_n2():
        @pl.loop(0, CHIPS)
        def _(r):
            m.n2[block(r)] = dot_cols(m.g_ff[block(r)], m.w_ff[...]).astype(LOW)
            gn2_copy(r).start()

    g_branch, g_mid = m.gn2, m.middle

    def grad_mid():
        m.hold[0] = jnp.zeros((8, width), F32)

        @pl.loop(0, CHIPS)
        def _(r):
            rows = block(r)
            gn2_copy(r).wait_recv()
            g_n2 = plus(m.n2[rows], m.gn2[rows], F32)
            middle = m.middle[rows]
            inv = inverse_rms(middle)
            m.hold[0, 1:2] += 0.5 * jnp.sum(g_n2 * middle * inv, axis=0, keepdims=True)
            a2 = g_n2 * gain_ffn[...][None]
            inner = jnp.mean(a2 * middle, axis=-1, keepdims=True)
            got = m.g_ffn[rows].astype(F32) + inv * (a2 - middle * (inv * inv * inner))
            g_branch[rows] = got.astype(LOW)
            g_mid[rows] = got

    def grad_out():
        @pl.loop(0, width // BLOCK)
        def _(t):
            rows = block(t)
            m.grad[OUT][rows] = dot_rows(m.att[:, rows], g_branch[:, pl.ds(mine, half)]).astype(LOW)

    g_att = m.hidden
    g_qkv = m.g_ff.at[:, pl.ds(0, 3 * half)]
    g_q, g_k, g_v = (m.g_ff.at[:, pl.ds(n * half, half)] for n in range(3))

    def grad_att():
        @pl.loop(0, CHIPS)
        def _(r):
            g_att[block(r), pl.ds(0, half)] = dot_cols(g_branch[block(r)], m.w_out[pl.ds(mine, half)]).astype(LOW)

    def heads(p):
        for i in range(CHIPS - 1, -1, -1):
            rows, size = pl.ds(BLOCK * i, BLOCK), BLOCK * (i + 1)
            past = pl.ds(0, size)
            kept = m.share[rows]
            share = jnp.concatenate(
                [
                    jnp.sum(jnp.where(lane == 2 * p + n, kept, 0.0), axis=-1, keepdims=True)
                    for n in range(2)
                ],
                axis=0,
            )
            g = both_heads(g_att[rows, lanes(p)]).astype(F32) * share
            q = both_heads(m.q[rows, lanes(p)])
            out = m.att[rows, att_cols(p)].astype(F32)
            delta = jnp.sum(g * jnp.concatenate([out, out], axis=0), axis=-1, keepdims=True)
            g = g.astype(LOW)
            prob = m.prob[i][p]
            g_prob = dot_cols(g, m.v[past, lanes(p)])
            g_score = (prob.astype(F32) * (g_prob - delta)).astype(LOW)
            got_q = one_pair(dot(g_score, m.k[past, lanes(p)])) * scale
            g_q[rows, lanes(p)] = turn(got_q, m.turns[0, rows], m.turns[1, rows], -1.0).astype(LOW)
            got_k, got_v = dot_rows(g_score, q), dot_rows(prob, g)
            if i == CHIPS - 1:
                m.dk[...] = got_k
                m.dv[...] = got_v
            else:
                m.dk[past] += got_k
                m.dv[past] += got_v
        for r in range(CHIPS):
            rows = pl.ds(BLOCK * r, BLOCK)
            g_k[rows, lanes(p)] = turn(m.dk[rows], m.turns[0, rows], m.turns[1, rows], -1.0).astype(LOW)
            g_v[rows, lanes(p)] = m.dv[rows].astype(LOW)

    def grad_qkv():
        @pl.loop(0, width // BLOCK)
        def _(t):
            rows = block(t)
            got = dot_rows(m.n1[:, rows], g_qkv[...]).astype(LOW)
            for n, name in enumerate((QUERY, KEY, VALUE)):
                m.grad[name][rows] = got[:, n * half : (n + 1) * half]

    def part_n1():
        @pl.loop(0, CHIPS)
        def _(chip):
            m.swap_out[chip] = dot_cols(g_qkv[half_block(chip, 1 - core)], m.w_qkv[...]).astype(LOW)

        swap(1).start()

    def own_n1():
        swap(1).wait()

        @pl.loop(0, CHIPS)
        def _(chip):
            rows = half_block(chip, core)
            got = dot_cols(g_qkv[rows], m.w_qkv[...]) + m.swap_in[1, chip].astype(F32)
            x = m.x[rows].astype(F32)
            inv = inverse_rms(x)
            m.hold[0, 0:1] += jnp.sum(got * x * inv, axis=0, keepdims=True)
            a1 = got * gain_attn[...][None]
            inner = jnp.mean(a1 * x, axis=-1, keepdims=True)
            m.swap_out[chip] = (g_mid[rows] + inv * (a1 - x * (inv * inv * inner))).astype(LOW)

    steps = {
        GRAD_DOWN: grad_down, PART_OUT: part_out, GRAD_N2: grad_n2, OWN_OUT: own_out, GRAD_MID: grad_mid,
        GRAD_OUT: grad_out, GRAD_ATT: grad_att, GRAD_QKV: grad_qkv, PART_N1: part_n1, OWN_N1: own_n1,
        SEND_OUT: back_out.start, SEND_X: back_x.start,
    }

    def do(name):
        if name <= SMALL:
            advance(name)
        else:
            steps[name]()

    def looped(body, first, last):
        gaps = [[]]
        for name in ORDER[ORDER.index(first) + 1 : ORDER.index(last)]:
            if first < name < last:
                gaps.append([])
            else:
                gaps[-1].append(name)

        @pl.loop(0, last - first + 1)
        def _(n):
            body(n)
            for at, gap in enumerate(gaps):
                if gap:

                    @pl.when(n == at)
                    def _():
                        for name in gap:
                            do(name)

    at = 0
    while at < len(ORDER):
        name = ORDER[at]
        if name == TILE0:
            looped(tile, TILE0, TILE3)
            at = ORDER.index(TILE3)
        elif name == HEADS0:
            looped(heads, HEADS0, HEADS2)
            at = ORDER.index(HEADS2)
        else:
            do(name)
        at += 1

    for total in sums:
        total.stage6()
    for p in range(pairs):
        att_copy(p).wait_send()
    for r in range(CHIPS):
        gn2_copy(r).wait_send()
    gather_x.drain()
    back_out.drain()
    back_x.drain()
    back_out.arrived()
    back_x.arrived()


def vmem_specs(count):
    return [pl.BlockSpec(memory_space=pltpu.VMEM)] * count


def any_specs(count):
    return [pl.BlockSpec(memory_space=pl.ANY)] * count


def finish_kernel(lengths, *refs):
    step = pl.program_id(0)
    blk = lax.axis_index(BAND)
    tiles, refs = refs[:CHIPS], refs[CHIPS:]
    down, output, query, key, value, out, back = refs[:7]
    r_out, r_back, r_query, r_key, r_value, r_output, r_gate, r_up, r_down = refs[7:]
    for src, dst in ((query, r_query), (key, r_key), (value, r_value), (output, r_output)):
        cols = src.shape[-1]
        for c in range(CORES):
            dst[:, c * cols : (c + 1) * cols] = src[c].astype(F32)
    for t, src in enumerate(tiles):
        for c in range(CORES):
            cols = pl.ds((t * CORES + c) * BLOCK, BLOCK)
            r_up[:, cols] = src[c, :, :BLOCK].astype(F32)
            r_gate[:, cols] = src[c, :, BLOCK:].astype(F32)
    r_back[...] = back[...]
    r_down[...] = down[0].astype(F32).T
    rows = out.shape[1]
    for i in range(2):
        place_ = blk * BLOCK + step * rows + lax.broadcasted_iota(jnp.int32, out.shape[1:], 0)
        r_out[i] = jnp.where(place_ < lengths[i], out[i].astype(F32), 0.0).astype(LOW)


def item_layer(
    tokens, cotangent, lengths, w_query, w_key, w_value, w_output, w_gate, w_up, w_down, gain_attn, gain_ffn
):
    width = tokens.shape[2]
    ff = w_gate.shape[1] // CORES
    half = width // 2
    keep, sems, results = layout(width, ff)
    scratch, tree = jax.tree.flatten((keep, sems))
    cosine, sine = turn_tables(CHIPS * BLOCK, width // HEADS)
    band = jax.ShapeDtypeStruct(tokens.shape, LOW)
    fins = pl.pallas_call(
        functools.partial(layer_kernel, tree),
        out_shape=[jax.ShapeDtypeStruct(shape, LOW) for shape in results]
        + [jax.ShapeDtypeStruct((8, width), F32), band, band],
        in_specs=any_specs(1) + vmem_specs(1) + [pl.BlockSpec(memory_space=pltpu.SMEM)] + any_specs(1)
        + vmem_specs(2) + any_specs(7),
        out_specs=any_specs(SMALL) + vmem_specs(1) + any_specs(2),
        scratch_shapes=scratch,
        compiler_params=pltpu.CompilerParams(
            collective_id=0, has_side_effects=True, vmem_limit_bytes=VMEM_BYTES
        ),
    )(
        tokens, cotangent, lengths, jnp.stack([cosine, sine]), gain_attn, gain_ffn,
        w_query, w_key, w_value, w_output, w_gate, w_up, w_down,
    )
    *sums, small, out_band, x_band = fins
    sums = [t.reshape(CORES, -1, t.shape[-1]) for t in sums]
    steps = 4
    rows = half // 2
    unit = ff // CHIPS

    def grad_spec(cols):
        return pl.BlockSpec((CORES, rows // steps, cols), lambda s: (0, s, 0))

    def wide_spec(cols):
        return pl.BlockSpec((rows // steps, cols), lambda s: (s, 0))

    band_spec = pl.BlockSpec((2, BLOCK // steps, width), lambda s: (0, s, 0))
    wide = lambda cols: jax.ShapeDtypeStruct((rows, cols), F32)
    output, g_tokens, g_query, g_key, g_value, g_output, g_gate, g_up, g_down = pl.pallas_call(
        finish_kernel,
        grid=(steps,),
        out_shape=[band] * 2 + [wide(width)] * 4 + [wide(2 * ff)] * 2
        + [jax.ShapeDtypeStruct((CORES * unit, width), F32)],
        in_specs=[pl.BlockSpec(memory_space=pltpu.SMEM)]
        + [grad_spec(2 * unit)] * CHIPS
        + [pl.BlockSpec((1, width, unit // 2), lambda s: (s // 2, 0, s % 2))] + [grad_spec(half)] * 4 + [band_spec] * 2,
        out_specs=[band_spec] * 2 + [wide_spec(width)] * 4 + [wide_spec(2 * ff)] * 2
        + [pl.BlockSpec((unit // 2, width), lambda s: (s, 0))],
        compiler_params=pltpu.CompilerParams(vmem_limit_bytes=VMEM_BYTES),
    )(lengths, *sums, out_band, x_band)
    gains = lax.dynamic_slice_in_dim(small, lax.axis_index(BAND) * (width // CHIPS), width // CHIPS, 1)
    return (output, g_tokens, g_query, g_key, g_value, g_output, g_gate, g_up, g_down, gains[0], gains[1])


VMEM_BYTES = 65 << 20


def turn_tables(length, head_dim):
    half_dim = head_dim // 2
    steps = np.arange(half_dim, dtype=np.float32) * np.float32(-2.0 * math.log(10000.0) / head_dim)
    angles = np.arange(length, dtype=np.float32)[:, None] * np.exp(steps)[None, :]
    cosine, sine = np.cos(angles), np.sin(angles)
    return (
        np.concatenate([cosine] * 4, axis=1).astype(np.float32),
        np.concatenate([-sine, sine, -sine, sine], axis=1).astype(np.float32),
    )


def solution(mesh):
    layer = item_layer if dict(mesh.shape) == {ITEM: 8, BAND: 4} else band_layer
    placed = (
        P("dp", "blk", None),
        P("dp", "blk", None),
        P("dp"),
        P(),
        P(),
        P(),
        P(),
        P(),
        P(),
        P(),
        P(),
        P(),
    )
    return jax.shard_map(
        layer,
        mesh=mesh,
        in_specs=placed,
        out_specs=(
            P("dp", "blk", None),
            P("dp", "blk", None),
            P("blk", None),
            P("blk", None),
            P("blk", None),
            P("blk", None),
            P("blk", None),
            P("blk", None),
            P("blk", None),
            P("blk"),
            P("blk"),
        ),
        check_vma=False,
    )
```

```python
import functools
import math
from types import SimpleNamespace

import jax
import jax.numpy as jnp
import numpy as np
from jax import lax
from jax.experimental import pallas as pl
from jax.experimental.pallas import tpu as pltpu
from jax.sharding import PartitionSpec as P

HEADS = 12


epsilon = 1e-05
masked_value = -1e30


def shifted(value, axis, by):
    size = lax.axis_size(axis)
    pairs = [(i, i + by) for i in range(size) if 0 <= i + by < size]
    return lax.ppermute(value, axis, pairs)


def tables(positions, head_dim):
    half_dim = head_dim // 2
    frequency = jnp.exp(
        jnp.arange(half_dim, dtype=jnp.float32) * (-2.0 * math.log(10000.0) / head_dim)
    )
    angles = positions[:, None] * frequency[None, :]
    return (jnp.cos(angles), jnp.sin(angles))


def rotate(tensor, cosine_table, sine_table):
    half_dim = tensor.shape[-1] // 2
    first = tensor[..., :half_dim]
    second = tensor[..., half_dim:]
    cosine_b = cosine_table[:, None, :]
    sine_b = sine_table[:, None, :]
    return jnp.concatenate(
        [first * cosine_b - second * sine_b, first * sine_b + second * cosine_b], axis=-1
    )


def contract_rows(left, right):
    return lax.dot_general(
        left, right, (((0,), (0,)), ((), ())), preferred_element_type=jnp.float32
    )


def times_transposed(left, right):
    return lax.dot_general(
        left, right, (((1,), (1,)), ((), ())), preferred_element_type=jnp.float32
    )


def band_layer(
    tokens,
    cotangent,
    lengths,
    w_query,
    w_key,
    w_value,
    w_output,
    w_gate,
    w_up,
    w_down,
    gain_attn,
    gain_ffn,
):
    item_count, band_len, model_width = tokens.shape
    head_count = HEADS
    head_dim = model_width // head_count
    band_count = lax.axis_size("blk")
    band_index = lax.axis_index("blk")
    seq_len = band_len * band_count
    row_count = item_count * band_len
    score_scale = head_dim ** (-0.5)
    positions = band_index * band_len + jnp.arange(band_len, dtype=jnp.int32)
    valid_rows = (positions[None, :] < lengths[:, None]).astype(jnp.float32).reshape(row_count, 1)
    cosine_table, sine_table = tables(positions.astype(jnp.float32), head_dim)
    key_positions = jnp.arange(seq_len, dtype=jnp.int32)
    allowed = key_positions[None, :] <= positions[:, None]
    incoming = tokens.astype(jnp.float32).reshape(row_count, model_width)
    inv_one = lax.rsqrt(jnp.mean(incoming * incoming, axis=-1, keepdims=True) + epsilon)
    normed_one = (incoming * inv_one * gain_attn).astype(jnp.bfloat16)
    query = rotate(
        jnp.dot(normed_one, w_query, preferred_element_type=jnp.float32).reshape(
            item_count, band_len, head_count, head_dim
        ),
        cosine_table,
        sine_table,
    ).astype(jnp.bfloat16)
    key_own = rotate(
        jnp.dot(normed_one, w_key, preferred_element_type=jnp.float32).reshape(
            item_count, band_len, head_count, head_dim
        ),
        cosine_table,
        sine_table,
    ).astype(jnp.bfloat16)
    value_own = jnp.dot(normed_one, w_value, preferred_element_type=jnp.float32).astype(
        jnp.bfloat16
    )
    pair = jnp.concatenate(
        [
            key_own.reshape(item_count, band_len, model_width),
            value_own.reshape(item_count, band_len, model_width),
        ],
        axis=-1,
    )
    buffer = jnp.zeros((item_count, band_count, band_len, 2 * model_width), jnp.bfloat16)
    buffer = lax.dynamic_update_slice_in_dim(buffer, pair[:, None], band_index, 1)

    def cycle_step(turn_index, state):
        carried, buffer = state
        carried = shifted(carried, "blk", 1)
        source = band_index - turn_index
        placed = lax.dynamic_update_slice_in_dim(
            buffer, carried[:, None], jnp.maximum(source, 0), 1
        )
        buffer = jnp.where(source >= 0, placed, buffer)
        return (carried, buffer)

    _, buffer = lax.fori_loop(1, band_count, cycle_step, (pair, buffer))
    whole = buffer.reshape(item_count, seq_len, 2 * model_width)
    keys_all = whole[..., :model_width].reshape(item_count, seq_len, head_count, head_dim)
    values_all = whole[..., model_width:].reshape(item_count, seq_len, head_count, head_dim)
    scores = (
        jnp.einsum("iqhd,ikhd->ihqk", query, keys_all, preferred_element_type=jnp.float32)
        * score_scale
    )
    scores = jnp.where(allowed[None, None], scores, masked_value)
    highest_s = jnp.max(scores, axis=-1, keepdims=True)
    expo = jnp.exp(scores - highest_s)
    totals = jnp.sum(expo, axis=-1, keepdims=True)
    softmax_w = expo / totals
    attended = jnp.einsum(
        "ihqk,ikhd->iqhd",
        softmax_w.astype(jnp.bfloat16),
        values_all,
        preferred_element_type=jnp.float32,
    )
    attended = attended.astype(jnp.bfloat16).reshape(row_count, model_width)
    middle = incoming + jnp.dot(attended, w_output, preferred_element_type=jnp.float32)
    inv_two = lax.rsqrt(jnp.mean(middle * middle, axis=-1, keepdims=True) + epsilon)
    normed_two = (middle * inv_two * gain_ffn).astype(jnp.bfloat16)
    gate_pre = jnp.dot(normed_two, w_gate, preferred_element_type=jnp.float32)
    up_pre = jnp.dot(normed_two, w_up, preferred_element_type=jnp.float32)
    sigmoid_g = jax.nn.sigmoid(gate_pre)
    silu_g = gate_pre * sigmoid_g
    hidden = (silu_g * up_pre).astype(jnp.bfloat16)
    ffn_out = jnp.dot(hidden, w_down, preferred_element_type=jnp.float32)
    result = (middle + ffn_out) * valid_rows
    output = result.astype(jnp.bfloat16).reshape(item_count, band_len, model_width)
    grad_res = cotangent.astype(jnp.float32).reshape(row_count, model_width) * valid_rows
    grad_ffn = grad_res.astype(jnp.bfloat16)
    grad_down = contract_rows(hidden, grad_ffn)
    grad_hidden = times_transposed(grad_ffn, w_down)
    grad_gate_pre = (
        grad_hidden * up_pre * (sigmoid_g * (1.0 + gate_pre * (1.0 - sigmoid_g)))
    ).astype(jnp.bfloat16)
    grad_up_pre = (grad_hidden * silu_g).astype(jnp.bfloat16)
    grad_gate = contract_rows(normed_two, grad_gate_pre)
    grad_up = contract_rows(normed_two, grad_up_pre)
    grad_normed_two = times_transposed(grad_gate_pre, w_gate) + times_transposed(grad_up_pre, w_up)
    grad_gain_ffn = jnp.sum(grad_normed_two * middle * inv_two, axis=0)
    scaled_two = grad_normed_two * gain_ffn
    grad_middle = grad_res + inv_two * (
        scaled_two
        - middle * inv_two * inv_two * jnp.mean(scaled_two * middle, axis=-1, keepdims=True)
    )
    grad_branch = grad_middle.astype(jnp.bfloat16)
    grad_output = contract_rows(attended, grad_branch)
    grad_attended = (
        times_transposed(grad_branch, w_output)
        .astype(jnp.bfloat16)
        .reshape(item_count, band_len, head_count, head_dim)
    )
    again = (
        jnp.einsum("iqhd,ikhd->ihqk", query, keys_all, preferred_element_type=jnp.float32)
        * score_scale
    )
    again = jnp.where(allowed[None, None], again, masked_value)
    probable = jnp.exp(again - highest_s) / totals
    grad_probs = jnp.einsum(
        "iqhd,ikhd->ihqk", grad_attended, values_all, preferred_element_type=jnp.float32
    )
    row_delta = jnp.sum(probable * grad_probs, axis=-1, keepdims=True)
    grad_scores = (probable * (grad_probs - row_delta)).astype(jnp.bfloat16)
    grad_query = (
        jnp.einsum("ihqk,ikhd->iqhd", grad_scores, keys_all, preferred_element_type=jnp.float32)
        * score_scale
    )
    grad_values = jnp.einsum(
        "ihqk,iqhd->ikhd",
        probable.astype(jnp.bfloat16),
        grad_attended,
        preferred_element_type=jnp.float32,
    )
    grad_keys = (
        jnp.einsum("ihqk,iqhd->ikhd", grad_scores, query, preferred_element_type=jnp.float32)
        * score_scale
    )
    grad_pair = jnp.concatenate(
        [
            grad_keys.reshape(item_count, seq_len, model_width),
            grad_values.reshape(item_count, seq_len, model_width),
        ],
        axis=-1,
    )
    blocks = grad_pair.reshape(item_count, band_count, band_len, 2 * model_width)
    empty_block = jnp.zeros((item_count, band_len, 2 * model_width), jnp.float32)

    def block_of(index):
        picked = lax.dynamic_index_in_dim(blocks, jnp.maximum(index, 0), 1, keepdims=False)
        return jnp.where(index >= 0, picked, empty_block)

    def cycle_back(turn_index, carried):
        carried = shifted(carried.astype(jnp.bfloat16), "blk", -1).astype(carried.dtype)
        return carried + block_of(band_index - (band_count - 1) + turn_index)

    own_grads = lax.fori_loop(1, band_count, cycle_back, block_of(band_index - (band_count - 1)))
    grad_key_own = own_grads[..., :model_width].reshape(item_count, band_len, head_count, head_dim)
    grad_value_raw = (
        own_grads[..., model_width:].astype(jnp.bfloat16).reshape(row_count, model_width)
    )
    grad_key_raw = (
        rotate(grad_key_own, cosine_table, -sine_table)
        .astype(jnp.bfloat16)
        .reshape(row_count, model_width)
    )
    grad_query_raw = (
        rotate(grad_query, cosine_table, -sine_table)
        .astype(jnp.bfloat16)
        .reshape(row_count, model_width)
    )
    grad_wquery = contract_rows(normed_one, grad_query_raw)
    grad_wkey = contract_rows(normed_one, grad_key_raw)
    grad_wvalue = contract_rows(normed_one, grad_value_raw)
    grad_normed_one = (
        times_transposed(grad_query_raw, w_query)
        + times_transposed(grad_key_raw, w_key)
        + times_transposed(grad_value_raw, w_value)
    )
    grad_gain_attn = jnp.sum(grad_normed_one * incoming * inv_one, axis=0)
    scaled_one = grad_normed_one * gain_attn
    grad_incoming = grad_middle + inv_one * (
        scaled_one
        - incoming * inv_one * inv_one * jnp.mean(scaled_one * incoming, axis=-1, keepdims=True)
    )
    grad_tokens = grad_incoming.astype(jnp.bfloat16).reshape(item_count, band_len, model_width)
    summed = (
        lax.psum_scatter(
            grad_wquery.astype(jnp.bfloat16), "blk", scatter_dimension=0, tiled=True
        ).astype(jnp.float32),
        lax.psum_scatter(
            grad_wkey.astype(jnp.bfloat16), "blk", scatter_dimension=0, tiled=True
        ).astype(jnp.float32),
        lax.psum_scatter(
            grad_wvalue.astype(jnp.bfloat16), "blk", scatter_dimension=0, tiled=True
        ).astype(jnp.float32),
        lax.psum_scatter(
            grad_output.astype(jnp.bfloat16), "blk", scatter_dimension=0, tiled=True
        ).astype(jnp.float32),
        lax.psum_scatter(
            grad_gate.astype(jnp.bfloat16), "blk", scatter_dimension=0, tiled=True
        ).astype(jnp.float32),
        lax.psum_scatter(
            grad_up.astype(jnp.bfloat16), "blk", scatter_dimension=0, tiled=True
        ).astype(jnp.float32),
        lax.psum_scatter(
            grad_down.astype(jnp.bfloat16), "blk", scatter_dimension=0, tiled=True
        ).astype(jnp.float32),
        lax.psum_scatter(
            grad_gain_attn.astype(jnp.bfloat16), "blk", scatter_dimension=0, tiled=True
        ).astype(jnp.float32),
        lax.psum_scatter(
            grad_gain_ffn.astype(jnp.bfloat16), "blk", scatter_dimension=0, tiled=True
        ).astype(jnp.float32),
    )
    summed = (
        lax.psum(summed[0].astype(jnp.bfloat16), "dp").astype(jnp.float32),
        lax.psum(summed[1].astype(jnp.bfloat16), "dp").astype(jnp.float32),
        lax.psum(summed[2].astype(jnp.bfloat16), "dp").astype(jnp.float32),
        lax.psum(summed[3].astype(jnp.bfloat16), "dp").astype(jnp.float32),
        lax.psum(summed[4].astype(jnp.bfloat16), "dp").astype(jnp.float32),
        lax.psum(summed[5].astype(jnp.bfloat16), "dp").astype(jnp.float32),
        lax.psum(summed[6].astype(jnp.bfloat16), "dp").astype(jnp.float32),
        lax.psum(summed[7].astype(jnp.bfloat16), "dp").astype(jnp.float32),
        lax.psum(summed[8].astype(jnp.bfloat16), "dp").astype(jnp.float32),
    )
    return (
        output,
        grad_tokens,
        summed[0],
        summed[1],
        summed[2],
        summed[3],
        summed[4],
        summed[5],
        summed[6],
        summed[7],
        summed[8],
    )


MESH = pl.DeviceIdType.MESH
ITEM, BAND = "dp", "blk"
CORES = 2
CHIPS = 4
BLOCK = 256
PAIR = 128
LOW = jnp.bfloat16
F32 = jnp.float32


def place():
    dp = lax.axis_index(ITEM)
    return dp, lax.axis_index(BAND), lax.rem(dp, CORES)


def near(dp, blk, core=0, chip=0, line=0):
    flip = core + CORES * line
    return {ITEM: dp ^ flip if flip else dp, BAND: blk ^ chip if chip else blk}


def greet(dp, blk, flips):
    barrier = pltpu.get_barrier_semaphore()
    for flip in flips:
        pl.semaphore_signal(barrier, inc=1, device_id=near(dp, blk, *flip), device_id_type=MESH)
    return barrier


def remote(src, dst, send, recv, where):
    return pltpu.make_async_remote_copy(
        src_ref=src, dst_ref=dst, send_sem=send, recv_sem=recv, device_id=where, device_id_type=MESH
    )


def part(start, size):
    return pl.ds(pl.multiple_of(start, size), size)


PLANE = [(core, chip, 0) for chip in range(CHIPS) for core in range(CORES) if core or chip]
REACH = PLANE + [(0, 0, 1), (0, 0, 3)]


def plus(one, other, kind=LOW):
    return (one.astype(F32) + other.astype(F32)).astype(kind)


class Gather:
    SEMS = [(2,), (4, 2), (4,), (4,), (4,)]

    def __init__(self, band, buf, sems):
        self.band, self.buf = band, buf
        self.own, self.send, self.recv, self.fsend, self.frecv = sems
        self.dp, self.blk, self.core = place()
        self.rows = band.shape[1]
        self.half = self.rows // 2
        self.mine = (self.blk // 2) == self.core

    def out(self, r, h):
        target = self.blk ^ r
        return remote(
            self.band.at[lax.rem(target, 2), pl.ds(h * self.half, self.half)],
            self.buf.at[part(self.blk * self.rows + h * self.half, self.half)],
            self.send.at[r, h],
            self.recv.at[r],
            {ITEM: self.dp - self.core + h, BAND: target},
        )

    def across(self, r):
        rows = self.buf.at[part((self.blk ^ r) * self.rows + self.core * self.half, self.half)]
        return remote(rows, rows, self.fsend.at[r], self.frecv.at[r], near(self.dp, self.blk, 1))

    def here(self):
        rows = self.buf.at[part(self.blk * self.rows, self.rows)]
        return pltpu.make_async_copy(self.band.at[lax.rem(self.blk, 2)], rows, self.own.at[0])

    def there(self):
        rows = self.buf.at[part(self.blk * self.rows, self.rows)]
        src = self.band.at[lax.rem(self.blk, 2)]
        return remote(src, rows, self.fsend.at[0], self.frecv.at[0], near(self.dp, self.blk, 1))

    def sends(self, r):
        return ((self.blk ^ r) // 2) == self.core

    def start(self):
        for r in (1, 2, 3):

            @pl.when(self.sends(r))
            def _():
                for h in range(2):
                    self.out(r, h).start()

        @pl.when(self.mine)
        def _():
            self.here().start()
            self.there().start()

    def forward(self, r):
        self.out(r, 0).wait_recv()
        self.across(r).start()

    def ready(self, r):
        if r:
            self.across(r).wait_recv()
            return

        @pl.when(self.mine)
        def _():
            self.here().wait()

        @pl.when(jnp.logical_not(self.mine))
        def _():
            self.there().wait_recv()

    def drain(self):
        @pl.when(self.mine)
        def _():
            self.there().wait_send()

        for r in (1, 2, 3):
            self.across(r).wait_send()

            @pl.when(self.sends(r))
            def _():
                for h in range(2):
                    self.out(r, h).wait_send()


class Return:
    SEMS = [(1,), (4,), (2, 2)]

    def __init__(self, src, band, sems):
        self.src, self.band = src, band
        self.own, self.send, self.recv = sems
        self.dp, self.blk, self.core = place()
        self.half = src.shape[1]
        self.home = self.blk // 2

    def slot(self):
        return self.band.at[lax.rem(self.blk, 2), part(self.core * self.half, self.half)]

    def out(self, r):
        chip = self.blk ^ r
        return remote(
            self.src.at[chip],
            self.slot(),
            self.send.at[r],
            self.recv.at[lax.rem(self.blk, 2), self.core],
            {ITEM: self.dp - self.core + self.home, BAND: chip},
        )

    def keep(self):
        return pltpu.make_async_copy(self.src.at[self.blk], self.slot(), self.own.at[0])

    def start(self):
        for r in (3, 1, 2):
            self.out(r).start()

        @pl.when(self.home == self.core)
        def _():
            self.keep().start()

        @pl.when(self.home != self.core)
        def _():
            self.out(0).start()

    def drain(self):
        @pl.when(self.home == self.core)
        def _():
            self.keep().wait()

        @pl.when(self.home != self.core)
        def _():
            self.out(0).wait_send()

        for r in (1, 2, 3):
            self.out(r).wait_send()

    def arrived(self):
        for i in range(2):
            for h in range(2):
                local = (self.core * 2 + i == self.blk) & (self.core == h)

                @pl.when(jnp.logical_not(local))
                def _():
                    remote(
                        self.src.at[0],
                        self.band.at[i, pl.ds(h * self.half, self.half)],
                        self.send.at[0],
                        self.recv.at[i, h],
                        near(self.dp, self.blk, 1),
                    ).wait_recv()


class Line:
    def locate(self):
        self.dp, self.blk, self.core = place()
        z = self.dp // CORES
        self.outer = (z == 0) | (z == 3)
        self.inner = jnp.logical_not(self.outer)

    def stage(self, n):
        (self.stage0, self.stage1, self.stage2, self.stage3, self.stage4, self.stage5, self.stage6)[n]()


class Chunk(Line):
    SEMS = [(2, 2, 2), (2, 2), (3, 2, 2), (2, 3)]

    def __init__(self, src, buffers, result, sems, turned=False):
        self.src, self.result, self.turned = src, result, turned
        self.first, self.second, self.line = buffers
        self.s1, self.s2, self.sz, self.sc = sems
        self.locate()

    @staticmethod
    def shapes(rows, cols, turned):
        half = (rows // 2, cols // CHIPS) if turned else (rows // CHIPS // 2, cols)
        return [(2, 2) + half, (2,) + half, (2, 2) + half], (CORES, 2) + half

    def piece(self, chip, h):
        rows, cols = self.first.shape[2:]
        if self.turned:
            return self.src.at[pl.ds(h * rows, rows), part(chip * cols, cols)]
        return self.src.at[part(chip * 2 * rows + h * rows, rows)]

    def ways(self, h):
        return (1, 2) if h == 0 else (2, 1)

    def step1(self, h, n):
        near_way, far_way = self.ways(h)
        chip = self.blk ^ near_way ^ (far_way if n else 0)
        return remote(
            self.piece(chip, h), self.first.at[h, n], self.s1.at[0, h, n], self.s1.at[1, h, n],
            near(self.dp, self.blk, 0, near_way),
        )

    def step2(self, h):
        return remote(
            self.first.at[h, 1], self.second.at[h], self.s2.at[0, h], self.s2.at[1, h],
            near(self.dp, self.blk, 0, self.ways(h)[1]),
        )

    def hop(self, n, h):
        src = (self.second.at[h], self.line.at[0, h], self.second.at[h])[n]
        dst = self.line.at[1 if n == 1 else 0, h]
        return remote(
            src, dst, self.sz.at[n, h, 0], self.sz.at[n, h, 1],
            near(self.dp, self.blk, 0, 0, 3 if n == 1 else 1),
        )

    def share(self, total, h):
        slot = self.result.at[self.core, h]
        return (
            remote(total, slot, self.sc.at[h, 0], self.sc.at[h, 1], near(self.dp, self.blk, 1)),
            pltpu.make_async_copy(total, slot, self.sc.at[h, 2]),
        )

    def xy_start(self):
        for n in (1, 0):
            for h in range(2):
                self.step1(h, n).start()

    def xy_turn(self):
        for h in range(2):
            self.step1(h, 1).wait_recv()
            chip = self.blk ^ self.ways(h)[1]
            self.first[h, 1] = plus(self.first[h, 1], self.piece(chip, h)[...])
            self.step2(h).start()

    def xy_end(self, h):
        self.step1(h, 0).wait_recv()
        self.step2(h).wait_recv()
        own = plus(self.first[h, 0], self.piece(self.blk, h)[...], F32)
        self.second[h] = plus(own, self.second[h])

    def xy_drain(self):
        for h in range(2):
            for n in range(2):
                self.step1(h, n).wait_send()
            self.step2(h).wait_send()

    def stage0(self):
        self.xy_start()

    def stage1(self):
        self.xy_turn()

    def stage2(self):
        for h in range(2):
            self.xy_end(h)

            @pl.when(self.outer)
            def _():
                self.hop(0, h).start()

    def stage3(self):
        @pl.when(self.inner)
        def _():
            for h in range(2):
                self.hop(0, h).wait_recv()
                self.line[0, h] = plus(self.line[0, h], self.second[h])
                self.hop(1, h).start()

    def stage4(self):
        @pl.when(self.inner)
        def _():
            for h in range(2):
                self.hop(1, h).wait_recv()
                self.second[h] = plus(self.line[0, h], self.line[1, h])
                self.hop(2, h).start()
                for copy in self.share(self.second.at[h], h):
                    copy.start()

    def stage5(self):
        @pl.when(self.outer)
        def _():
            for h in range(2):
                self.hop(2, h).wait_recv()
                for copy in self.share(self.line.at[0, h], h):
                    copy.start()

    def stage6(self):
        for h in range(2):
            for copy in self.share(self.second.at[h], h):
                copy.wait()
        self.xy_drain()

        @pl.when(self.outer)
        def _():
            for h in range(2):
                self.hop(0, h).wait_send()

        @pl.when(self.inner)
        def _():
            for h in range(2):
                self.hop(1, h).wait_send()
                self.hop(2, h).wait_send()


class PairChunk(Chunk):
    SEMS = [(CHIPS, 2), (2, 2, 2), (2, 2), (2, 2), (3,)]

    def __init__(self, src, buffers, result, sems, turned=False):
        self.src, self.result, self.turned = src, result, turned
        self.pair, self.first, self.second, self.line, self.total = buffers
        self.sp, self.s1, self.s2, self.sz, self.sc = sems
        self.locate()
        self.kept = lax.rem((self.dp // CORES + 1) // 2, 2)

    @staticmethod
    def shapes(rows, cols, turned):
        whole = (rows // 2, cols // CHIPS) if turned else (rows // CHIPS // 2, cols)
        half = (whole[0] // 2, whole[1])
        return [(CHIPS,) + whole, (2, 2) + half, (2,) + half, (2,) + half, (2, 2) + half], (CORES, 2, 2) + half

    def share_of(self, chip, s):
        rows, cols = self.pair.shape[1:]
        if self.turned:
            return self.src.at[part(s * rows, rows), pl.ds(chip * cols, cols)]
        return self.src.at[part(chip * 2 * rows + s * rows, rows)]

    def piece(self, chip, h):
        rows = self.pair.shape[1] // 2
        return self.pair.at[chip, pl.ds(h * rows, rows)]

    def swap(self, chip):
        return remote(
            self.share_of(chip, 1 - self.kept), self.pair.at[chip], self.sp.at[chip, 0], self.sp.at[chip, 1],
            near(self.dp, self.blk, 0, 0, 1),
        )

    def middle(self):
        return remote(
            self.second, self.line, self.sz.at[0, 0], self.sz.at[0, 1], near(self.dp, self.blk, 0, 0, 3)
        )

    def hand(self):
        half = self.total.at[self.kept]
        return remote(half, half, self.sz.at[1, 0], self.sz.at[1, 1], near(self.dp, self.blk, 0, 0, 1))

    def spread(self):
        slot = self.result.at[self.core]
        return (
            remote(self.total, slot, self.sc.at[0], self.sc.at[1], near(self.dp, self.blk, 1)),
            pltpu.make_async_copy(self.total, slot, self.sc.at[2]),
        )

    def stage0(self):
        for chip in range(CHIPS):
            self.swap(chip).start()

    def stage1(self):
        for chip in range(CHIPS):
            self.swap(chip).wait_recv()
            self.pair[chip] = plus(self.pair[chip], self.share_of(chip, self.kept)[...])
        self.xy_start()

    def stage2(self):
        self.xy_turn()

    def stage3(self):
        for h in range(2):
            self.xy_end(h)
        self.middle().start()

    def stage4(self):
        self.middle().wait_recv()
        for h in range(2):
            self.total[self.kept, h] = plus(self.second[h], self.line[h])
        self.hand().start()

    def stage5(self):
        self.hand().wait_recv()
        for copy in self.spread():
            copy.start()

    def stage6(self):
        for copy in self.spread():
            copy.wait()
        for chip in range(CHIPS):
            self.swap(chip).wait_send()
        self.xy_drain()
        self.middle().wait_send()
        self.hand().wait_send()


class Small(Line):
    SEMS = [(6, 2)]
    SLOTS = 11

    def __init__(self, hold, result, sems):
        self.hold, self.result = hold, result
        (self.sem,) = sems
        self.locate()

    def go(self, n):
        flips = ((1, 0, 0), (0, 1, 0), (0, 2, 0), (0, 0, 1), (0, 0, 3), (0, 0, 1))
        src, dst = (10, 10) if n == 5 else (2 * n, 2 * n + 1)
        return remote(
            self.hold.at[src], self.hold.at[dst], self.sem.at[n, 0], self.sem.at[n, 1],
            near(self.dp, self.blk, *flips[n]),
        )

    def add(self, n, to):
        self.go(n).wait_recv()
        self.hold[to] = self.hold[2 * n] + self.hold[2 * n + 1]

    def stage0(self):
        self.go(0).start()

    def stage1(self):
        for n in range(2):
            self.add(n, 2 * n + 2)
            self.go(n + 1).start()

    def stage2(self):
        self.add(2, 6)

        @pl.when(self.outer)
        def _():
            self.go(3).start()

    def stage3(self):
        @pl.when(self.inner)
        def _():
            self.add(3, 8)
            self.go(4).start()

    def stage4(self):
        @pl.when(self.inner)
        def _():
            self.add(4, 10)
            self.go(5).start()

    def stage5(self):
        @pl.when(self.outer)
        def _():
            self.go(5).wait_recv()

        self.result[...] = self.hold[10]

    def stage6(self):
        for n in range(3):
            self.go(n).wait_send()

        @pl.when(self.outer)
        def _():
            self.go(3).wait_send()

        @pl.when(self.inner)
        def _():
            self.go(4).wait_send()
            self.go(5).wait_send()


def dot(left, right):
    return jnp.dot(left, right, preferred_element_type=F32)


def dot_rows(left, right):
    return lax.dot_general(left, right, (((0,), (0,)), ((), ())), preferred_element_type=F32)


def dot_cols(left, right):
    return lax.dot_general(left, right, (((1,), (1,)), ((), ())), preferred_element_type=F32)


def inverse_rms(values):
    return lax.rsqrt(jnp.mean(values * values, axis=-1, keepdims=True) + epsilon)


def turn(t, cosine, sine, sign):
    quarter = PAIR // 4
    lane = lax.broadcasted_iota(jnp.int32, t.shape, 1)
    other = jnp.where(
        lane % (2 * quarter) < quarter,
        pltpu.roll(t, PAIR - quarter, 1),
        pltpu.roll(t, quarter, 1),
    )
    return t * cosine + (sign * sine) * other


def both_heads(t):
    lane = lax.broadcasted_iota(jnp.int32, t.shape, 1)
    zero = jnp.zeros_like(t)
    return jnp.concatenate(
        [jnp.where(lane < PAIR // 2, t, zero), jnp.where(lane < PAIR // 2, zero, t)], axis=0
    )


def one_pair(t):
    rows = t.shape[0] // 2
    lane = lax.broadcasted_iota(jnp.int32, (rows, PAIR), 1)
    return jnp.where(lane < PAIR // 2, t[:rows], t[rows:])


FF0, FF1, FF2, FF3, DOWN, OUT, QUERY, KEY, VALUE, SMALL = range(10)
TILES = (FF0, FF1, FF2, FF3)
PAIRED = (FF2, OUT)
(
    TILE0, TILE1, TILE2, TILE3, GRAD_DOWN, PART_OUT, GRAD_N2, OWN_OUT, GRAD_MID, GRAD_OUT, GRAD_ATT,
    HEADS0, HEADS1, HEADS2, GRAD_QKV, PART_N1, OWN_N1, SEND_OUT, SEND_X,
) = range(100, 119)
ORDER = (
    TILE0, FF0, TILE1, FF1, TILE2, FF0, FF2, TILE3, FF3, PART_OUT, GRAD_N2, FF1, FF0, GRAD_DOWN, FF2, OWN_OUT, FF3,
    GRAD_MID, FF1, FF2, DOWN, GRAD_OUT, FF0, OUT, GRAD_ATT, HEADS0, HEADS1, FF1, FF3, FF0, DOWN, HEADS2, OUT, FF2,
    GRAD_QKV, VALUE, FF1, FF3, DOWN, PART_N1, OUT, VALUE, KEY, FF1, OUT, FF2, QUERY, OWN_N1, SMALL, VALUE, FF3,
    DOWN, SMALL, QUERY, OUT, KEY, FF3, SEND_X, DOWN, SEND_OUT, QUERY, VALUE, QUERY, VALUE, SMALL, KEY, VALUE, KEY,
    DOWN, SMALL, FF0, QUERY, OUT, KEY, QUERY, SMALL, FF2, KEY, SMALL,
)


def layout(width, ff):
    seq = CHIPS * BLOCK
    half = width // 2
    pairs = half // PAIR

    def low(*shape):
        return pltpu.VMEM(shape, LOW)

    def wide(*shape):
        return pltpu.VMEM(shape, F32)

    grads, sums = [], []
    keep = dict(
        w_qkv=low(width, 3 * half), w_out=low(width, width), w_ff=low(width, 2 * ff),
        w_down=low(ff, width), turns=wide(2, seq, PAIR),
        x=low(seq, width), g_ffn=low(seq, width), n1=low(seq, width),
        q=low(seq, half), k=low(seq, half), v=low(seq, half),
        prob=[low(pairs, 2 * BLOCK, (i + 1) * BLOCK) for i in range(CHIPS)],
        att=low(seq, width), middle=wide(seq, width), n2=low(seq, width), n2_turned=low(width, seq),
        hidden=low(seq, ff), g_ff=low(seq, 2 * ff), share=wide(seq, PAIR), gn2=low(seq, width),
        swap_out=low(CHIPS, BLOCK // 2, width), swap_in=low(2, CHIPS, BLOCK // 2, width),
        band=low(CHIPS, BLOCK // 2, width),
        dk=wide(seq, PAIR), dv=wide(seq, PAIR), hold=wide(Small.SLOTS, 8, width),
        grad=grads, sums=sums,
    )
    sems = dict(
        load=[(18,)], gather_x=Gather.SEMS, gather_g=Gather.SEMS, att=[(2, pairs)], swap=[(2, 2)], gn2=[(2, CHIPS)],
        back_out=Return.SEMS, back_x=Return.SEMS, small=Small.SEMS,
        sums=[PairChunk.SEMS if name in PAIRED else Chunk.SEMS for name in range(SMALL)],
    )
    sems = jax.tree.map(pltpu.SemaphoreType.DMA, sems, is_leaf=lambda t: isinstance(t, tuple))
    results = []
    for name in range(SMALL):
        cols = ff if name == DOWN else 2 * (ff // CHIPS) if name in TILES else half
        kind = PairChunk if name in PAIRED else Chunk
        shapes, result = kind.shapes(width, cols, name == DOWN)
        results.append(result)
        grads.append(low(width, cols))
        sums.append([low(*shape) for shape in shapes])
    return keep, sems, results


def layer_kernel(
    scratch, tokens, cotangent, lengths, turns, gain_attn, gain_ffn,
    w_query, w_key, w_value, w_output, w_gate, w_up, w_down, *refs,
):
    width, ff = tokens.shape[2], w_gate.shape[1] // CORES
    results, (small_result, out_band, x_band) = refs[:SMALL], refs[SMALL : SMALL + 3]
    keep, sems = jax.tree.unflatten(scratch, refs[SMALL + 3 :])
    m, sem = SimpleNamespace(**keep), SimpleNamespace(**sems)
    dp, blk, core = place()
    partner = near(dp, blk, 1)
    half = width // 2
    pairs = half // PAIR
    scale = (width // HEADS) ** (-0.5)
    mine = pl.multiple_of(core * half, half)

    def block(r):
        return part(r * BLOCK, BLOCK)

    def half_block(chip, c):
        return part(chip * BLOCK + c * (BLOCK // 2), BLOCK // 2)

    def lanes(p):
        return part(p * PAIR, PAIR)

    barrier = greet(dp, blk, REACH)

    loads = []

    def load(src, dst):
        copy = pltpu.make_async_copy(src, dst, sem.load[0].at[len(loads)])
        copy.start()
        loads.append(copy)

    stage = m.band.reshape(2, BLOCK, width)
    load(cotangent, stage)
    load(turns, m.turns)
    for n, weight in enumerate((w_query, w_key, w_value)):
        load(weight.at[:, pl.ds(mine, half)], m.w_qkv.at[:, pl.ds(n * half, half)])

    gather_x = Gather(tokens, m.x, sem.gather_x)
    gather_g = Gather(stage, m.g_ffn, sem.gather_g)
    pl.semaphore_wait(barrier, len(REACH))
    gather_x.start()
    load(w_output, m.w_out)
    unit = ff // CHIPS
    for chip in range(CHIPS):
        there = part(chip * CORES * unit + core * unit, unit)
        load(w_up.at[:, there], m.w_ff.at[:, pl.ds(2 * chip * unit, unit)])
        load(w_gate.at[:, there], m.w_ff.at[:, pl.ds((2 * chip + 1) * unit, unit)])
        load(w_down.at[there], m.w_down.at[pl.ds(chip * unit, unit)])
    for copy in loads[:5]:
        copy.wait()
    for i in range(2):
        row = blk * BLOCK + lax.broadcasted_iota(jnp.int32, (BLOCK, width), 0)
        stage[i] = jnp.where(row < lengths[i], stage[i].astype(F32), 0.0).astype(LOW)

    def project(r):
        rows = block(blk ^ r)
        x = m.x[rows].astype(F32)
        n1 = (x * inverse_rms(x) * gain_attn[...][None]).astype(LOW)
        m.n1[rows] = n1
        cosine, sine = m.turns[0, rows], m.turns[1, rows]
        for n, store in enumerate((m.q, m.k, m.v)):
            full = dot(n1, m.w_qkv[:, n * half : (n + 1) * half])
            for p in range(pairs):
                t = full[:, p * PAIR : (p + 1) * PAIR]
                if n < 2:
                    t = turn(t, cosine, sine, 1.0)
                if n == 0:
                    t = t.astype(LOW).astype(F32) * scale
                store[rows, p * PAIR : (p + 1) * PAIR] = t.astype(LOW)

    gather_x.ready(0)
    project(0)
    gather_x.forward(1)
    gather_x.forward(2)
    gather_x.ready(1)
    project(1)
    gather_x.forward(3)
    gather_x.ready(2)
    project(2)
    gather_x.ready(3)
    gather_g.start()
    project(3)

    row = lax.broadcasted_iota(jnp.int32, (2 * BLOCK, BLOCK), 0) % BLOCK
    seen = lax.broadcasted_iota(jnp.int32, (2 * BLOCK, BLOCK), 1) <= row

    lane = lax.broadcasted_iota(jnp.int32, (BLOCK, PAIR), 1)

    def att_cols(p):
        return part(core * half + p * PAIR, PAIR)

    def att_copy(p):
        cols = m.att.at[:, att_cols(p)]
        return remote(cols, cols, sem.att[0].at[0, p], sem.att[0].at[1, p], partner)

    @pl.loop(0, pairs)
    def _(p):
        for i in range(CHIPS):
            size = BLOCK * i
            q = both_heads(m.q[pl.ds(size, BLOCK), lanes(p)])
            score = dot_cols(q, m.k[pl.ds(0, size + BLOCK), lanes(p)])
            own = jnp.where(seen, score[:, size:], masked_value)
            score = jnp.concatenate([score[:, :size], own], axis=1) if i else own
            slabs = [score[:, n : n + PAIR] for n in range(0, size + BLOCK, PAIR)]
            top = jnp.max(functools.reduce(jnp.maximum, slabs), axis=-1, keepdims=True)
            prob = jnp.exp(score - top).astype(LOW)
            m.prob[i][p] = prob
            v = m.v[pl.ds(0, size + BLOCK), lanes(p)]
            both = dot(prob, jnp.concatenate([v, jnp.ones_like(v)], axis=1))
            att, share = both[:, :PAIR], 1.0 / both[:, PAIR:]
            kept = m.share[pl.ds(size, BLOCK)]
            kept = jnp.where(lane == 2 * p, share[:BLOCK], kept)
            m.share[pl.ds(size, BLOCK)] = jnp.where(lane == 2 * p + 1, share[BLOCK:], kept)
            m.att[pl.ds(size, BLOCK), att_cols(p)] = one_pair(att * share).astype(LOW)
        att_copy(p).start()

    for r in (1, 2, 3):
        gather_g.forward(r)
    loads[5].wait()
    for p in range(pairs):
        att_copy(p).wait_recv()

    @pl.loop(0, CHIPS, unroll=True)
    def _(r):
        rows = block(r)
        middle = m.x[rows].astype(F32) + dot(m.att[rows], m.w_out[...])
        m.middle[rows] = middle
        n2 = (middle * inverse_rms(middle) * gain_ffn[...][None]).astype(LOW)
        m.n2[rows] = n2
        m.n2_turned[:, rows] = n2.T

    for r in range(CHIPS):
        gather_g.ready(r)
    for copy in loads[6:]:
        copy.wait()

    sums = []
    for name in range(SMALL):
        own = (m.grad[name], m.sums[name], results[name], sem.sums[name])
        sums.append((PairChunk if name in PAIRED else Chunk)(*own, name == DOWN))
    sums.append(Small(m.hold, small_result, sem.small))
    done = [0] * len(sums)

    def advance(*names):
        for name in names:
            sums[name].stage(done[name])
            done[name] += 1

    def tile(t):
        units, both = block(t), part(t * 2 * BLOCK, 2 * BLOCK)

        @pl.loop(0, CHIPS, unroll=True)
        def _(r):
            rows = block(r)
            pre = dot(m.n2[rows], m.w_ff[:, both])
            up, gate = pre[:, :BLOCK], pre[:, BLOCK:]
            g_hidden = dot_cols(m.g_ffn[rows], m.w_down[units])
            sig = 0.5 * jnp.tanh(0.5 * gate) + 0.5
            silu = gate * sig
            m.hidden[rows, units] = (silu * up).astype(LOW)
            m.g_ff[rows, part(t * 2 * BLOCK, BLOCK)] = (g_hidden * silu).astype(LOW)
            g_gate = g_hidden * up * (sig * (1.0 + gate * (1.0 - sig)))
            m.g_ff[rows, part(t * 2 * BLOCK + BLOCK, BLOCK)] = g_gate.astype(LOW)

        for name in TILES:

            @pl.when(t == name)
            def _():
                for r in range(width // BLOCK):
                    rows = pl.ds(r * BLOCK, BLOCK)
                    m.grad[name][rows] = dot(m.n2_turned[rows], m.g_ff[:, both]).astype(LOW)

    def grad_down():
        @pl.loop(0, width // BLOCK, unroll=True)
        def _(t):
            rows = block(t)
            m.grad[DOWN][rows] = dot_rows(m.g_ffn[:, rows], m.hidden[...]).astype(LOW)

    def swap(n):
        return remote(m.swap_out, m.swap_in.at[n], sem.swap[0].at[n, 0], sem.swap[0].at[n, 1], partner)

    def part_out():
        @pl.loop(0, CHIPS, unroll=True)
        def _(chip):
            m.swap_out[chip] = dot(m.hidden[half_block(chip, 1 - core)], m.w_down[...]).astype(LOW)

        swap(0).start()

    back_out = Return(m.band, out_band, sem.back_out)
    back_x = Return(m.swap_out, x_band, sem.back_x)

    def own_out():
        swap(0).wait()
        gather_g.drain()

        @pl.loop(0, CHIPS, unroll=True)
        def _(chip):
            rows = half_block(chip, core)
            out = dot(m.hidden[rows], m.w_down[...]) + m.swap_in[0, chip].astype(F32)
            m.band[chip] = (m.middle[rows] + out).astype(LOW)

    def gn2_copy(r):
        return remote(
            m.n2.at[block(r)], m.gn2.at[block(r)], sem.gn2[0].at[0, r], sem.gn2[0].at[1, r], partner,
        )

    def grad_n2():
        @pl.loop(0, CHIPS, unroll=True)
        def _(r):
            m.n2[block(r)] = dot_cols(m.g_ff[block(r)], m.w_ff[...]).astype(LOW)
            gn2_copy(r).start()

    g_branch, g_mid = m.gn2, m.middle

    def grad_mid():
        m.hold[0] = jnp.zeros((8, width), F32)

        @pl.loop(0, CHIPS, unroll=True)
        def _(r):
            rows = block(r)
            gn2_copy(r).wait_recv()
            g_n2 = plus(m.n2[rows], m.gn2[rows], F32)
            middle = m.middle[rows]
            inv = inverse_rms(middle)
            m.hold[0, 1:2] += 0.5 * jnp.sum(g_n2 * middle * inv, axis=0, keepdims=True)
            a2 = g_n2 * gain_ffn[...][None]
            inner = jnp.mean(a2 * middle, axis=-1, keepdims=True)
            got = m.g_ffn[rows].astype(F32) + inv * (a2 - middle * (inv * inv * inner))
            g_branch[rows] = got.astype(LOW)
            g_mid[rows] = got

    def grad_out():
        @pl.loop(0, width // BLOCK, unroll=True)
        def _(t):
            rows = block(t)
            m.grad[OUT][rows] = dot_rows(m.att[:, rows], g_branch[:, pl.ds(mine, half)]).astype(LOW)

    g_att = m.hidden
    g_qkv = m.g_ff.at[:, pl.ds(0, 3 * half)]
    g_q, g_k, g_v = (m.g_ff.at[:, pl.ds(n * half, half)] for n in range(3))

    def grad_att():
        @pl.loop(0, CHIPS, unroll=True)
        def _(r):
            g_att[block(r), pl.ds(0, half)] = dot_cols(g_branch[block(r)], m.w_out[pl.ds(mine, half)]).astype(LOW)

    def heads(p):
        for i in range(CHIPS - 1, -1, -1):
            rows, size = pl.ds(BLOCK * i, BLOCK), BLOCK * (i + 1)
            past = pl.ds(0, size)
            kept = m.share[rows]
            share = jnp.concatenate(
                [
                    jnp.sum(jnp.where(lane == 2 * p + n, kept, 0.0), axis=-1, keepdims=True)
                    for n in range(2)
                ],
                axis=0,
            )
            g = both_heads(g_att[rows, lanes(p)]).astype(F32) * share
            q = both_heads(m.q[rows, lanes(p)])
            out = m.att[rows, att_cols(p)].astype(F32)
            delta = jnp.sum(g * jnp.concatenate([out, out], axis=0), axis=-1, keepdims=True)
            g = g.astype(LOW)
            prob = m.prob[i][p]
            g_prob = dot_cols(g, m.v[past, lanes(p)])
            g_score = (prob.astype(F32) * (g_prob - delta)).astype(LOW)
            got_q = one_pair(dot(g_score, m.k[past, lanes(p)])) * scale
            g_q[rows, lanes(p)] = turn(got_q, m.turns[0, rows], m.turns[1, rows], -1.0).astype(LOW)
            got_k, got_v = dot_rows(g_score, q), dot_rows(prob, g)
            if i == CHIPS - 1:
                m.dk[...] = got_k
                m.dv[...] = got_v
            else:
                m.dk[past] += got_k
                m.dv[past] += got_v
        for r in range(CHIPS):
            rows = pl.ds(BLOCK * r, BLOCK)
            g_k[rows, lanes(p)] = turn(m.dk[rows], m.turns[0, rows], m.turns[1, rows], -1.0).astype(LOW)
            g_v[rows, lanes(p)] = m.dv[rows].astype(LOW)

    def grad_qkv():
        @pl.loop(0, width // BLOCK, unroll=True)
        def _(t):
            rows = block(t)
            got = dot_rows(m.n1[:, rows], g_qkv[...]).astype(LOW)
            for n, name in enumerate((QUERY, KEY, VALUE)):
                m.grad[name][rows] = got[:, n * half : (n + 1) * half]

    def part_n1():
        @pl.loop(0, CHIPS, unroll=True)
        def _(chip):
            m.swap_out[chip] = dot_cols(g_qkv[half_block(chip, 1 - core)], m.w_qkv[...]).astype(LOW)

        swap(1).start()

    def own_n1():
        swap(1).wait()

        @pl.loop(0, CHIPS, unroll=True)
        def _(chip):
            rows = half_block(chip, core)
            got = dot_cols(g_qkv[rows], m.w_qkv[...]) + m.swap_in[1, chip].astype(F32)
            x = m.x[rows].astype(F32)
            inv = inverse_rms(x)
            m.hold[0, 0:1] += jnp.sum(got * x * inv, axis=0, keepdims=True)
            a1 = got * gain_attn[...][None]
            inner = jnp.mean(a1 * x, axis=-1, keepdims=True)
            m.swap_out[chip] = (g_mid[rows] + inv * (a1 - x * (inv * inv * inner))).astype(LOW)

    steps = {
        GRAD_DOWN: grad_down, PART_OUT: part_out, GRAD_N2: grad_n2, OWN_OUT: own_out, GRAD_MID: grad_mid,
        GRAD_OUT: grad_out, GRAD_ATT: grad_att, GRAD_QKV: grad_qkv, PART_N1: part_n1, OWN_N1: own_n1,
        SEND_OUT: back_out.start, SEND_X: back_x.start,
    }

    def do(name):
        if name <= SMALL:
            advance(name)
        else:
            steps[name]()

    def looped(body, first, last):
        gaps = [[]]
        for name in ORDER[ORDER.index(first) + 1 : ORDER.index(last)]:
            if first < name < last:
                gaps.append([])
            else:
                gaps[-1].append(name)

        @pl.loop(0, last - first + 1)
        def _(n):
            body(n)
            for at, gap in enumerate(gaps):
                if gap:

                    @pl.when(n == at)
                    def _():
                        for name in gap:
                            do(name)

    at = 0
    while at < len(ORDER):
        name = ORDER[at]
        if name == TILE0:
            looped(tile, TILE0, TILE3)
            at = ORDER.index(TILE3)
        elif name == HEADS0:
            looped(heads, HEADS0, HEADS2)
            at = ORDER.index(HEADS2)
        else:
            do(name)
        at += 1

    for total in sums:
        total.stage6()
    for p in range(pairs):
        att_copy(p).wait_send()
    for r in range(CHIPS):
        gn2_copy(r).wait_send()
    gather_x.drain()
    back_out.drain()
    back_x.drain()
    back_out.arrived()
    back_x.arrived()


def vmem_specs(count):
    return [pl.BlockSpec(memory_space=pltpu.VMEM)] * count


def any_specs(count):
    return [pl.BlockSpec(memory_space=pl.ANY)] * count


def finish_kernel(lengths, *refs):
    step = pl.program_id(0)
    blk = lax.axis_index(BAND)
    tiles, refs = refs[:CHIPS], refs[CHIPS:]
    down, output, query, key, value, out, back, small = refs[:8]
    r_out, r_back, r_query, r_key, r_value, r_output, r_gate, r_up, r_down, r_gains = refs[8:]
    for src, dst in ((query, r_query), (key, r_key), (value, r_value), (output, r_output)):
        cols = src.shape[-1]
        for c in range(CORES):
            dst[:, c * cols : (c + 1) * cols] = src[c].astype(F32)
    for t, src in enumerate(tiles):
        for c in range(CORES):
            cols = pl.ds((t * CORES + c) * BLOCK, BLOCK)
            r_up[:, cols] = src[c, :, :BLOCK].astype(F32)
            r_gate[:, cols] = src[c, :, BLOCK:].astype(F32)
    r_back[...] = back[...]
    r_gains[...] = pltpu.roll(small[...], (CHIPS - blk) * (small.shape[1] // CHIPS), 1)
    r_down[...] = down[0].astype(F32).T
    rows = out.shape[1]
    for i in range(2):
        place_ = blk * BLOCK + step * rows + lax.broadcasted_iota(jnp.int32, out.shape[1:], 0)
        r_out[i] = jnp.where(place_ < lengths[i], out[i].astype(F32), 0.0).astype(LOW)


def item_layer(
    tokens, cotangent, lengths, w_query, w_key, w_value, w_output, w_gate, w_up, w_down, gain_attn, gain_ffn
):
    width = tokens.shape[2]
    ff = w_gate.shape[1] // CORES
    half = width // 2
    keep, sems, results = layout(width, ff)
    scratch, tree = jax.tree.flatten((keep, sems))
    cosine, sine = turn_tables(CHIPS * BLOCK, width // HEADS)
    band = jax.ShapeDtypeStruct(tokens.shape, LOW)
    fins = pl.pallas_call(
        functools.partial(layer_kernel, tree),
        out_shape=[jax.ShapeDtypeStruct(shape, LOW) for shape in results]
        + [jax.ShapeDtypeStruct((8, width), F32), band, band],
        in_specs=any_specs(2) + [pl.BlockSpec(memory_space=pltpu.SMEM)] + any_specs(1)
        + vmem_specs(2) + any_specs(7),
        out_specs=any_specs(SMALL) + vmem_specs(1) + any_specs(2),
        scratch_shapes=scratch,
        compiler_params=pltpu.CompilerParams(
            collective_id=0, has_side_effects=True, vmem_limit_bytes=VMEM_BYTES
        ),
    )(
        tokens, cotangent, lengths, jnp.stack([cosine, sine]), gain_attn, gain_ffn,
        w_query, w_key, w_value, w_output, w_gate, w_up, w_down,
    )
    *sums, small, out_band, x_band = fins
    sums = [t.reshape(CORES, -1, t.shape[-1]) for t in sums]
    steps = 4
    rows = half // 2
    unit = ff // CHIPS

    def grad_spec(cols):
        return pl.BlockSpec((CORES, rows // steps, cols), lambda s: (0, s, 0))

    def wide_spec(cols):
        return pl.BlockSpec((rows // steps, cols), lambda s: (s, 0))

    band_spec = pl.BlockSpec((2, BLOCK // steps, width), lambda s: (0, s, 0))
    wide = lambda cols: jax.ShapeDtypeStruct((rows, cols), F32)
    output, g_tokens, g_query, g_key, g_value, g_output, g_gate, g_up, g_down, gains = pl.pallas_call(
        finish_kernel,
        grid=(steps,),
        out_shape=[band] * 2 + [wide(width)] * 4 + [wide(2 * ff)] * 2
        + [jax.ShapeDtypeStruct((CORES * unit, width), F32), jax.ShapeDtypeStruct((8, width), F32)],
        in_specs=[pl.BlockSpec(memory_space=pltpu.SMEM)]
        + [grad_spec(2 * unit)] * CHIPS
        + [pl.BlockSpec((1, width, unit // 2), lambda s: (s // 2, 0, s % 2))] + [grad_spec(half)] * 4 + [band_spec] * 2
        + [pl.BlockSpec((8, width), lambda s: (0, 0))],
        out_specs=[band_spec] * 2 + [wide_spec(width)] * 4 + [wide_spec(2 * ff)] * 2
        + [pl.BlockSpec((unit // 2, width), lambda s: (s, 0)), pl.BlockSpec((8, width), lambda s: (0, 0))],
        compiler_params=pltpu.CompilerParams(vmem_limit_bytes=VMEM_BYTES),
    )(lengths, *sums, out_band, x_band, small)
    return (output, g_tokens, g_query, g_key, g_value, g_output, g_gate, g_up, g_down, gains[0, : width // CHIPS], gains[1, : width // CHIPS])


VMEM_BYTES = 65 << 20


def turn_tables(length, head_dim):
    half_dim = head_dim // 2
    steps = np.arange(half_dim, dtype=np.float32) * np.float32(-2.0 * math.log(10000.0) / head_dim)
    angles = np.arange(length, dtype=np.float32)[:, None] * np.exp(steps)[None, :]
    cosine, sine = np.cos(angles), np.sin(angles)
    return (
        np.concatenate([cosine] * 4, axis=1).astype(np.float32),
        np.concatenate([-sine, sine, -sine, sine], axis=1).astype(np.float32),
    )


def solution(mesh):
    layer = item_layer if dict(mesh.shape) == {ITEM: 8, BAND: 4} else band_layer
    placed = (
        P("dp", "blk", None),
        P("dp", "blk", None),
        P("dp"),
        P(),
        P(),
        P(),
        P(),
        P(),
        P(),
        P(),
        P(),
        P(),
    )
    return jax.shard_map(
        layer,
        mesh=mesh,
        in_specs=placed,
        out_specs=(
            P("dp", "blk", None),
            P("dp", "blk", None),
            P("blk", None),
            P("blk", None),
            P("blk", None),
            P("blk", None),
            P("blk", None),
            P("blk", None),
            P("blk", None),
            P("blk"),
            P("blk"),
        ),
        check_vma=False,
    )
```

```python
import functools
import math
from types import SimpleNamespace

import jax
import jax.numpy as jnp
import numpy as np
from jax import lax
from jax.experimental import pallas as pl
from jax.experimental.pallas import tpu as pltpu
from jax.sharding import PartitionSpec as P

HEADS = 12


epsilon = 1e-05
masked_value = -1e30


def shifted(value, axis, by):
    size = lax.axis_size(axis)
    pairs = [(i, i + by) for i in range(size) if 0 <= i + by < size]
    return lax.ppermute(value, axis, pairs)


def tables(positions, head_dim):
    half_dim = head_dim // 2
    frequency = jnp.exp(
        jnp.arange(half_dim, dtype=jnp.float32) * (-2.0 * math.log(10000.0) / head_dim)
    )
    angles = positions[:, None] * frequency[None, :]
    return (jnp.cos(angles), jnp.sin(angles))


def rotate(tensor, cosine_table, sine_table):
    half_dim = tensor.shape[-1] // 2
    first = tensor[..., :half_dim]
    second = tensor[..., half_dim:]
    cosine_b = cosine_table[:, None, :]
    sine_b = sine_table[:, None, :]
    return jnp.concatenate(
        [first * cosine_b - second * sine_b, first * sine_b + second * cosine_b], axis=-1
    )


def contract_rows(left, right):
    return lax.dot_general(
        left, right, (((0,), (0,)), ((), ())), preferred_element_type=jnp.float32
    )


def times_transposed(left, right):
    return lax.dot_general(
        left, right, (((1,), (1,)), ((), ())), preferred_element_type=jnp.float32
    )


def band_layer(
    tokens,
    cotangent,
    lengths,
    w_query,
    w_key,
    w_value,
    w_output,
    w_gate,
    w_up,
    w_down,
    gain_attn,
    gain_ffn,
):
    item_count, band_len, model_width = tokens.shape
    head_count = HEADS
    head_dim = model_width // head_count
    band_count = lax.axis_size("blk")
    band_index = lax.axis_index("blk")
    seq_len = band_len * band_count
    row_count = item_count * band_len
    score_scale = head_dim ** (-0.5)
    positions = band_index * band_len + jnp.arange(band_len, dtype=jnp.int32)
    valid_rows = (positions[None, :] < lengths[:, None]).astype(jnp.float32).reshape(row_count, 1)
    cosine_table, sine_table = tables(positions.astype(jnp.float32), head_dim)
    key_positions = jnp.arange(seq_len, dtype=jnp.int32)
    allowed = key_positions[None, :] <= positions[:, None]
    incoming = tokens.astype(jnp.float32).reshape(row_count, model_width)
    inv_one = lax.rsqrt(jnp.mean(incoming * incoming, axis=-1, keepdims=True) + epsilon)
    normed_one = (incoming * inv_one * gain_attn).astype(jnp.bfloat16)
    query = rotate(
        jnp.dot(normed_one, w_query, preferred_element_type=jnp.float32).reshape(
            item_count, band_len, head_count, head_dim
        ),
        cosine_table,
        sine_table,
    ).astype(jnp.bfloat16)
    key_own = rotate(
        jnp.dot(normed_one, w_key, preferred_element_type=jnp.float32).reshape(
            item_count, band_len, head_count, head_dim
        ),
        cosine_table,
        sine_table,
    ).astype(jnp.bfloat16)
    value_own = jnp.dot(normed_one, w_value, preferred_element_type=jnp.float32).astype(
        jnp.bfloat16
    )
    pair = jnp.concatenate(
        [
            key_own.reshape(item_count, band_len, model_width),
            value_own.reshape(item_count, band_len, model_width),
        ],
        axis=-1,
    )
    buffer = jnp.zeros((item_count, band_count, band_len, 2 * model_width), jnp.bfloat16)
    buffer = lax.dynamic_update_slice_in_dim(buffer, pair[:, None], band_index, 1)

    def cycle_step(turn_index, state):
        carried, buffer = state
        carried = shifted(carried, "blk", 1)
        source = band_index - turn_index
        placed = lax.dynamic_update_slice_in_dim(
            buffer, carried[:, None], jnp.maximum(source, 0), 1
        )
        buffer = jnp.where(source >= 0, placed, buffer)
        return (carried, buffer)

    _, buffer = lax.fori_loop(1, band_count, cycle_step, (pair, buffer))
    whole = buffer.reshape(item_count, seq_len, 2 * model_width)
    keys_all = whole[..., :model_width].reshape(item_count, seq_len, head_count, head_dim)
    values_all = whole[..., model_width:].reshape(item_count, seq_len, head_count, head_dim)
    scores = (
        jnp.einsum("iqhd,ikhd->ihqk", query, keys_all, preferred_element_type=jnp.float32)
        * score_scale
    )
    scores = jnp.where(allowed[None, None], scores, masked_value)
    highest_s = jnp.max(scores, axis=-1, keepdims=True)
    expo = jnp.exp(scores - highest_s)
    totals = jnp.sum(expo, axis=-1, keepdims=True)
    softmax_w = expo / totals
    attended = jnp.einsum(
        "ihqk,ikhd->iqhd",
        softmax_w.astype(jnp.bfloat16),
        values_all,
        preferred_element_type=jnp.float32,
    )
    attended = attended.astype(jnp.bfloat16).reshape(row_count, model_width)
    middle = incoming + jnp.dot(attended, w_output, preferred_element_type=jnp.float32)
    inv_two = lax.rsqrt(jnp.mean(middle * middle, axis=-1, keepdims=True) + epsilon)
    normed_two = (middle * inv_two * gain_ffn).astype(jnp.bfloat16)
    gate_pre = jnp.dot(normed_two, w_gate, preferred_element_type=jnp.float32)
    up_pre = jnp.dot(normed_two, w_up, preferred_element_type=jnp.float32)
    sigmoid_g = jax.nn.sigmoid(gate_pre)
    silu_g = gate_pre * sigmoid_g
    hidden = (silu_g * up_pre).astype(jnp.bfloat16)
    ffn_out = jnp.dot(hidden, w_down, preferred_element_type=jnp.float32)
    result = (middle + ffn_out) * valid_rows
    output = result.astype(jnp.bfloat16).reshape(item_count, band_len, model_width)
    grad_res = cotangent.astype(jnp.float32).reshape(row_count, model_width) * valid_rows
    grad_ffn = grad_res.astype(jnp.bfloat16)
    grad_down = contract_rows(hidden, grad_ffn)
    grad_hidden = times_transposed(grad_ffn, w_down)
    grad_gate_pre = (
        grad_hidden * up_pre * (sigmoid_g * (1.0 + gate_pre * (1.0 - sigmoid_g)))
    ).astype(jnp.bfloat16)
    grad_up_pre = (grad_hidden * silu_g).astype(jnp.bfloat16)
    grad_gate = contract_rows(normed_two, grad_gate_pre)
    grad_up = contract_rows(normed_two, grad_up_pre)
    grad_normed_two = times_transposed(grad_gate_pre, w_gate) + times_transposed(grad_up_pre, w_up)
    grad_gain_ffn = jnp.sum(grad_normed_two * middle * inv_two, axis=0)
    scaled_two = grad_normed_two * gain_ffn
    grad_middle = grad_res + inv_two * (
        scaled_two
        - middle * inv_two * inv_two * jnp.mean(scaled_two * middle, axis=-1, keepdims=True)
    )
    grad_branch = grad_middle.astype(jnp.bfloat16)
    grad_output = contract_rows(attended, grad_branch)
    grad_attended = (
        times_transposed(grad_branch, w_output)
        .astype(jnp.bfloat16)
        .reshape(item_count, band_len, head_count, head_dim)
    )
    again = (
        jnp.einsum("iqhd,ikhd->ihqk", query, keys_all, preferred_element_type=jnp.float32)
        * score_scale
    )
    again = jnp.where(allowed[None, None], again, masked_value)
    probable = jnp.exp(again - highest_s) / totals
    grad_probs = jnp.einsum(
        "iqhd,ikhd->ihqk", grad_attended, values_all, preferred_element_type=jnp.float32
    )
    row_delta = jnp.sum(probable * grad_probs, axis=-1, keepdims=True)
    grad_scores = (probable * (grad_probs - row_delta)).astype(jnp.bfloat16)
    grad_query = (
        jnp.einsum("ihqk,ikhd->iqhd", grad_scores, keys_all, preferred_element_type=jnp.float32)
        * score_scale
    )
    grad_values = jnp.einsum(
        "ihqk,iqhd->ikhd",
        probable.astype(jnp.bfloat16),
        grad_attended,
        preferred_element_type=jnp.float32,
    )
    grad_keys = (
        jnp.einsum("ihqk,iqhd->ikhd", grad_scores, query, preferred_element_type=jnp.float32)
        * score_scale
    )
    grad_pair = jnp.concatenate(
        [
            grad_keys.reshape(item_count, seq_len, model_width),
            grad_values.reshape(item_count, seq_len, model_width),
        ],
        axis=-1,
    )
    blocks = grad_pair.reshape(item_count, band_count, band_len, 2 * model_width)
    empty_block = jnp.zeros((item_count, band_len, 2 * model_width), jnp.float32)

    def block_of(index):
        picked = lax.dynamic_index_in_dim(blocks, jnp.maximum(index, 0), 1, keepdims=False)
        return jnp.where(index >= 0, picked, empty_block)

    def cycle_back(turn_index, carried):
        carried = shifted(carried.astype(jnp.bfloat16), "blk", -1).astype(carried.dtype)
        return carried + block_of(band_index - (band_count - 1) + turn_index)

    own_grads = lax.fori_loop(1, band_count, cycle_back, block_of(band_index - (band_count - 1)))
    grad_key_own = own_grads[..., :model_width].reshape(item_count, band_len, head_count, head_dim)
    grad_value_raw = (
        own_grads[..., model_width:].astype(jnp.bfloat16).reshape(row_count, model_width)
    )
    grad_key_raw = (
        rotate(grad_key_own, cosine_table, -sine_table)
        .astype(jnp.bfloat16)
        .reshape(row_count, model_width)
    )
    grad_query_raw = (
        rotate(grad_query, cosine_table, -sine_table)
        .astype(jnp.bfloat16)
        .reshape(row_count, model_width)
    )
    grad_wquery = contract_rows(normed_one, grad_query_raw)
    grad_wkey = contract_rows(normed_one, grad_key_raw)
    grad_wvalue = contract_rows(normed_one, grad_value_raw)
    grad_normed_one = (
        times_transposed(grad_query_raw, w_query)
        + times_transposed(grad_key_raw, w_key)
        + times_transposed(grad_value_raw, w_value)
    )
    grad_gain_attn = jnp.sum(grad_normed_one * incoming * inv_one, axis=0)
    scaled_one = grad_normed_one * gain_attn
    grad_incoming = grad_middle + inv_one * (
        scaled_one
        - incoming * inv_one * inv_one * jnp.mean(scaled_one * incoming, axis=-1, keepdims=True)
    )
    grad_tokens = grad_incoming.astype(jnp.bfloat16).reshape(item_count, band_len, model_width)
    summed = (
        lax.psum_scatter(
            grad_wquery.astype(jnp.bfloat16), "blk", scatter_dimension=0, tiled=True
        ).astype(jnp.float32),
        lax.psum_scatter(
            grad_wkey.astype(jnp.bfloat16), "blk", scatter_dimension=0, tiled=True
        ).astype(jnp.float32),
        lax.psum_scatter(
            grad_wvalue.astype(jnp.bfloat16), "blk", scatter_dimension=0, tiled=True
        ).astype(jnp.float32),
        lax.psum_scatter(
            grad_output.astype(jnp.bfloat16), "blk", scatter_dimension=0, tiled=True
        ).astype(jnp.float32),
        lax.psum_scatter(
            grad_gate.astype(jnp.bfloat16), "blk", scatter_dimension=0, tiled=True
        ).astype(jnp.float32),
        lax.psum_scatter(
            grad_up.astype(jnp.bfloat16), "blk", scatter_dimension=0, tiled=True
        ).astype(jnp.float32),
        lax.psum_scatter(
            grad_down.astype(jnp.bfloat16), "blk", scatter_dimension=0, tiled=True
        ).astype(jnp.float32),
        lax.psum_scatter(
            grad_gain_attn.astype(jnp.bfloat16), "blk", scatter_dimension=0, tiled=True
        ).astype(jnp.float32),
        lax.psum_scatter(
            grad_gain_ffn.astype(jnp.bfloat16), "blk", scatter_dimension=0, tiled=True
        ).astype(jnp.float32),
    )
    summed = (
        lax.psum(summed[0].astype(jnp.bfloat16), "dp").astype(jnp.float32),
        lax.psum(summed[1].astype(jnp.bfloat16), "dp").astype(jnp.float32),
        lax.psum(summed[2].astype(jnp.bfloat16), "dp").astype(jnp.float32),
        lax.psum(summed[3].astype(jnp.bfloat16), "dp").astype(jnp.float32),
        lax.psum(summed[4].astype(jnp.bfloat16), "dp").astype(jnp.float32),
        lax.psum(summed[5].astype(jnp.bfloat16), "dp").astype(jnp.float32),
        lax.psum(summed[6].astype(jnp.bfloat16), "dp").astype(jnp.float32),
        lax.psum(summed[7].astype(jnp.bfloat16), "dp").astype(jnp.float32),
        lax.psum(summed[8].astype(jnp.bfloat16), "dp").astype(jnp.float32),
    )
    return (
        output,
        grad_tokens,
        summed[0],
        summed[1],
        summed[2],
        summed[3],
        summed[4],
        summed[5],
        summed[6],
        summed[7],
        summed[8],
    )


MESH = pl.DeviceIdType.MESH
ITEM, BAND = "dp", "blk"
CORES = 2
CHIPS = 4
BLOCK = 256
PAIR = 128
LOW = jnp.bfloat16
F32 = jnp.float32


def place():
    dp = lax.axis_index(ITEM)
    return dp, lax.axis_index(BAND), lax.rem(dp, CORES)


def near(dp, blk, core=0, chip=0, line=0):
    flip = core + CORES * line
    return {ITEM: dp ^ flip if flip else dp, BAND: blk ^ chip if chip else blk}


def greet(dp, blk, flips):
    barrier = pltpu.get_barrier_semaphore()
    for flip in flips:
        pl.semaphore_signal(barrier, inc=1, device_id=near(dp, blk, *flip), device_id_type=MESH)
    return barrier


def remote(src, dst, send, recv, where):
    return pltpu.make_async_remote_copy(
        src_ref=src, dst_ref=dst, send_sem=send, recv_sem=recv, device_id=where, device_id_type=MESH
    )


def part(start, size):
    return pl.ds(pl.multiple_of(start, size), size)


PLANE = [(core, chip, 0) for chip in range(CHIPS) for core in range(CORES) if core or chip]
REACH = PLANE + [(0, 0, 1), (0, 0, 3)]


def plus(one, other, kind=LOW):
    return (one.astype(F32) + other.astype(F32)).astype(kind)


class Gather:
    SEMS = [(2,), (4, 2), (4,), (4,), (4,)]

    def __init__(self, band, buf, sems):
        self.band, self.buf = band, buf
        self.own, self.send, self.recv, self.fsend, self.frecv = sems
        self.dp, self.blk, self.core = place()
        self.rows = band.shape[1]
        self.half = self.rows // 2
        self.mine = (self.blk // 2) == self.core

    def out(self, r, h):
        target = self.blk ^ r
        return remote(
            self.band.at[lax.rem(target, 2), pl.ds(h * self.half, self.half)],
            self.buf.at[part(self.blk * self.rows + h * self.half, self.half)],
            self.send.at[r, h],
            self.recv.at[r],
            {ITEM: self.dp - self.core + h, BAND: target},
        )

    def across(self, r):
        rows = self.buf.at[part((self.blk ^ r) * self.rows + self.core * self.half, self.half)]
        return remote(rows, rows, self.fsend.at[r], self.frecv.at[r], near(self.dp, self.blk, 1))

    def here(self):
        rows = self.buf.at[part(self.blk * self.rows, self.rows)]
        return pltpu.make_async_copy(self.band.at[lax.rem(self.blk, 2)], rows, self.own.at[0])

    def there(self):
        rows = self.buf.at[part(self.blk * self.rows, self.rows)]
        src = self.band.at[lax.rem(self.blk, 2)]
        return remote(src, rows, self.fsend.at[0], self.frecv.at[0], near(self.dp, self.blk, 1))

    def sends(self, r):
        return ((self.blk ^ r) // 2) == self.core

    def start(self):
        for r in (1, 2, 3):

            @pl.when(self.sends(r))
            def _():
                for h in range(2):
                    self.out(r, h).start()

        @pl.when(self.mine)
        def _():
            self.here().start()
            self.there().start()

    def forward(self, r):
        self.out(r, 0).wait_recv()
        self.across(r).start()

    def ready(self, r):
        if r:
            self.across(r).wait_recv()
            return

        @pl.when(self.mine)
        def _():
            self.here().wait()

        @pl.when(jnp.logical_not(self.mine))
        def _():
            self.there().wait_recv()

    def drain(self):
        @pl.when(self.mine)
        def _():
            self.there().wait_send()

        for r in (1, 2, 3):
            self.across(r).wait_send()

            @pl.when(self.sends(r))
            def _():
                for h in range(2):
                    self.out(r, h).wait_send()


class Return:
    SEMS = [(1,), (4,), (2, 2)]

    def __init__(self, src, band, sems):
        self.src, self.band = src, band
        self.own, self.send, self.recv = sems
        self.dp, self.blk, self.core = place()
        self.half = src.shape[1]
        self.home = self.blk // 2

    def slot(self):
        return self.band.at[lax.rem(self.blk, 2), part(self.core * self.half, self.half)]

    def out(self, r):
        chip = self.blk ^ r
        return remote(
            self.src.at[chip],
            self.slot(),
            self.send.at[r],
            self.recv.at[lax.rem(self.blk, 2), self.core],
            {ITEM: self.dp - self.core + self.home, BAND: chip},
        )

    def keep(self):
        return pltpu.make_async_copy(self.src.at[self.blk], self.slot(), self.own.at[0])

    def start(self):
        for r in (3, 1, 2):
            self.out(r).start()

        @pl.when(self.home == self.core)
        def _():
            self.keep().start()

        @pl.when(self.home != self.core)
        def _():
            self.out(0).start()

    def drain(self):
        @pl.when(self.home == self.core)
        def _():
            self.keep().wait()

        @pl.when(self.home != self.core)
        def _():
            self.out(0).wait_send()

        for r in (1, 2, 3):
            self.out(r).wait_send()

    def arrived(self):
        for i in range(2):
            for h in range(2):
                local = (self.core * 2 + i == self.blk) & (self.core == h)

                @pl.when(jnp.logical_not(local))
                def _():
                    remote(
                        self.src.at[0],
                        self.band.at[i, pl.ds(h * self.half, self.half)],
                        self.send.at[0],
                        self.recv.at[i, h],
                        near(self.dp, self.blk, 1),
                    ).wait_recv()


class Line:
    def locate(self):
        self.dp, self.blk, self.core = place()
        z = self.dp // CORES
        self.outer = (z == 0) | (z == 3)
        self.inner = jnp.logical_not(self.outer)

    def stage(self, n):
        (self.stage0, self.stage1, self.stage2, self.stage3, self.stage4, self.stage5, self.stage6)[n]()


class Chunk(Line):
    SEMS = [(2, 2, 2), (2, 2), (3, 2, 2), (2, 3)]

    def __init__(self, src, buffers, result, sems, turned=False):
        self.src, self.result, self.turned = src, result, turned
        self.first, self.second, self.line = buffers
        self.s1, self.s2, self.sz, self.sc = sems
        self.locate()

    @staticmethod
    def shapes(rows, cols, turned):
        half = (rows // 2, cols // CHIPS) if turned else (rows // CHIPS // 2, cols)
        return [(2, 2) + half, (2,) + half, (2, 2) + half], (CORES, 2) + half

    def piece(self, chip, h):
        rows, cols = self.first.shape[2:]
        if self.turned:
            return self.src.at[pl.ds(h * rows, rows), part(chip * cols, cols)]
        return self.src.at[part(chip * 2 * rows + h * rows, rows)]

    def ways(self, h):
        return (1, 2) if h == 0 else (2, 1)

    def step1(self, h, n):
        near_way, far_way = self.ways(h)
        chip = self.blk ^ near_way ^ (far_way if n else 0)
        return remote(
            self.piece(chip, h), self.first.at[h, n], self.s1.at[0, h, n], self.s1.at[1, h, n],
            near(self.dp, self.blk, 0, near_way),
        )

    def step2(self, h):
        return remote(
            self.first.at[h, 1], self.second.at[h], self.s2.at[0, h], self.s2.at[1, h],
            near(self.dp, self.blk, 0, self.ways(h)[1]),
        )

    def hop(self, n, h):
        src = (self.second.at[h], self.line.at[0, h], self.second.at[h])[n]
        dst = self.line.at[1 if n == 1 else 0, h]
        return remote(
            src, dst, self.sz.at[n, h, 0], self.sz.at[n, h, 1],
            near(self.dp, self.blk, 0, 0, 3 if n == 1 else 1),
        )

    def share(self, total, h):
        slot = self.result.at[self.core, h]
        return (
            remote(total, slot, self.sc.at[h, 0], self.sc.at[h, 1], near(self.dp, self.blk, 1)),
            pltpu.make_async_copy(total, slot, self.sc.at[h, 2]),
        )

    def xy_start(self):
        for n in (1, 0):
            for h in range(2):
                self.step1(h, n).start()

    def xy_turn(self):
        for h in range(2):
            self.step1(h, 1).wait_recv()
            chip = self.blk ^ self.ways(h)[1]
            self.first[h, 1] = plus(self.first[h, 1], self.piece(chip, h)[...])
            self.step2(h).start()

    def xy_end(self, h):
        self.step1(h, 0).wait_recv()
        self.step2(h).wait_recv()
        own = plus(self.first[h, 0], self.piece(self.blk, h)[...], F32)
        self.second[h] = plus(own, self.second[h])

    def xy_drain(self):
        for h in range(2):
            for n in range(2):
                self.step1(h, n).wait_send()
            self.step2(h).wait_send()

    def stage0(self):
        self.xy_start()

    def stage1(self):
        self.xy_turn()

    def stage2(self):
        for h in range(2):
            self.xy_end(h)

            @pl.when(self.outer)
            def _():
                self.hop(0, h).start()

    def stage3(self):
        @pl.when(self.inner)
        def _():
            for h in range(2):
                self.hop(0, h).wait_recv()
                self.line[0, h] = plus(self.line[0, h], self.second[h])
                self.hop(1, h).start()

    def stage4(self):
        @pl.when(self.inner)
        def _():
            for h in range(2):
                self.hop(1, h).wait_recv()
                self.second[h] = plus(self.line[0, h], self.line[1, h])
                self.hop(2, h).start()
                for copy in self.share(self.second.at[h], h):
                    copy.start()

    def stage5(self):
        @pl.when(self.outer)
        def _():
            for h in range(2):
                self.hop(2, h).wait_recv()
                for copy in self.share(self.line.at[0, h], h):
                    copy.start()

    def stage6(self):
        for h in range(2):
            for copy in self.share(self.second.at[h], h):
                copy.wait()
        self.xy_drain()

        @pl.when(self.outer)
        def _():
            for h in range(2):
                self.hop(0, h).wait_send()

        @pl.when(self.inner)
        def _():
            for h in range(2):
                self.hop(1, h).wait_send()
                self.hop(2, h).wait_send()


class PairChunk(Chunk):
    SEMS = [(CHIPS, 2), (2, 2, 2), (2, 2), (2, 2), (3,)]

    def __init__(self, src, buffers, result, sems, turned=False):
        self.src, self.result, self.turned = src, result, turned
        self.pair, self.first, self.second, self.line, self.total = buffers
        self.sp, self.s1, self.s2, self.sz, self.sc = sems
        self.locate()
        self.kept = lax.rem((self.dp // CORES + 1) // 2, 2)

    @staticmethod
    def shapes(rows, cols, turned):
        whole = (rows // 2, cols // CHIPS) if turned else (rows // CHIPS // 2, cols)
        half = (whole[0] // 2, whole[1])
        return [(CHIPS,) + whole, (2, 2) + half, (2,) + half, (2,) + half, (2, 2) + half], (CORES, 2, 2) + half

    def share_of(self, chip, s):
        rows, cols = self.pair.shape[1:]
        if self.turned:
            return self.src.at[part(s * rows, rows), pl.ds(chip * cols, cols)]
        return self.src.at[part(chip * 2 * rows + s * rows, rows)]

    def piece(self, chip, h):
        rows = self.pair.shape[1] // 2
        return self.pair.at[chip, pl.ds(h * rows, rows)]

    def swap(self, chip):
        return remote(
            self.share_of(chip, 1 - self.kept), self.pair.at[chip], self.sp.at[chip, 0], self.sp.at[chip, 1],
            near(self.dp, self.blk, 0, 0, 1),
        )

    def middle(self):
        return remote(
            self.second, self.line, self.sz.at[0, 0], self.sz.at[0, 1], near(self.dp, self.blk, 0, 0, 3)
        )

    def hand(self):
        half = self.total.at[self.kept]
        return remote(half, half, self.sz.at[1, 0], self.sz.at[1, 1], near(self.dp, self.blk, 0, 0, 1))

    def spread(self):
        slot = self.result.at[self.core]
        return (
            remote(self.total, slot, self.sc.at[0], self.sc.at[1], near(self.dp, self.blk, 1)),
            pltpu.make_async_copy(self.total, slot, self.sc.at[2]),
        )

    def stage0(self):
        for chip in range(CHIPS):
            self.swap(chip).start()

    def stage1(self):
        for chip in range(CHIPS):
            self.swap(chip).wait_recv()
            self.pair[chip] = plus(self.pair[chip], self.share_of(chip, self.kept)[...])
        self.xy_start()

    def stage2(self):
        self.xy_turn()

    def stage3(self):
        for h in range(2):
            self.xy_end(h)
        self.middle().start()

    def stage4(self):
        self.middle().wait_recv()
        for h in range(2):
            self.total[self.kept, h] = plus(self.second[h], self.line[h])
        self.hand().start()

    def stage5(self):
        self.hand().wait_recv()
        for copy in self.spread():
            copy.start()

    def stage6(self):
        for copy in self.spread():
            copy.wait()
        for chip in range(CHIPS):
            self.swap(chip).wait_send()
        self.xy_drain()
        self.middle().wait_send()
        self.hand().wait_send()


class Small(Line):
    SEMS = [(6, 2)]
    SLOTS = 11

    def __init__(self, hold, result, sems):
        self.hold, self.result = hold, result
        (self.sem,) = sems
        self.locate()

    def go(self, n):
        flips = ((1, 0, 0), (0, 1, 0), (0, 2, 0), (0, 0, 1), (0, 0, 3), (0, 0, 1))
        src, dst = (10, 10) if n == 5 else (2 * n, 2 * n + 1)
        return remote(
            self.hold.at[src], self.hold.at[dst], self.sem.at[n, 0], self.sem.at[n, 1],
            near(self.dp, self.blk, *flips[n]),
        )

    def add(self, n, to):
        self.go(n).wait_recv()
        self.hold[to] = self.hold[2 * n] + self.hold[2 * n + 1]

    def stage0(self):
        self.go(0).start()

    def stage1(self):
        for n in range(2):
            self.add(n, 2 * n + 2)
            self.go(n + 1).start()

    def stage2(self):
        self.add(2, 6)

        @pl.when(self.outer)
        def _():
            self.go(3).start()

    def stage3(self):
        @pl.when(self.inner)
        def _():
            self.add(3, 8)
            self.go(4).start()

    def stage4(self):
        @pl.when(self.inner)
        def _():
            self.add(4, 10)
            self.go(5).start()

    def stage5(self):
        @pl.when(self.outer)
        def _():
            self.go(5).wait_recv()

        self.result[...] = self.hold[10]

    def stage6(self):
        for n in range(3):
            self.go(n).wait_send()

        @pl.when(self.outer)
        def _():
            self.go(3).wait_send()

        @pl.when(self.inner)
        def _():
            self.go(4).wait_send()
            self.go(5).wait_send()


def dot(left, right):
    return jnp.dot(left, right, preferred_element_type=F32)


def dot_rows(left, right):
    return lax.dot_general(left, right, (((0,), (0,)), ((), ())), preferred_element_type=F32)


def dot_cols(left, right):
    return lax.dot_general(left, right, (((1,), (1,)), ((), ())), preferred_element_type=F32)


def inverse_rms(values):
    return lax.rsqrt(jnp.mean(values * values, axis=-1, keepdims=True) + epsilon)


def turn(t, cosine, sine, sign):
    quarter = PAIR // 4
    lane = lax.broadcasted_iota(jnp.int32, t.shape, 1)
    other = jnp.where(
        lane % (2 * quarter) < quarter,
        pltpu.roll(t, PAIR - quarter, 1),
        pltpu.roll(t, quarter, 1),
    )
    return t * cosine + (sign * sine) * other


def both_heads(t):
    lane = lax.broadcasted_iota(jnp.int32, t.shape, 1)
    zero = jnp.zeros_like(t)
    return jnp.concatenate(
        [jnp.where(lane < PAIR // 2, t, zero), jnp.where(lane < PAIR // 2, zero, t)], axis=0
    )


def one_pair(t):
    rows = t.shape[0] // 2
    lane = lax.broadcasted_iota(jnp.int32, (rows, PAIR), 1)
    return jnp.where(lane < PAIR // 2, t[:rows], t[rows:])


FF0, FF1, FF2, FF3, DOWN, OUT, QUERY, KEY, VALUE, SMALL = range(10)
TILES = (FF0, FF1, FF2, FF3)
PAIRED = (FF2, OUT)
(
    TILE0, TILE1, TILE2, TILE3, GRAD_DOWN, PART_OUT, GRAD_N2, OWN_OUT, GRAD_MID, GRAD_OUT, GRAD_ATT,
    HEADS0, HEADS1, HEADS2, GRAD_QKV, PART_N1, OWN_N1, SEND_OUT, SEND_X,
) = range(100, 119)
ORDER = (
    TILE0, FF0, TILE1, FF1, TILE2, FF0, FF2, TILE3, FF3, PART_OUT, GRAD_N2, FF1, FF0, GRAD_DOWN, FF2, OWN_OUT, FF3,
    GRAD_MID, FF1, FF2, DOWN, GRAD_OUT, FF0, OUT, GRAD_ATT, HEADS0, HEADS1, FF1, FF3, FF0, DOWN, HEADS2, OUT, FF2,
    GRAD_QKV, VALUE, FF1, FF3, DOWN, PART_N1, OUT, VALUE, KEY, FF1, OUT, FF2, QUERY, OWN_N1, SMALL, VALUE, FF3,
    DOWN, SMALL, QUERY, OUT, KEY, FF3, SEND_X, DOWN, SEND_OUT, QUERY, VALUE, QUERY, VALUE, SMALL, KEY, VALUE, KEY,
    DOWN, SMALL, FF0, QUERY, OUT, KEY, QUERY, SMALL, FF2, KEY, SMALL,
)


def layout(width, ff):
    seq = CHIPS * BLOCK
    half = width // 2
    pairs = half // PAIR

    def low(*shape):
        return pltpu.VMEM(shape, LOW)

    def wide(*shape):
        return pltpu.VMEM(shape, F32)

    grads, sums = [], []
    keep = dict(
        w_qkv=low(width, 3 * half), w_out=low(width, width), w_ff=low(width, 2 * ff),
        w_down=low(ff, width), turns=wide(2, seq, PAIR),
        x=low(seq, width), g_ffn=low(seq, width), n1=low(seq, width),
        q=low(seq, half), k=low(seq, half), v=low(seq, half),
        prob=[low(pairs, 2 * BLOCK, (i + 1) * BLOCK) for i in range(CHIPS)],
        att=low(seq, width), middle=wide(seq, width), n2=low(seq, width), n2_turned=low(width, seq),
        hidden=low(seq, ff), g_ff=low(seq, 2 * ff), share=wide(seq, PAIR), gn2=low(seq, width),
        swap_out=low(CHIPS, BLOCK // 2, width), swap_in=low(2, CHIPS, BLOCK // 2, width),
        band=low(CHIPS, BLOCK // 2, width),
        dk=wide(seq, PAIR), dv=wide(seq, PAIR), hold=wide(Small.SLOTS, 8, width),
        grad=grads, sums=sums,
    )
    sems = dict(
        load=[(18,)], gather_x=Gather.SEMS, gather_g=Gather.SEMS, att=[(2, pairs)], swap=[(2, 2)], gn2=[(2, CHIPS)],
        back_out=Return.SEMS, back_x=Return.SEMS, small=Small.SEMS,
        sums=[PairChunk.SEMS if name in PAIRED else Chunk.SEMS for name in range(SMALL)],
    )
    sems = jax.tree.map(pltpu.SemaphoreType.DMA, sems, is_leaf=lambda t: isinstance(t, tuple))
    results = []
    for name in range(SMALL):
        cols = ff if name == DOWN else 2 * (ff // CHIPS) if name in TILES else half
        kind = PairChunk if name in PAIRED else Chunk
        shapes, result = kind.shapes(width, cols, name == DOWN)
        results.append(result)
        grads.append(low(width, cols))
        sums.append([low(*shape) for shape in shapes])
    return keep, sems, results


def layer_kernel(
    scratch, tokens, cotangent, lengths, turns, gain_attn, gain_ffn,
    w_query, w_key, w_value, w_output, w_gate, w_up, w_down, *refs,
):
    width, ff = tokens.shape[2], w_gate.shape[1] // CORES
    results, (small_result, out_band, x_band) = refs[:SMALL], refs[SMALL : SMALL + 3]
    keep, sems = jax.tree.unflatten(scratch, refs[SMALL + 3 :])
    m, sem = SimpleNamespace(**keep), SimpleNamespace(**sems)
    dp, blk, core = place()
    partner = near(dp, blk, 1)
    half = width // 2
    pairs = half // PAIR
    scale = (width // HEADS) ** (-0.5)
    mine = pl.multiple_of(core * half, half)

    def block(r):
        return part(r * BLOCK, BLOCK)

    def half_block(chip, c):
        return part(chip * BLOCK + c * (BLOCK // 2), BLOCK // 2)

    def lanes(p):
        return part(p * PAIR, PAIR)

    barrier = greet(dp, blk, REACH)

    loads = []

    def load(src, dst):
        copy = pltpu.make_async_copy(src, dst, sem.load[0].at[len(loads)])
        copy.start()
        loads.append(copy)

    stage = m.band.reshape(2, BLOCK, width)
    load(cotangent, stage)
    load(turns, m.turns)
    for n, weight in enumerate((w_query, w_key, w_value)):
        load(weight.at[:, pl.ds(mine, half)], m.w_qkv.at[:, pl.ds(n * half, half)])

    gather_x = Gather(tokens, m.x, sem.gather_x)
    gather_g = Gather(stage, m.g_ffn, sem.gather_g)
    pl.semaphore_wait(barrier, len(REACH))
    gather_x.start()
    load(w_output, m.w_out)
    unit = ff // CHIPS
    for chip in range(CHIPS):
        there = part(chip * CORES * unit + core * unit, unit)
        load(w_up.at[:, there], m.w_ff.at[:, pl.ds(2 * chip * unit, unit)])
        load(w_gate.at[:, there], m.w_ff.at[:, pl.ds((2 * chip + 1) * unit, unit)])
        load(w_down.at[there], m.w_down.at[pl.ds(chip * unit, unit)])
    for copy in loads[:5]:
        copy.wait()
    for i in range(2):
        row = blk * BLOCK + lax.broadcasted_iota(jnp.int32, (BLOCK, width), 0)
        stage[i] = jnp.where(row < lengths[i], stage[i].astype(F32), 0.0).astype(LOW)

    def project(r):
        rows = block(blk ^ r)
        x = m.x[rows].astype(F32)
        n1 = (x * inverse_rms(x) * gain_attn[...][None]).astype(LOW)
        m.n1[rows] = n1
        cosine, sine = m.turns[0, rows], m.turns[1, rows]
        for n, store in enumerate((m.q, m.k, m.v)):
            full = dot(n1, m.w_qkv[:, n * half : (n + 1) * half])
            for p in range(pairs):
                t = full[:, p * PAIR : (p + 1) * PAIR]
                if n < 2:
                    t = turn(t, cosine, sine, 1.0)
                if n == 0:
                    t = t.astype(LOW).astype(F32) * scale
                store[rows, p * PAIR : (p + 1) * PAIR] = t.astype(LOW)

    gather_x.ready(0)
    project(0)
    gather_x.forward(1)
    gather_x.forward(2)
    gather_x.ready(1)
    gather_x.forward(3)
    gather_g.start()
    project(1)
    gather_x.ready(2)
    project(2)
    gather_x.ready(3)
    project(3)

    row = lax.broadcasted_iota(jnp.int32, (2 * BLOCK, BLOCK), 0) % BLOCK
    seen = lax.broadcasted_iota(jnp.int32, (2 * BLOCK, BLOCK), 1) <= row

    lane = lax.broadcasted_iota(jnp.int32, (BLOCK, PAIR), 1)

    def att_cols(p):
        return part(core * half + p * PAIR, PAIR)

    def att_copy(p):
        cols = m.att.at[:, att_cols(p)]
        return remote(cols, cols, sem.att[0].at[0, p], sem.att[0].at[1, p], partner)

    def scores(p, i):
        size = BLOCK * i
        q = both_heads(m.q[pl.ds(size, BLOCK), lanes(p)])
        score = dot_cols(q, m.k[pl.ds(0, size + BLOCK), lanes(p)])
        own = jnp.where(seen, score[:, size:], masked_value)
        return jnp.concatenate([score[:, :size], own], axis=1) if i else own

    def attend(p, i, prob):
        rows = pl.ds(BLOCK * i, BLOCK)
        v = m.v[pl.ds(0, BLOCK * (i + 1)), lanes(p)]
        both = dot(prob, jnp.concatenate([v, jnp.ones_like(v)], axis=1))
        att, share = both[:, :PAIR], 1.0 / both[:, PAIR:]
        kept = jnp.where(lane == 2 * p, share[:BLOCK], m.share[rows])
        m.share[rows] = jnp.where(lane == 2 * p + 1, share[BLOCK:], kept)
        m.att[rows, att_cols(p)] = one_pair(att * share).astype(LOW)

    @pl.loop(0, pairs)
    def _(p):
        later = scores(p, 0)
        for i in range(CHIPS):
            score = later
            if i + 1 < CHIPS:
                later = scores(p, i + 1)
            slabs = [score[:, n : n + PAIR] for n in range(0, BLOCK * (i + 1), PAIR)]
            top = jnp.max(functools.reduce(jnp.maximum, slabs), axis=-1, keepdims=True)
            if i:
                attend(p, i - 1, prob)
            prob = jnp.exp(score - top).astype(LOW)
            m.prob[i][p] = prob
        attend(p, CHIPS - 1, prob)
        att_copy(p).start()

    for r in (1, 2, 3):
        gather_g.forward(r)
    loads[5].wait()
    for p in range(pairs):
        att_copy(p).wait_recv()

    @pl.loop(0, CHIPS, unroll=True)
    def _(r):
        rows = block(r)
        middle = m.x[rows].astype(F32) + dot(m.att[rows], m.w_out[...])
        m.middle[rows] = middle
        n2 = (middle * inverse_rms(middle) * gain_ffn[...][None]).astype(LOW)
        m.n2[rows] = n2
        m.n2_turned[:, rows] = n2.T

    for r in range(CHIPS):
        gather_g.ready(r)
    for copy in loads[6:]:
        copy.wait()

    sums = []
    for name in range(SMALL):
        own = (m.grad[name], m.sums[name], results[name], sem.sums[name])
        sums.append((PairChunk if name in PAIRED else Chunk)(*own, name == DOWN))
    sums.append(Small(m.hold, small_result, sem.small))
    done = [0] * len(sums)

    def advance(*names):
        for name in names:
            sums[name].stage(done[name])
            done[name] += 1

    def tile(t):
        units, both = block(t), part(t * 2 * BLOCK, 2 * BLOCK)

        @pl.loop(0, CHIPS, unroll=True)
        def _(r):
            rows = block(r)
            pre = dot(m.n2[rows], m.w_ff[:, both])
            up, gate = pre[:, :BLOCK], pre[:, BLOCK:]
            g_hidden = dot_cols(m.g_ffn[rows], m.w_down[units])
            sig = 0.5 * jnp.tanh(0.5 * gate) + 0.5
            silu = gate * sig
            m.hidden[rows, units] = (silu * up).astype(LOW)
            m.g_ff[rows, part(t * 2 * BLOCK, BLOCK)] = (g_hidden * silu).astype(LOW)
            g_gate = g_hidden * up * (sig * (1.0 + gate * (1.0 - sig)))
            m.g_ff[rows, part(t * 2 * BLOCK + BLOCK, BLOCK)] = g_gate.astype(LOW)

        for name in TILES:

            @pl.when(t == name)
            def _():
                for r in range(width // BLOCK):
                    rows = pl.ds(r * BLOCK, BLOCK)
                    m.grad[name][rows] = dot(m.n2_turned[rows], m.g_ff[:, both]).astype(LOW)

    def grad_down():
        @pl.loop(0, width // BLOCK, unroll=True)
        def _(t):
            rows = block(t)
            m.grad[DOWN][rows] = dot_rows(m.g_ffn[:, rows], m.hidden[...]).astype(LOW)

    def swap(n):
        return remote(m.swap_out, m.swap_in.at[n], sem.swap[0].at[n, 0], sem.swap[0].at[n, 1], partner)

    def part_out():
        @pl.loop(0, CHIPS, unroll=True)
        def _(chip):
            m.swap_out[chip] = dot(m.hidden[half_block(chip, 1 - core)], m.w_down[...]).astype(LOW)

        swap(0).start()

    back_out = Return(m.band, out_band, sem.back_out)
    back_x = Return(m.swap_out, x_band, sem.back_x)

    def own_out():
        swap(0).wait()
        gather_g.drain()

        @pl.loop(0, CHIPS, unroll=True)
        def _(chip):
            rows = half_block(chip, core)
            out = dot(m.hidden[rows], m.w_down[...]) + m.swap_in[0, chip].astype(F32)
            m.band[chip] = (m.middle[rows] + out).astype(LOW)

    def gn2_copy(r):
        return remote(
            m.n2.at[block(r)], m.gn2.at[block(r)], sem.gn2[0].at[0, r], sem.gn2[0].at[1, r], partner,
        )

    def grad_n2():
        @pl.loop(0, CHIPS, unroll=True)
        def _(r):
            m.n2[block(r)] = dot_cols(m.g_ff[block(r)], m.w_ff[...]).astype(LOW)
            gn2_copy(r).start()

    g_branch, g_mid = m.gn2, m.middle

    def grad_mid():
        m.hold[0] = jnp.zeros((8, width), F32)

        @pl.loop(0, CHIPS, unroll=True)
        def _(r):
            rows = block(r)
            gn2_copy(r).wait_recv()
            g_n2 = plus(m.n2[rows], m.gn2[rows], F32)
            middle = m.middle[rows]
            inv = inverse_rms(middle)
            m.hold[0, 1:2] += 0.5 * jnp.sum(g_n2 * middle * inv, axis=0, keepdims=True)
            a2 = g_n2 * gain_ffn[...][None]
            inner = jnp.mean(a2 * middle, axis=-1, keepdims=True)
            got = m.g_ffn[rows].astype(F32) + inv * (a2 - middle * (inv * inv * inner))
            g_branch[rows] = got.astype(LOW)
            g_mid[rows] = got

    def grad_out():
        @pl.loop(0, width // BLOCK, unroll=True)
        def _(t):
            rows = block(t)
            m.grad[OUT][rows] = dot_rows(m.att[:, rows], g_branch[:, pl.ds(mine, half)]).astype(LOW)

    g_att = m.hidden
    g_qkv = m.g_ff.at[:, pl.ds(0, 3 * half)]
    g_q, g_k, g_v = (m.g_ff.at[:, pl.ds(n * half, half)] for n in range(3))

    def grad_att():
        @pl.loop(0, CHIPS, unroll=True)
        def _(r):
            g_att[block(r), pl.ds(0, half)] = dot_cols(g_branch[block(r)], m.w_out[pl.ds(mine, half)]).astype(LOW)

    def heads(p):
        for i in range(CHIPS - 1, -1, -1):
            rows, size = pl.ds(BLOCK * i, BLOCK), BLOCK * (i + 1)
            past = pl.ds(0, size)
            kept = m.share[rows]
            share = jnp.concatenate(
                [
                    jnp.sum(jnp.where(lane == 2 * p + n, kept, 0.0), axis=-1, keepdims=True)
                    for n in range(2)
                ],
                axis=0,
            )
            g = both_heads(g_att[rows, lanes(p)]).astype(F32) * share
            q = both_heads(m.q[rows, lanes(p)])
            out = m.att[rows, att_cols(p)].astype(F32)
            delta = jnp.sum(g * jnp.concatenate([out, out], axis=0), axis=-1, keepdims=True)
            g = g.astype(LOW)
            prob = m.prob[i][p]
            g_prob = dot_cols(g, m.v[past, lanes(p)])
            g_score = (prob.astype(F32) * (g_prob - delta)).astype(LOW)
            got_q = one_pair(dot(g_score, m.k[past, lanes(p)])) * scale
            g_q[rows, lanes(p)] = turn(got_q, m.turns[0, rows], m.turns[1, rows], -1.0).astype(LOW)
            got_k, got_v = dot_rows(g_score, q), dot_rows(prob, g)
            if i == CHIPS - 1:
                m.dk[...] = got_k
                m.dv[...] = got_v
            else:
                m.dk[past] += got_k
                m.dv[past] += got_v
        for r in range(CHIPS):
            rows = pl.ds(BLOCK * r, BLOCK)
            g_k[rows, lanes(p)] = turn(m.dk[rows], m.turns[0, rows], m.turns[1, rows], -1.0).astype(LOW)
            g_v[rows, lanes(p)] = m.dv[rows].astype(LOW)

    def grad_qkv():
        @pl.loop(0, width // BLOCK, unroll=True)
        def _(t):
            rows = block(t)
            got = dot_rows(m.n1[:, rows], g_qkv[...]).astype(LOW)
            for n, name in enumerate((QUERY, KEY, VALUE)):
                m.grad[name][rows] = got[:, n * half : (n + 1) * half]

    def part_n1():
        @pl.loop(0, CHIPS, unroll=True)
        def _(chip):
            m.swap_out[chip] = dot_cols(g_qkv[half_block(chip, 1 - core)], m.w_qkv[...]).astype(LOW)

        swap(1).start()

    def own_n1():
        swap(1).wait()

        @pl.loop(0, CHIPS, unroll=True)
        def _(chip):
            rows = half_block(chip, core)
            got = dot_cols(g_qkv[rows], m.w_qkv[...]) + m.swap_in[1, chip].astype(F32)
            x = m.x[rows].astype(F32)
            inv = inverse_rms(x)
            m.hold[0, 0:1] += jnp.sum(got * x * inv, axis=0, keepdims=True)
            a1 = got * gain_attn[...][None]
            inner = jnp.mean(a1 * x, axis=-1, keepdims=True)
            m.swap_out[chip] = (g_mid[rows] + inv * (a1 - x * (inv * inv * inner))).astype(LOW)

    steps = {
        GRAD_DOWN: grad_down, PART_OUT: part_out, GRAD_N2: grad_n2, OWN_OUT: own_out, GRAD_MID: grad_mid,
        GRAD_OUT: grad_out, GRAD_ATT: grad_att, GRAD_QKV: grad_qkv, PART_N1: part_n1, OWN_N1: own_n1,
        SEND_OUT: back_out.start, SEND_X: back_x.start,
    }

    def do(name):
        if name <= SMALL:
            advance(name)
        else:
            steps[name]()

    def looped(body, first, last):
        gaps = [[]]
        for name in ORDER[ORDER.index(first) + 1 : ORDER.index(last)]:
            if first < name < last:
                gaps.append([])
            else:
                gaps[-1].append(name)

        @pl.loop(0, last - first + 1)
        def _(n):
            body(n)
            for at, gap in enumerate(gaps):
                if gap:

                    @pl.when(n == at)
                    def _():
                        for name in gap:
                            do(name)

    at = 0
    while at < len(ORDER):
        name = ORDER[at]
        if name == TILE0:
            looped(tile, TILE0, TILE3)
            at = ORDER.index(TILE3)
        elif name == HEADS0:
            looped(heads, HEADS0, HEADS2)
            at = ORDER.index(HEADS2)
        else:
            do(name)
        at += 1

    for total in sums:
        total.stage6()
    for p in range(pairs):
        att_copy(p).wait_send()
    for r in range(CHIPS):
        gn2_copy(r).wait_send()
    gather_x.drain()
    back_out.drain()
    back_x.drain()
    back_out.arrived()
    back_x.arrived()


def vmem_specs(count):
    return [pl.BlockSpec(memory_space=pltpu.VMEM)] * count


def any_specs(count):
    return [pl.BlockSpec(memory_space=pl.ANY)] * count


def finish_kernel(lengths, *refs):
    step = pl.program_id(0)
    blk = lax.axis_index(BAND)
    tiles, refs = refs[:CHIPS], refs[CHIPS:]
    down, output, query, key, value, out, back, small = refs[:8]
    r_out, r_back, r_query, r_key, r_value, r_output, r_gate, r_up, r_down, r_gain_attn, r_gain_ffn = refs[8:]
    for src, dst in ((query, r_query), (key, r_key), (value, r_value), (output, r_output)):
        cols = src.shape[-1]
        for c in range(CORES):
            dst[:, c * cols : (c + 1) * cols] = src[c].astype(F32)
    for t, src in enumerate(tiles):
        for c in range(CORES):
            cols = pl.ds((t * CORES + c) * BLOCK, BLOCK)
            r_up[:, cols] = src[c, :, :BLOCK].astype(F32)
            r_gate[:, cols] = src[c, :, BLOCK:].astype(F32)
    r_back[...] = back[...]
    gains = pltpu.roll(small[...], (CHIPS - blk) * (small.shape[1] // CHIPS), 1)
    r_gain_attn[...] = gains[0, : r_gain_attn.shape[0]]
    r_gain_ffn[...] = gains[1, : r_gain_ffn.shape[0]]
    r_down[...] = down[0].astype(F32).T
    rows = out.shape[1]
    for i in range(2):
        place_ = blk * BLOCK + step * rows + lax.broadcasted_iota(jnp.int32, out.shape[1:], 0)
        r_out[i] = jnp.where(place_ < lengths[i], out[i].astype(F32), 0.0).astype(LOW)


def item_layer(
    tokens, cotangent, lengths, w_query, w_key, w_value, w_output, w_gate, w_up, w_down, gain_attn, gain_ffn
):
    width = tokens.shape[2]
    ff = w_gate.shape[1] // CORES
    half = width // 2
    keep, sems, results = layout(width, ff)
    scratch, tree = jax.tree.flatten((keep, sems))
    cosine, sine = turn_tables(CHIPS * BLOCK, width // HEADS)
    band = jax.ShapeDtypeStruct(tokens.shape, LOW)
    fins = pl.pallas_call(
        functools.partial(layer_kernel, tree),
        out_shape=[jax.ShapeDtypeStruct(shape, LOW) for shape in results]
        + [jax.ShapeDtypeStruct((8, width), F32), band, band],
        in_specs=any_specs(2) + [pl.BlockSpec(memory_space=pltpu.SMEM)] + any_specs(1)
        + vmem_specs(2) + any_specs(7),
        out_specs=any_specs(SMALL) + vmem_specs(1) + any_specs(2),
        scratch_shapes=scratch,
        compiler_params=pltpu.CompilerParams(
            collective_id=0, has_side_effects=True, vmem_limit_bytes=VMEM_BYTES
        ),
    )(
        tokens, cotangent, lengths, jnp.stack([cosine, sine]), gain_attn, gain_ffn,
        w_query, w_key, w_value, w_output, w_gate, w_up, w_down,
    )
    *sums, small, out_band, x_band = fins
    sums = [t.reshape(CORES, -1, t.shape[-1]) for t in sums]
    steps = 2
    rows = half // 2
    unit = ff // CHIPS

    def grad_spec(cols):
        return pl.BlockSpec((CORES, rows // steps, cols), lambda s: (0, s, 0))

    def wide_spec(cols):
        return pl.BlockSpec((rows // steps, cols), lambda s: (s, 0))

    band_spec = pl.BlockSpec((2, BLOCK // steps, width), lambda s: (0, s, 0))
    wide = lambda cols: jax.ShapeDtypeStruct((rows, cols), F32)
    output, g_tokens, g_query, g_key, g_value, g_output, g_gate, g_up, g_down, *gains = pl.pallas_call(
        finish_kernel,
        grid=(steps,),
        out_shape=[band] * 2 + [wide(width)] * 4 + [wide(2 * ff)] * 2
        + [jax.ShapeDtypeStruct((CORES * unit, width), F32)]
        + [jax.ShapeDtypeStruct((width // CHIPS,), F32)] * 2,
        in_specs=[pl.BlockSpec(memory_space=pltpu.SMEM)]
        + [grad_spec(2 * unit)] * CHIPS
        + [pl.BlockSpec((1, width, unit), lambda s: (s, 0, 0))] + [grad_spec(half)] * 4 + [band_spec] * 2
        + [pl.BlockSpec((8, width), lambda s: (0, 0))],
        out_specs=[band_spec] * 2 + [wide_spec(width)] * 4 + [wide_spec(2 * ff)] * 2
        + [pl.BlockSpec((unit, width), lambda s: (s, 0))]
        + [pl.BlockSpec((width // CHIPS,), lambda s: (0,))] * 2,
        compiler_params=pltpu.CompilerParams(vmem_limit_bytes=VMEM_BYTES),
    )(lengths, *sums, out_band, x_band, small)
    return (output, g_tokens, g_query, g_key, g_value, g_output, g_gate, g_up, g_down, *gains)


VMEM_BYTES = 65 << 20


def turn_tables(length, head_dim):
    half_dim = head_dim // 2
    steps = np.arange(half_dim, dtype=np.float32) * np.float32(-2.0 * math.log(10000.0) / head_dim)
    angles = np.arange(length, dtype=np.float32)[:, None] * np.exp(steps)[None, :]
    cosine, sine = np.cos(angles), np.sin(angles)
    return (
        np.concatenate([cosine] * 4, axis=1).astype(np.float32),
        np.concatenate([-sine, sine, -sine, sine], axis=1).astype(np.float32),
    )


def solution(mesh):
    layer = item_layer if dict(mesh.shape) == {ITEM: 8, BAND: 4} else band_layer
    placed = (
        P("dp", "blk", None),
        P("dp", "blk", None),
        P("dp"),
        P(),
        P(),
        P(),
        P(),
        P(),
        P(),
        P(),
        P(),
        P(),
    )
    return jax.shard_map(
        layer,
        mesh=mesh,
        in_specs=placed,
        out_specs=(
            P("dp", "blk", None),
            P("dp", "blk", None),
            P("blk", None),
            P("blk", None),
            P("blk", None),
            P("blk", None),
            P("blk", None),
            P("blk", None),
            P("blk", None),
            P("blk"),
            P("blk"),
        ),
        check_vma=False,
    )
```

```python
import functools
import math
from types import SimpleNamespace

import jax
import jax.numpy as jnp
import numpy as np
from jax import lax
from jax.experimental import pallas as pl
from jax.experimental.pallas import tpu as pltpu
from jax.sharding import PartitionSpec as P

HEADS = 12


epsilon = 1e-05
masked_value = -1e30


def shifted(value, axis, by):
    size = lax.axis_size(axis)
    pairs = [(i, i + by) for i in range(size) if 0 <= i + by < size]
    return lax.ppermute(value, axis, pairs)


def tables(positions, head_dim):
    half_dim = head_dim // 2
    frequency = jnp.exp(
        jnp.arange(half_dim, dtype=jnp.float32) * (-2.0 * math.log(10000.0) / head_dim)
    )
    angles = positions[:, None] * frequency[None, :]
    return (jnp.cos(angles), jnp.sin(angles))


def rotate(tensor, cosine_table, sine_table):
    half_dim = tensor.shape[-1] // 2
    first = tensor[..., :half_dim]
    second = tensor[..., half_dim:]
    cosine_b = cosine_table[:, None, :]
    sine_b = sine_table[:, None, :]
    return jnp.concatenate(
        [first * cosine_b - second * sine_b, first * sine_b + second * cosine_b], axis=-1
    )


def contract_rows(left, right):
    return lax.dot_general(
        left, right, (((0,), (0,)), ((), ())), preferred_element_type=jnp.float32
    )


def times_transposed(left, right):
    return lax.dot_general(
        left, right, (((1,), (1,)), ((), ())), preferred_element_type=jnp.float32
    )


def band_layer(
    tokens,
    cotangent,
    lengths,
    w_query,
    w_key,
    w_value,
    w_output,
    w_gate,
    w_up,
    w_down,
    gain_attn,
    gain_ffn,
):
    item_count, band_len, model_width = tokens.shape
    head_count = HEADS
    head_dim = model_width // head_count
    band_count = lax.axis_size("blk")
    band_index = lax.axis_index("blk")
    seq_len = band_len * band_count
    row_count = item_count * band_len
    score_scale = head_dim ** (-0.5)
    positions = band_index * band_len + jnp.arange(band_len, dtype=jnp.int32)
    valid_rows = (positions[None, :] < lengths[:, None]).astype(jnp.float32).reshape(row_count, 1)
    cosine_table, sine_table = tables(positions.astype(jnp.float32), head_dim)
    key_positions = jnp.arange(seq_len, dtype=jnp.int32)
    allowed = key_positions[None, :] <= positions[:, None]
    incoming = tokens.astype(jnp.float32).reshape(row_count, model_width)
    inv_one = lax.rsqrt(jnp.mean(incoming * incoming, axis=-1, keepdims=True) + epsilon)
    normed_one = (incoming * inv_one * gain_attn).astype(jnp.bfloat16)
    query = rotate(
        jnp.dot(normed_one, w_query, preferred_element_type=jnp.float32).reshape(
            item_count, band_len, head_count, head_dim
        ),
        cosine_table,
        sine_table,
    ).astype(jnp.bfloat16)
    key_own = rotate(
        jnp.dot(normed_one, w_key, preferred_element_type=jnp.float32).reshape(
            item_count, band_len, head_count, head_dim
        ),
        cosine_table,
        sine_table,
    ).astype(jnp.bfloat16)
    value_own = jnp.dot(normed_one, w_value, preferred_element_type=jnp.float32).astype(
        jnp.bfloat16
    )
    pair = jnp.concatenate(
        [
            key_own.reshape(item_count, band_len, model_width),
            value_own.reshape(item_count, band_len, model_width),
        ],
        axis=-1,
    )
    buffer = jnp.zeros((item_count, band_count, band_len, 2 * model_width), jnp.bfloat16)
    buffer = lax.dynamic_update_slice_in_dim(buffer, pair[:, None], band_index, 1)

    def cycle_step(turn_index, state):
        carried, buffer = state
        carried = shifted(carried, "blk", 1)
        source = band_index - turn_index
        placed = lax.dynamic_update_slice_in_dim(
            buffer, carried[:, None], jnp.maximum(source, 0), 1
        )
        buffer = jnp.where(source >= 0, placed, buffer)
        return (carried, buffer)

    _, buffer = lax.fori_loop(1, band_count, cycle_step, (pair, buffer))
    whole = buffer.reshape(item_count, seq_len, 2 * model_width)
    keys_all = whole[..., :model_width].reshape(item_count, seq_len, head_count, head_dim)
    values_all = whole[..., model_width:].reshape(item_count, seq_len, head_count, head_dim)
    scores = (
        jnp.einsum("iqhd,ikhd->ihqk", query, keys_all, preferred_element_type=jnp.float32)
        * score_scale
    )
    scores = jnp.where(allowed[None, None], scores, masked_value)
    highest_s = jnp.max(scores, axis=-1, keepdims=True)
    expo = jnp.exp(scores - highest_s)
    totals = jnp.sum(expo, axis=-1, keepdims=True)
    softmax_w = expo / totals
    attended = jnp.einsum(
        "ihqk,ikhd->iqhd",
        softmax_w.astype(jnp.bfloat16),
        values_all,
        preferred_element_type=jnp.float32,
    )
    attended = attended.astype(jnp.bfloat16).reshape(row_count, model_width)
    middle = incoming + jnp.dot(attended, w_output, preferred_element_type=jnp.float32)
    inv_two = lax.rsqrt(jnp.mean(middle * middle, axis=-1, keepdims=True) + epsilon)
    normed_two = (middle * inv_two * gain_ffn).astype(jnp.bfloat16)
    gate_pre = jnp.dot(normed_two, w_gate, preferred_element_type=jnp.float32)
    up_pre = jnp.dot(normed_two, w_up, preferred_element_type=jnp.float32)
    sigmoid_g = jax.nn.sigmoid(gate_pre)
    silu_g = gate_pre * sigmoid_g
    hidden = (silu_g * up_pre).astype(jnp.bfloat16)
    ffn_out = jnp.dot(hidden, w_down, preferred_element_type=jnp.float32)
    result = (middle + ffn_out) * valid_rows
    output = result.astype(jnp.bfloat16).reshape(item_count, band_len, model_width)
    grad_res = cotangent.astype(jnp.float32).reshape(row_count, model_width) * valid_rows
    grad_ffn = grad_res.astype(jnp.bfloat16)
    grad_down = contract_rows(hidden, grad_ffn)
    grad_hidden = times_transposed(grad_ffn, w_down)
    grad_gate_pre = (
        grad_hidden * up_pre * (sigmoid_g * (1.0 + gate_pre * (1.0 - sigmoid_g)))
    ).astype(jnp.bfloat16)
    grad_up_pre = (grad_hidden * silu_g).astype(jnp.bfloat16)
    grad_gate = contract_rows(normed_two, grad_gate_pre)
    grad_up = contract_rows(normed_two, grad_up_pre)
    grad_normed_two = times_transposed(grad_gate_pre, w_gate) + times_transposed(grad_up_pre, w_up)
    grad_gain_ffn = jnp.sum(grad_normed_two * middle * inv_two, axis=0)
    scaled_two = grad_normed_two * gain_ffn
    grad_middle = grad_res + inv_two * (
        scaled_two
        - middle * inv_two * inv_two * jnp.mean(scaled_two * middle, axis=-1, keepdims=True)
    )
    grad_branch = grad_middle.astype(jnp.bfloat16)
    grad_output = contract_rows(attended, grad_branch)
    grad_attended = (
        times_transposed(grad_branch, w_output)
        .astype(jnp.bfloat16)
        .reshape(item_count, band_len, head_count, head_dim)
    )
    again = (
        jnp.einsum("iqhd,ikhd->ihqk", query, keys_all, preferred_element_type=jnp.float32)
        * score_scale
    )
    again = jnp.where(allowed[None, None], again, masked_value)
    probable = jnp.exp(again - highest_s) / totals
    grad_probs = jnp.einsum(
        "iqhd,ikhd->ihqk", grad_attended, values_all, preferred_element_type=jnp.float32
    )
    row_delta = jnp.sum(probable * grad_probs, axis=-1, keepdims=True)
    grad_scores = (probable * (grad_probs - row_delta)).astype(jnp.bfloat16)
    grad_query = (
        jnp.einsum("ihqk,ikhd->iqhd", grad_scores, keys_all, preferred_element_type=jnp.float32)
        * score_scale
    )
    grad_values = jnp.einsum(
        "ihqk,iqhd->ikhd",
        probable.astype(jnp.bfloat16),
        grad_attended,
        preferred_element_type=jnp.float32,
    )
    grad_keys = (
        jnp.einsum("ihqk,iqhd->ikhd", grad_scores, query, preferred_element_type=jnp.float32)
        * score_scale
    )
    grad_pair = jnp.concatenate(
        [
            grad_keys.reshape(item_count, seq_len, model_width),
            grad_values.reshape(item_count, seq_len, model_width),
        ],
        axis=-1,
    )
    blocks = grad_pair.reshape(item_count, band_count, band_len, 2 * model_width)
    empty_block = jnp.zeros((item_count, band_len, 2 * model_width), jnp.float32)

    def block_of(index):
        picked = lax.dynamic_index_in_dim(blocks, jnp.maximum(index, 0), 1, keepdims=False)
        return jnp.where(index >= 0, picked, empty_block)

    def cycle_back(turn_index, carried):
        carried = shifted(carried.astype(jnp.bfloat16), "blk", -1).astype(carried.dtype)
        return carried + block_of(band_index - (band_count - 1) + turn_index)

    own_grads = lax.fori_loop(1, band_count, cycle_back, block_of(band_index - (band_count - 1)))
    grad_key_own = own_grads[..., :model_width].reshape(item_count, band_len, head_count, head_dim)
    grad_value_raw = (
        own_grads[..., model_width:].astype(jnp.bfloat16).reshape(row_count, model_width)
    )
    grad_key_raw = (
        rotate(grad_key_own, cosine_table, -sine_table)
        .astype(jnp.bfloat16)
        .reshape(row_count, model_width)
    )
    grad_query_raw = (
        rotate(grad_query, cosine_table, -sine_table)
        .astype(jnp.bfloat16)
        .reshape(row_count, model_width)
    )
    grad_wquery = contract_rows(normed_one, grad_query_raw)
    grad_wkey = contract_rows(normed_one, grad_key_raw)
    grad_wvalue = contract_rows(normed_one, grad_value_raw)
    grad_normed_one = (
        times_transposed(grad_query_raw, w_query)
        + times_transposed(grad_key_raw, w_key)
        + times_transposed(grad_value_raw, w_value)
    )
    grad_gain_attn = jnp.sum(grad_normed_one * incoming * inv_one, axis=0)
    scaled_one = grad_normed_one * gain_attn
    grad_incoming = grad_middle + inv_one * (
        scaled_one
        - incoming * inv_one * inv_one * jnp.mean(scaled_one * incoming, axis=-1, keepdims=True)
    )
    grad_tokens = grad_incoming.astype(jnp.bfloat16).reshape(item_count, band_len, model_width)
    summed = (
        lax.psum_scatter(
            grad_wquery.astype(jnp.bfloat16), "blk", scatter_dimension=0, tiled=True
        ).astype(jnp.float32),
        lax.psum_scatter(
            grad_wkey.astype(jnp.bfloat16), "blk", scatter_dimension=0, tiled=True
        ).astype(jnp.float32),
        lax.psum_scatter(
            grad_wvalue.astype(jnp.bfloat16), "blk", scatter_dimension=0, tiled=True
        ).astype(jnp.float32),
        lax.psum_scatter(
            grad_output.astype(jnp.bfloat16), "blk", scatter_dimension=0, tiled=True
        ).astype(jnp.float32),
        lax.psum_scatter(
            grad_gate.astype(jnp.bfloat16), "blk", scatter_dimension=0, tiled=True
        ).astype(jnp.float32),
        lax.psum_scatter(
            grad_up.astype(jnp.bfloat16), "blk", scatter_dimension=0, tiled=True
        ).astype(jnp.float32),
        lax.psum_scatter(
            grad_down.astype(jnp.bfloat16), "blk", scatter_dimension=0, tiled=True
        ).astype(jnp.float32),
        lax.psum_scatter(
            grad_gain_attn.astype(jnp.bfloat16), "blk", scatter_dimension=0, tiled=True
        ).astype(jnp.float32),
        lax.psum_scatter(
            grad_gain_ffn.astype(jnp.bfloat16), "blk", scatter_dimension=0, tiled=True
        ).astype(jnp.float32),
    )
    summed = (
        lax.psum(summed[0].astype(jnp.bfloat16), "dp").astype(jnp.float32),
        lax.psum(summed[1].astype(jnp.bfloat16), "dp").astype(jnp.float32),
        lax.psum(summed[2].astype(jnp.bfloat16), "dp").astype(jnp.float32),
        lax.psum(summed[3].astype(jnp.bfloat16), "dp").astype(jnp.float32),
        lax.psum(summed[4].astype(jnp.bfloat16), "dp").astype(jnp.float32),
        lax.psum(summed[5].astype(jnp.bfloat16), "dp").astype(jnp.float32),
        lax.psum(summed[6].astype(jnp.bfloat16), "dp").astype(jnp.float32),
        lax.psum(summed[7].astype(jnp.bfloat16), "dp").astype(jnp.float32),
        lax.psum(summed[8].astype(jnp.bfloat16), "dp").astype(jnp.float32),
    )
    return (
        output,
        grad_tokens,
        summed[0],
        summed[1],
        summed[2],
        summed[3],
        summed[4],
        summed[5],
        summed[6],
        summed[7],
        summed[8],
    )


MESH = pl.DeviceIdType.MESH
ITEM, BAND = "dp", "blk"
CORES = 2
CHIPS = 4
BLOCK = 256
PAIR = 128
LOW = jnp.bfloat16
F32 = jnp.float32


def place():
    dp = lax.axis_index(ITEM)
    return dp, lax.axis_index(BAND), lax.rem(dp, CORES)


def near(dp, blk, core=0, chip=0, line=0):
    flip = core + CORES * line
    return {ITEM: dp ^ flip if flip else dp, BAND: blk ^ chip if chip else blk}


def greet(dp, blk, flips):
    barrier = pltpu.get_barrier_semaphore()
    for flip in flips:
        pl.semaphore_signal(barrier, inc=1, device_id=near(dp, blk, *flip), device_id_type=MESH)
    return barrier


def remote(src, dst, send, recv, where):
    return pltpu.make_async_remote_copy(
        src_ref=src, dst_ref=dst, send_sem=send, recv_sem=recv, device_id=where, device_id_type=MESH
    )


def part(start, size):
    return pl.ds(pl.multiple_of(start, size), size)


PLANE = [(core, chip, 0) for chip in range(CHIPS) for core in range(CORES) if core or chip]
REACH = PLANE + [(0, 0, 1), (0, 0, 3)]


def plus(one, other, kind=LOW):
    return (one.astype(F32) + other.astype(F32)).astype(kind)


class Gather:
    SEMS = [(2,), (4, 2), (4,), (4,), (4,)]

    def __init__(self, band, buf, sems):
        self.band, self.buf = band, buf
        self.own, self.send, self.recv, self.fsend, self.frecv = sems
        self.dp, self.blk, self.core = place()
        self.rows = band.shape[1]
        self.half = self.rows // 2
        self.mine = (self.blk // 2) == self.core

    def out(self, r, h):
        target = self.blk ^ r
        return remote(
            self.band.at[lax.rem(target, 2), pl.ds(h * self.half, self.half)],
            self.buf.at[part(self.blk * self.rows + h * self.half, self.half)],
            self.send.at[r, h],
            self.recv.at[r],
            {ITEM: self.dp - self.core + h, BAND: target},
        )

    def across(self, r):
        rows = self.buf.at[part((self.blk ^ r) * self.rows + self.core * self.half, self.half)]
        return remote(rows, rows, self.fsend.at[r], self.frecv.at[r], near(self.dp, self.blk, 1))

    def here(self):
        rows = self.buf.at[part(self.blk * self.rows, self.rows)]
        return pltpu.make_async_copy(self.band.at[lax.rem(self.blk, 2)], rows, self.own.at[0])

    def there(self):
        rows = self.buf.at[part(self.blk * self.rows, self.rows)]
        src = self.band.at[lax.rem(self.blk, 2)]
        return remote(src, rows, self.fsend.at[0], self.frecv.at[0], near(self.dp, self.blk, 1))

    def sends(self, r):
        return ((self.blk ^ r) // 2) == self.core

    def start(self):
        for r in (1, 2, 3):

            @pl.when(self.sends(r))
            def _():
                for h in range(2):
                    self.out(r, h).start()

        @pl.when(self.mine)
        def _():
            self.here().start()
            self.there().start()

    def forward(self, r):
        self.out(r, 0).wait_recv()
        self.across(r).start()

    def ready(self, r):
        if r:
            self.across(r).wait_recv()
            return

        @pl.when(self.mine)
        def _():
            self.here().wait()

        @pl.when(jnp.logical_not(self.mine))
        def _():
            self.there().wait_recv()

    def drain(self):
        @pl.when(self.mine)
        def _():
            self.there().wait_send()

        for r in (1, 2, 3):
            self.across(r).wait_send()

            @pl.when(self.sends(r))
            def _():
                for h in range(2):
                    self.out(r, h).wait_send()


class Return:
    SEMS = [(1,), (4,), (2, 2)]

    def __init__(self, src, band, sems):
        self.src, self.band = src, band
        self.own, self.send, self.recv = sems
        self.dp, self.blk, self.core = place()
        self.half = src.shape[1]
        self.home = self.blk // 2

    def slot(self):
        return self.band.at[lax.rem(self.blk, 2), part(self.core * self.half, self.half)]

    def out(self, r):
        chip = self.blk ^ r
        return remote(
            self.src.at[chip],
            self.slot(),
            self.send.at[r],
            self.recv.at[lax.rem(self.blk, 2), self.core],
            {ITEM: self.dp - self.core + self.home, BAND: chip},
        )

    def keep(self):
        return pltpu.make_async_copy(self.src.at[self.blk], self.slot(), self.own.at[0])

    def start(self):
        for r in (3, 1, 2):
            self.out(r).start()

        @pl.when(self.home == self.core)
        def _():
            self.keep().start()

        @pl.when(self.home != self.core)
        def _():
            self.out(0).start()

    def drain(self):
        @pl.when(self.home == self.core)
        def _():
            self.keep().wait()

        @pl.when(self.home != self.core)
        def _():
            self.out(0).wait_send()

        for r in (1, 2, 3):
            self.out(r).wait_send()

    def arrived(self):
        for i in range(2):
            for h in range(2):
                local = (self.core * 2 + i == self.blk) & (self.core == h)

                @pl.when(jnp.logical_not(local))
                def _():
                    remote(
                        self.src.at[0],
                        self.band.at[i, pl.ds(h * self.half, self.half)],
                        self.send.at[0],
                        self.recv.at[i, h],
                        near(self.dp, self.blk, 1),
                    ).wait_recv()


class Line:
    def locate(self):
        self.dp, self.blk, self.core = place()
        z = self.dp // CORES
        self.outer = (z == 0) | (z == 3)
        self.inner = jnp.logical_not(self.outer)

    def stage(self, n):
        (self.stage0, self.stage1, self.stage2, self.stage3, self.stage4, self.stage5, self.stage6)[n]()


class Chunk(Line):
    SEMS = [(2, 2, 2), (2, 2), (3, 2, 2), (2, 3)]

    def __init__(self, src, buffers, result, sems, turned=False):
        self.src, self.result, self.turned = src, result, turned
        self.first, self.second, self.line = buffers
        self.s1, self.s2, self.sz, self.sc = sems
        self.locate()

    @staticmethod
    def shapes(rows, cols, turned):
        half = (rows // 2, cols // CHIPS) if turned else (rows // CHIPS // 2, cols)
        return [(2, 2) + half, (2,) + half, (2, 2) + half], (CORES, 2) + half

    def piece(self, chip, h):
        rows, cols = self.first.shape[2:]
        if self.turned:
            return self.src.at[pl.ds(h * rows, rows), part(chip * cols, cols)]
        return self.src.at[part(chip * 2 * rows + h * rows, rows)]

    def ways(self, h):
        return (1, 2) if h == 0 else (2, 1)

    def step1(self, h, n):
        near_way, far_way = self.ways(h)
        chip = self.blk ^ near_way ^ (far_way if n else 0)
        return remote(
            self.piece(chip, h), self.first.at[h, n], self.s1.at[0, h, n], self.s1.at[1, h, n],
            near(self.dp, self.blk, 0, near_way),
        )

    def step2(self, h):
        return remote(
            self.first.at[h, 1], self.second.at[h], self.s2.at[0, h], self.s2.at[1, h],
            near(self.dp, self.blk, 0, self.ways(h)[1]),
        )

    def hop(self, n, h):
        src = (self.second.at[h], self.line.at[0, h], self.second.at[h])[n]
        dst = self.line.at[1 if n == 1 else 0, h]
        return remote(
            src, dst, self.sz.at[n, h, 0], self.sz.at[n, h, 1],
            near(self.dp, self.blk, 0, 0, 3 if n == 1 else 1),
        )

    def share(self, total, h):
        slot = self.result.at[self.core, h]
        return (
            remote(total, slot, self.sc.at[h, 0], self.sc.at[h, 1], near(self.dp, self.blk, 1)),
            pltpu.make_async_copy(total, slot, self.sc.at[h, 2]),
        )

    def xy_start(self):
        for n in (1, 0):
            for h in range(2):
                self.step1(h, n).start()

    def xy_turn(self):
        for h in range(2):
            self.step1(h, 1).wait_recv()
            chip = self.blk ^ self.ways(h)[1]
            self.first[h, 1] = plus(self.first[h, 1], self.piece(chip, h)[...])
            self.step2(h).start()

    def xy_end(self, h):
        self.step1(h, 0).wait_recv()
        self.step2(h).wait_recv()
        own = plus(self.first[h, 0], self.piece(self.blk, h)[...], F32)
        self.second[h] = plus(own, self.second[h])

    def xy_drain(self):
        for h in range(2):
            for n in range(2):
                self.step1(h, n).wait_send()
            self.step2(h).wait_send()

    def stage0(self):
        self.xy_start()

    def stage1(self):
        self.xy_turn()

    def stage2(self):
        for h in range(2):
            self.xy_end(h)

            @pl.when(self.outer)
            def _():
                self.hop(0, h).start()

    def stage3(self):
        @pl.when(self.inner)
        def _():
            for h in range(2):
                self.hop(0, h).wait_recv()
                self.line[0, h] = plus(self.line[0, h], self.second[h])
                self.hop(1, h).start()

    def stage4(self):
        @pl.when(self.inner)
        def _():
            for h in range(2):
                self.hop(1, h).wait_recv()
                self.second[h] = plus(self.line[0, h], self.line[1, h])
                self.hop(2, h).start()
                for copy in self.share(self.second.at[h], h):
                    copy.start()

    def stage5(self):
        @pl.when(self.outer)
        def _():
            for h in range(2):
                self.hop(2, h).wait_recv()
                for copy in self.share(self.line.at[0, h], h):
                    copy.start()

    def stage6(self):
        for h in range(2):
            for copy in self.share(self.second.at[h], h):
                copy.wait()
        self.xy_drain()

        @pl.when(self.outer)
        def _():
            for h in range(2):
                self.hop(0, h).wait_send()

        @pl.when(self.inner)
        def _():
            for h in range(2):
                self.hop(1, h).wait_send()
                self.hop(2, h).wait_send()


class PairChunk(Chunk):
    SEMS = [(CHIPS, 2), (2, 2, 2), (2, 2), (2, 2), (3,)]

    def __init__(self, src, buffers, result, sems, turned=False):
        self.src, self.result, self.turned = src, result, turned
        self.pair, self.first, self.second, self.line, self.total = buffers
        self.sp, self.s1, self.s2, self.sz, self.sc = sems
        self.locate()
        self.kept = lax.rem((self.dp // CORES + 1) // 2, 2)

    @staticmethod
    def shapes(rows, cols, turned):
        whole = (rows // 2, cols // CHIPS) if turned else (rows // CHIPS // 2, cols)
        half = (whole[0] // 2, whole[1])
        return [(CHIPS,) + whole, (2, 2) + half, (2,) + half, (2,) + half, (2, 2) + half], (CORES, 2, 2) + half

    def share_of(self, chip, s):
        rows, cols = self.pair.shape[1:]
        if self.turned:
            return self.src.at[part(s * rows, rows), pl.ds(chip * cols, cols)]
        return self.src.at[part(chip * 2 * rows + s * rows, rows)]

    def piece(self, chip, h):
        rows = self.pair.shape[1] // 2
        return self.pair.at[chip, pl.ds(h * rows, rows)]

    def swap(self, chip):
        return remote(
            self.share_of(chip, 1 - self.kept), self.pair.at[chip], self.sp.at[chip, 0], self.sp.at[chip, 1],
            near(self.dp, self.blk, 0, 0, 1),
        )

    def middle(self):
        return remote(
            self.second, self.line, self.sz.at[0, 0], self.sz.at[0, 1], near(self.dp, self.blk, 0, 0, 3)
        )

    def hand(self):
        half = self.total.at[self.kept]
        return remote(half, half, self.sz.at[1, 0], self.sz.at[1, 1], near(self.dp, self.blk, 0, 0, 1))

    def spread(self):
        slot = self.result.at[self.core]
        return (
            remote(self.total, slot, self.sc.at[0], self.sc.at[1], near(self.dp, self.blk, 1)),
            pltpu.make_async_copy(self.total, slot, self.sc.at[2]),
        )

    def stage0(self):
        for chip in range(CHIPS):
            self.swap(chip).start()

    def stage1(self):
        for chip in range(CHIPS):
            self.swap(chip).wait_recv()
            self.pair[chip] = plus(self.pair[chip], self.share_of(chip, self.kept)[...])
        self.xy_start()

    def stage2(self):
        self.xy_turn()

    def stage3(self):
        for h in range(2):
            self.xy_end(h)
        self.middle().start()

    def stage4(self):
        self.middle().wait_recv()
        for h in range(2):
            self.total[self.kept, h] = plus(self.second[h], self.line[h])
        self.hand().start()

    def stage5(self):
        self.hand().wait_recv()
        for copy in self.spread():
            copy.start()

    def stage6(self):
        for copy in self.spread():
            copy.wait()
        for chip in range(CHIPS):
            self.swap(chip).wait_send()
        self.xy_drain()
        self.middle().wait_send()
        self.hand().wait_send()


class Small(Line):
    SEMS = [(6, 2)]
    SLOTS = 11

    def __init__(self, hold, result, sems):
        self.hold, self.result = hold, result
        (self.sem,) = sems
        self.locate()

    def go(self, n):
        flips = ((1, 0, 0), (0, 1, 0), (0, 2, 0), (0, 0, 1), (0, 0, 3), (0, 0, 1))
        src, dst = (10, 10) if n == 5 else (2 * n, 2 * n + 1)
        return remote(
            self.hold.at[src], self.hold.at[dst], self.sem.at[n, 0], self.sem.at[n, 1],
            near(self.dp, self.blk, *flips[n]),
        )

    def add(self, n, to):
        self.go(n).wait_recv()
        self.hold[to] = self.hold[2 * n] + self.hold[2 * n + 1]

    def stage0(self):
        self.go(0).start()

    def stage1(self):
        for n in range(2):
            self.add(n, 2 * n + 2)
            self.go(n + 1).start()

    def stage2(self):
        self.add(2, 6)

        @pl.when(self.outer)
        def _():
            self.go(3).start()

    def stage3(self):
        @pl.when(self.inner)
        def _():
            self.add(3, 8)
            self.go(4).start()

    def stage4(self):
        @pl.when(self.inner)
        def _():
            self.add(4, 10)
            self.go(5).start()

    def stage5(self):
        @pl.when(self.outer)
        def _():
            self.go(5).wait_recv()

        self.result[...] = self.hold[10]

    def stage6(self):
        for n in range(3):
            self.go(n).wait_send()

        @pl.when(self.outer)
        def _():
            self.go(3).wait_send()

        @pl.when(self.inner)
        def _():
            self.go(4).wait_send()
            self.go(5).wait_send()


def dot(left, right):
    return jnp.dot(left, right, preferred_element_type=F32)


def dot_rows(left, right):
    return lax.dot_general(left, right, (((0,), (0,)), ((), ())), preferred_element_type=F32)


def dot_cols(left, right):
    return lax.dot_general(left, right, (((1,), (1,)), ((), ())), preferred_element_type=F32)


def inverse_rms(values):
    return lax.rsqrt(jnp.mean(values * values, axis=-1, keepdims=True) + epsilon)


def turn(t, cosine, sine, sign):
    quarter = PAIR // 4
    lane = lax.broadcasted_iota(jnp.int32, t.shape, 1)
    other = jnp.where(
        lane % (2 * quarter) < quarter,
        pltpu.roll(t, PAIR - quarter, 1),
        pltpu.roll(t, quarter, 1),
    )
    return t * cosine + (sign * sine) * other


def both_heads(t):
    lane = lax.broadcasted_iota(jnp.int32, t.shape, 1)
    zero = jnp.zeros_like(t)
    return jnp.concatenate(
        [jnp.where(lane < PAIR // 2, t, zero), jnp.where(lane < PAIR // 2, zero, t)], axis=0
    )


def one_pair(t):
    rows = t.shape[0] // 2
    lane = lax.broadcasted_iota(jnp.int32, (rows, PAIR), 1)
    return jnp.where(lane < PAIR // 2, t[:rows], t[rows:])


FF0, FF1, FF2, FF3, DOWN, OUT, QUERY, KEY, VALUE, SMALL = range(10)
TILES = (FF0, FF1, FF2, FF3)
PAIRED = (FF2, OUT)
(
    TILE0, TILE1, TILE2, TILE3, GRAD_DOWN, PART_OUT, GRAD_N2, OWN_OUT, GRAD_MID, GRAD_OUT, GRAD_ATT,
    HEADS0, HEADS1, HEADS2, GRAD_QKV, PART_N1, OWN_N1, SEND_OUT, SEND_X,
) = range(100, 119)
ORDER = (
    TILE0, FF0, TILE1, FF1, TILE2, FF0, FF2, TILE3, FF3, PART_OUT, GRAD_N2, FF1, FF0, GRAD_DOWN, FF2, OWN_OUT, FF3,
    GRAD_MID, FF1, FF2, DOWN, GRAD_OUT, FF0, OUT, GRAD_ATT, HEADS0, HEADS1, FF1, FF3, FF0, DOWN, HEADS2, OUT, FF2,
    GRAD_QKV, VALUE, FF1, FF3, DOWN, PART_N1, OUT, VALUE, KEY, FF1, OUT, FF2, QUERY, OWN_N1, SMALL, VALUE, FF3,
    DOWN, SMALL, QUERY, OUT, KEY, FF3, SEND_X, DOWN, SEND_OUT, QUERY, VALUE, QUERY, VALUE, SMALL, KEY, VALUE, KEY,
    DOWN, SMALL, FF0, QUERY, OUT, KEY, QUERY, SMALL, FF2, KEY, SMALL,
)


def layout(width, ff):
    seq = CHIPS * BLOCK
    half = width // 2
    pairs = half // PAIR

    def low(*shape):
        return pltpu.VMEM(shape, LOW)

    def wide(*shape):
        return pltpu.VMEM(shape, F32)

    grads, sums = [], []
    keep = dict(
        w_qkv=low(width, 3 * half), w_out=low(width, width), w_ff=low(width, 2 * ff),
        w_down=low(ff, width), turns=wide(2, seq, PAIR),
        x=low(seq, width), g_ffn=low(seq, width), n1=low(seq, width),
        q=low(seq, half), k=low(seq, half), v=low(seq, half),
        prob=[low(pairs, 2 * BLOCK, (i + 1) * BLOCK) for i in range(CHIPS)],
        att=low(seq, width), middle=wide(seq, width), n2=low(seq, width), n2_turned=low(width, seq),
        hidden=low(seq, ff), g_ff=low(seq, 2 * ff), share=wide(seq, PAIR), gn2=low(seq, width),
        swap_out=low(CHIPS, BLOCK // 2, width), swap_in=low(2, CHIPS, BLOCK // 2, width),
        band=low(CHIPS, BLOCK // 2, width),
        dk=wide(seq, PAIR), dv=wide(seq, PAIR), hold=wide(Small.SLOTS, 8, width),
        grad=grads, sums=sums,
    )
    sems = dict(
        load=[(18,)], gather_x=Gather.SEMS, gather_g=Gather.SEMS, att=[(2, pairs)], swap=[(2, 2)], gn2=[(2, CHIPS)],
        back_out=Return.SEMS, back_x=Return.SEMS, small=Small.SEMS,
        sums=[PairChunk.SEMS if name in PAIRED else Chunk.SEMS for name in range(SMALL)],
    )
    sems = jax.tree.map(pltpu.SemaphoreType.DMA, sems, is_leaf=lambda t: isinstance(t, tuple))
    results = []
    for name in range(SMALL):
        cols = ff if name == DOWN else 2 * (ff // CHIPS) if name in TILES else half
        kind = PairChunk if name in PAIRED else Chunk
        shapes, result = kind.shapes(width, cols, name == DOWN)
        results.append(result)
        grads.append(low(width, cols))
        sums.append([low(*shape) for shape in shapes])
    return keep, sems, results


def layer_kernel(
    scratch, tokens, cotangent, lengths, turns, gain_attn, gain_ffn,
    w_query, w_key, w_value, w_output, w_gate, w_up, w_down, *refs,
):
    width, ff = tokens.shape[2], w_gate.shape[1] // CORES
    results, (small_result, out_band, x_band) = refs[:SMALL], refs[SMALL : SMALL + 3]
    keep, sems = jax.tree.unflatten(scratch, refs[SMALL + 3 :])
    m, sem = SimpleNamespace(**keep), SimpleNamespace(**sems)
    dp, blk, core = place()
    partner = near(dp, blk, 1)
    half = width // 2
    pairs = half // PAIR
    scale = (width // HEADS) ** (-0.5)
    mine = pl.multiple_of(core * half, half)

    def block(r):
        return part(r * BLOCK, BLOCK)

    def half_block(chip, c):
        return part(chip * BLOCK + c * (BLOCK // 2), BLOCK // 2)

    def lanes(p):
        return part(p * PAIR, PAIR)

    barrier = greet(dp, blk, REACH)

    loads = []

    def load(src, dst):
        copy = pltpu.make_async_copy(src, dst, sem.load[0].at[len(loads)])
        copy.start()
        loads.append(copy)

    stage = m.band.reshape(2, BLOCK, width)
    load(cotangent, stage)
    load(turns, m.turns)
    for n, weight in enumerate((w_query, w_key, w_value)):
        load(weight.at[:, pl.ds(mine, half)], m.w_qkv.at[:, pl.ds(n * half, half)])

    gather_x = Gather(tokens, m.x, sem.gather_x)
    gather_g = Gather(stage, m.g_ffn, sem.gather_g)
    pl.semaphore_wait(barrier, len(REACH))
    gather_x.start()
    load(w_output, m.w_out)
    unit = ff // CHIPS
    for chip in range(CHIPS):
        there = part(chip * CORES * unit + core * unit, unit)
        load(w_up.at[:, there], m.w_ff.at[:, pl.ds(2 * chip * unit, unit)])
        load(w_gate.at[:, there], m.w_ff.at[:, pl.ds((2 * chip + 1) * unit, unit)])
        load(w_down.at[there], m.w_down.at[pl.ds(chip * unit, unit)])
    for copy in loads[:5]:
        copy.wait()
    for i in range(2):
        row = blk * BLOCK + lax.broadcasted_iota(jnp.int32, (BLOCK, width), 0)
        stage[i] = jnp.where(row < lengths[i], stage[i].astype(F32), 0.0).astype(LOW)

    def project(r):
        rows = block(blk ^ r)
        x = m.x[rows].astype(F32)
        n1 = (x * inverse_rms(x) * gain_attn[...][None]).astype(LOW)
        m.n1[rows] = n1
        cosine, sine = m.turns[0, rows], m.turns[1, rows]
        for n, store in enumerate((m.q, m.k, m.v)):
            full = dot(n1, m.w_qkv[:, n * half : (n + 1) * half])
            for p in range(pairs):
                t = full[:, p * PAIR : (p + 1) * PAIR]
                if n < 2:
                    t = turn(t, cosine, sine, 1.0)
                if n == 0:
                    t = t.astype(LOW).astype(F32) * scale
                store[rows, p * PAIR : (p + 1) * PAIR] = t.astype(LOW)

    gather_x.ready(0)
    project(0)
    gather_x.forward(1)
    gather_x.forward(2)
    gather_x.ready(1)
    gather_x.forward(3)
    gather_g.start()
    project(1)
    gather_x.ready(2)
    project(2)
    gather_x.ready(3)
    project(3)

    row = lax.broadcasted_iota(jnp.int32, (2 * BLOCK, BLOCK), 0) % BLOCK
    seen = lax.broadcasted_iota(jnp.int32, (2 * BLOCK, BLOCK), 1) <= row

    lane = lax.broadcasted_iota(jnp.int32, (BLOCK, PAIR), 1)

    def att_cols(p):
        return part(core * half + p * PAIR, PAIR)

    def att_copy(p):
        cols = m.att.at[:, att_cols(p)]
        return remote(cols, cols, sem.att[0].at[0, p], sem.att[0].at[1, p], partner)

    def scores(p, i):
        size = BLOCK * i
        q = both_heads(m.q[pl.ds(size, BLOCK), lanes(p)])
        score = dot_cols(q, m.k[pl.ds(0, size + BLOCK), lanes(p)])
        own = jnp.where(seen, score[:, size:], masked_value)
        return jnp.concatenate([score[:, :size], own], axis=1) if i else own

    def attend(p, i, prob):
        rows = pl.ds(BLOCK * i, BLOCK)
        v = m.v[pl.ds(0, BLOCK * (i + 1)), lanes(p)]
        both = dot(prob, jnp.concatenate([v, jnp.ones_like(v)], axis=1))
        att, share = both[:, :PAIR], 1.0 / both[:, PAIR:]
        kept = jnp.where(lane == 2 * p, share[:BLOCK], m.share[rows])
        m.share[rows] = jnp.where(lane == 2 * p + 1, share[BLOCK:], kept)
        m.att[rows, att_cols(p)] = one_pair(att * share).astype(LOW)

    @pl.loop(0, pairs)
    def _(p):
        later = scores(p, 0)
        for i in range(CHIPS):
            score = later
            if i + 1 < CHIPS:
                later = scores(p, i + 1)
            slabs = [score[:, n : n + PAIR] for n in range(0, BLOCK * (i + 1), PAIR)]
            top = jnp.max(functools.reduce(jnp.maximum, slabs), axis=-1, keepdims=True)
            if i:
                attend(p, i - 1, prob)
            prob = jnp.exp(score - top).astype(LOW)
            m.prob[i][p] = prob
        attend(p, CHIPS - 1, prob)
        att_copy(p).start()

    for r in (1, 2, 3):
        gather_g.forward(r)
    loads[5].wait()

    @pl.loop(0, CHIPS, unroll=True)
    def _(r):
        rows = block(r)
        m.middle[rows] = m.x[rows].astype(F32) + dot(m.att[rows, pl.ds(mine, half)], m.w_out[pl.ds(mine, half)])

    for p in range(pairs):
        att_copy(p).wait_recv()
    theirs = pl.multiple_of((1 - core) * half, half)

    @pl.loop(0, CHIPS, unroll=True)
    def _(r):
        rows = block(r)
        middle = m.middle[rows] + dot(m.att[rows, pl.ds(theirs, half)], m.w_out[pl.ds(theirs, half)])
        m.middle[rows] = middle
        n2 = (middle * inverse_rms(middle) * gain_ffn[...][None]).astype(LOW)
        m.n2[rows] = n2
        m.n2_turned[:, rows] = n2.T

    for r in range(CHIPS):
        gather_g.ready(r)
    for copy in loads[6:]:
        copy.wait()

    sums = []
    for name in range(SMALL):
        own = (m.grad[name], m.sums[name], results[name], sem.sums[name])
        sums.append((PairChunk if name in PAIRED else Chunk)(*own, name == DOWN))
    sums.append(Small(m.hold, small_result, sem.small))
    done = [0] * len(sums)

    def advance(*names):
        for name in names:
            sums[name].stage(done[name])
            done[name] += 1

    def tile(t):
        units, both = block(t), part(t * 2 * BLOCK, 2 * BLOCK)

        @pl.loop(0, CHIPS, unroll=True)
        def _(r):
            rows = block(r)
            pre = dot(m.n2[rows], m.w_ff[:, both])
            up, gate = pre[:, :BLOCK], pre[:, BLOCK:]
            g_hidden = dot_cols(m.g_ffn[rows], m.w_down[units])
            sig = 0.5 * jnp.tanh(0.5 * gate) + 0.5
            silu = gate * sig
            m.hidden[rows, units] = (silu * up).astype(LOW)
            m.g_ff[rows, part(t * 2 * BLOCK, BLOCK)] = (g_hidden * silu).astype(LOW)
            g_gate = g_hidden * up * (sig * (1.0 + gate * (1.0 - sig)))
            m.g_ff[rows, part(t * 2 * BLOCK + BLOCK, BLOCK)] = g_gate.astype(LOW)

        for name in TILES:

            @pl.when(t == name)
            def _():
                for r in range(width // BLOCK):
                    rows = pl.ds(r * BLOCK, BLOCK)
                    m.grad[name][rows] = dot(m.n2_turned[rows], m.g_ff[:, both]).astype(LOW)

    def grad_down():
        @pl.loop(0, width // BLOCK, unroll=True)
        def _(t):
            rows = block(t)
            m.grad[DOWN][rows] = dot_rows(m.g_ffn[:, rows], m.hidden[...]).astype(LOW)

    def swap(n):
        return remote(m.swap_out, m.swap_in.at[n], sem.swap[0].at[n, 0], sem.swap[0].at[n, 1], partner)

    def part_out():
        @pl.loop(0, CHIPS, unroll=True)
        def _(chip):
            m.swap_out[chip] = dot(m.hidden[half_block(chip, 1 - core)], m.w_down[...]).astype(LOW)

        swap(0).start()

    back_out = Return(m.band, out_band, sem.back_out)
    back_x = Return(m.swap_out, x_band, sem.back_x)

    def own_out():
        swap(0).wait()
        gather_g.drain()

        @pl.loop(0, CHIPS, unroll=True)
        def _(chip):
            rows = half_block(chip, core)
            out = dot(m.hidden[rows], m.w_down[...]) + m.swap_in[0, chip].astype(F32)
            m.band[chip] = (m.middle[rows] + out).astype(LOW)

    def gn2_copy(r):
        return remote(
            m.n2.at[block(r)], m.gn2.at[block(r)], sem.gn2[0].at[0, r], sem.gn2[0].at[1, r], partner,
        )

    def grad_n2():
        @pl.loop(0, CHIPS, unroll=True)
        def _(r):
            m.n2[block(r)] = dot_cols(m.g_ff[block(r)], m.w_ff[...]).astype(LOW)
            gn2_copy(r).start()

    g_branch, g_mid = m.gn2, m.middle

    def grad_mid():
        m.hold[0] = jnp.zeros((8, width), F32)

        @pl.loop(0, CHIPS, unroll=True)
        def _(r):
            rows = block(r)
            gn2_copy(r).wait_recv()
            g_n2 = plus(m.n2[rows], m.gn2[rows], F32)
            middle = m.middle[rows]
            inv = inverse_rms(middle)
            m.hold[0, 1:2] += 0.5 * jnp.sum(g_n2 * middle * inv, axis=0, keepdims=True)
            a2 = g_n2 * gain_ffn[...][None]
            inner = jnp.mean(a2 * middle, axis=-1, keepdims=True)
            got = m.g_ffn[rows].astype(F32) + inv * (a2 - middle * (inv * inv * inner))
            g_branch[rows] = got.astype(LOW)
            g_mid[rows] = got

    def grad_out():
        @pl.loop(0, width // BLOCK, unroll=True)
        def _(t):
            rows = block(t)
            m.grad[OUT][rows] = dot_rows(m.att[:, rows], g_branch[:, pl.ds(mine, half)]).astype(LOW)

    g_att = m.hidden
    g_qkv = m.g_ff.at[:, pl.ds(0, 3 * half)]
    g_q, g_k, g_v = (m.g_ff.at[:, pl.ds(n * half, half)] for n in range(3))

    def grad_att():
        @pl.loop(0, CHIPS, unroll=True)
        def _(r):
            g_att[block(r), pl.ds(0, half)] = dot_cols(g_branch[block(r)], m.w_out[pl.ds(mine, half)]).astype(LOW)

    def heads(p):
        for i in range(CHIPS - 1, -1, -1):
            rows, size = pl.ds(BLOCK * i, BLOCK), BLOCK * (i + 1)
            past = pl.ds(0, size)
            kept = m.share[rows]
            share = jnp.concatenate(
                [
                    jnp.sum(jnp.where(lane == 2 * p + n, kept, 0.0), axis=-1, keepdims=True)
                    for n in range(2)
                ],
                axis=0,
            )
            g = both_heads(g_att[rows, lanes(p)]).astype(F32) * share
            q = both_heads(m.q[rows, lanes(p)])
            out = m.att[rows, att_cols(p)].astype(F32)
            delta = jnp.sum(g * jnp.concatenate([out, out], axis=0), axis=-1, keepdims=True)
            g = g.astype(LOW)
            prob = m.prob[i][p]
            g_prob = dot_cols(g, m.v[past, lanes(p)])
            g_score = (prob.astype(F32) * (g_prob - delta)).astype(LOW)
            got_q = one_pair(dot(g_score, m.k[past, lanes(p)])) * scale
            g_q[rows, lanes(p)] = turn(got_q, m.turns[0, rows], m.turns[1, rows], -1.0).astype(LOW)
            got_k, got_v = dot_rows(g_score, q), dot_rows(prob, g)
            if i == CHIPS - 1:
                m.dk[...] = got_k
                m.dv[...] = got_v
            else:
                m.dk[past] += got_k
                m.dv[past] += got_v
        for r in range(CHIPS):
            rows = pl.ds(BLOCK * r, BLOCK)
            g_k[rows, lanes(p)] = turn(m.dk[rows], m.turns[0, rows], m.turns[1, rows], -1.0).astype(LOW)
            g_v[rows, lanes(p)] = m.dv[rows].astype(LOW)

    def grad_qkv():
        @pl.loop(0, width // BLOCK, unroll=True)
        def _(t):
            rows = block(t)
            got = dot_rows(m.n1[:, rows], g_qkv[...]).astype(LOW)
            for n, name in enumerate((QUERY, KEY, VALUE)):
                m.grad[name][rows] = got[:, n * half : (n + 1) * half]

    def part_n1():
        @pl.loop(0, CHIPS, unroll=True)
        def _(chip):
            m.swap_out[chip] = dot_cols(g_qkv[half_block(chip, 1 - core)], m.w_qkv[...]).astype(LOW)

        swap(1).start()

    def own_n1():
        swap(1).wait()

        @pl.loop(0, CHIPS, unroll=True)
        def _(chip):
            rows = half_block(chip, core)
            got = dot_cols(g_qkv[rows], m.w_qkv[...]) + m.swap_in[1, chip].astype(F32)
            x = m.x[rows].astype(F32)
            inv = inverse_rms(x)
            m.hold[0, 0:1] += jnp.sum(got * x * inv, axis=0, keepdims=True)
            a1 = got * gain_attn[...][None]
            inner = jnp.mean(a1 * x, axis=-1, keepdims=True)
            m.swap_out[chip] = (g_mid[rows] + inv * (a1 - x * (inv * inv * inner))).astype(LOW)

    steps = {
        GRAD_DOWN: grad_down, PART_OUT: part_out, GRAD_N2: grad_n2, OWN_OUT: own_out, GRAD_MID: grad_mid,
        GRAD_OUT: grad_out, GRAD_ATT: grad_att, GRAD_QKV: grad_qkv, PART_N1: part_n1, OWN_N1: own_n1,
        SEND_OUT: back_out.start, SEND_X: back_x.start,
    }

    def do(name):
        if name <= SMALL:
            advance(name)
        else:
            steps[name]()

    def looped(body, first, last):
        gaps = [[]]
        for name in ORDER[ORDER.index(first) + 1 : ORDER.index(last)]:
            if first < name < last:
                gaps.append([])
            else:
                gaps[-1].append(name)

        @pl.loop(0, last - first + 1)
        def _(n):
            body(n)
            for at, gap in enumerate(gaps):
                if gap:

                    @pl.when(n == at)
                    def _():
                        for name in gap:
                            do(name)

    at = 0
    while at < len(ORDER):
        name = ORDER[at]
        if name == TILE0:
            looped(tile, TILE0, TILE3)
            at = ORDER.index(TILE3)
        elif name == HEADS0:
            looped(heads, HEADS0, HEADS2)
            at = ORDER.index(HEADS2)
        else:
            do(name)
        at += 1

    for total in sums:
        total.stage6()
    for p in range(pairs):
        att_copy(p).wait_send()
    for r in range(CHIPS):
        gn2_copy(r).wait_send()
    gather_x.drain()
    back_out.drain()
    back_x.drain()
    back_out.arrived()
    back_x.arrived()


def vmem_specs(count):
    return [pl.BlockSpec(memory_space=pltpu.VMEM)] * count


def any_specs(count):
    return [pl.BlockSpec(memory_space=pl.ANY)] * count


def finish_kernel(lengths, *refs):
    step = pl.program_id(0)
    blk = lax.axis_index(BAND)
    tiles, refs = refs[:CHIPS], refs[CHIPS:]
    down, output, query, key, value, out, back, small = refs[:8]
    r_out, r_back, r_query, r_key, r_value, r_output, r_gate, r_up, r_down, r_gain_attn, r_gain_ffn = refs[8:]
    for src, dst in ((query, r_query), (key, r_key), (value, r_value), (output, r_output)):
        cols = src.shape[-1]
        for c in range(CORES):
            dst[:, c * cols : (c + 1) * cols] = src[c].astype(F32)
    for t, src in enumerate(tiles):
        for c in range(CORES):
            cols = pl.ds((t * CORES + c) * BLOCK, BLOCK)
            r_up[:, cols] = src[c, :, :BLOCK].astype(F32)
            r_gate[:, cols] = src[c, :, BLOCK:].astype(F32)
    r_back[...] = back[...]
    gains = pltpu.roll(small[...], lax.rem(CHIPS - blk, CHIPS) * (small.shape[1] // CHIPS), 1)
    r_gain_attn[...] = gains[0, : r_gain_attn.shape[0]]
    r_gain_ffn[...] = gains[1, : r_gain_ffn.shape[0]]
    r_down[...] = down[0].astype(F32).T
    rows = out.shape[1]
    for i in range(2):
        place_ = blk * BLOCK + step * rows + lax.broadcasted_iota(jnp.int32, out.shape[1:], 0)
        r_out[i] = jnp.where(place_ < lengths[i], out[i].astype(F32), 0.0).astype(LOW)


def item_layer(
    tokens, cotangent, lengths, w_query, w_key, w_value, w_output, w_gate, w_up, w_down, gain_attn, gain_ffn
):
    width = tokens.shape[2]
    ff = w_gate.shape[1] // CORES
    half = width // 2
    keep, sems, results = layout(width, ff)
    scratch, tree = jax.tree.flatten((keep, sems))
    cosine, sine = turn_tables(CHIPS * BLOCK, width // HEADS)
    band = jax.ShapeDtypeStruct(tokens.shape, LOW)
    fins = pl.pallas_call(
        functools.partial(layer_kernel, tree),
        out_shape=[jax.ShapeDtypeStruct(shape, LOW) for shape in results]
        + [jax.ShapeDtypeStruct((8, width), F32), band, band],
        in_specs=any_specs(2) + [pl.BlockSpec(memory_space=pltpu.SMEM)] + any_specs(1)
        + vmem_specs(2) + any_specs(7),
        out_specs=any_specs(SMALL) + vmem_specs(1) + any_specs(2),
        scratch_shapes=scratch,
        compiler_params=pltpu.CompilerParams(
            collective_id=0, has_side_effects=True, vmem_limit_bytes=VMEM_BYTES
        ),
    )(
        tokens, cotangent, lengths, jnp.stack([cosine, sine]), gain_attn, gain_ffn,
        w_query, w_key, w_value, w_output, w_gate, w_up, w_down,
    )
    *sums, small, out_band, x_band = fins
    sums = [t.reshape(CORES, -1, t.shape[-1]) for t in sums]
    steps = 2
    rows = half // 2
    unit = ff // CHIPS

    def grad_spec(cols):
        return pl.BlockSpec((CORES, rows // steps, cols), lambda s: (0, s, 0))

    def wide_spec(cols):
        return pl.BlockSpec((rows // steps, cols), lambda s: (s, 0))

    band_spec = pl.BlockSpec((2, BLOCK // steps, width), lambda s: (0, s, 0))
    wide = lambda cols: jax.ShapeDtypeStruct((rows, cols), F32)
    output, g_tokens, g_query, g_key, g_value, g_output, g_gate, g_up, g_down, *gains = pl.pallas_call(
        finish_kernel,
        grid=(steps,),
        out_shape=[band] * 2 + [wide(width)] * 4 + [wide(2 * ff)] * 2
        + [jax.ShapeDtypeStruct((CORES * unit, width), F32)]
        + [jax.ShapeDtypeStruct((width // CHIPS,), F32)] * 2,
        in_specs=[pl.BlockSpec(memory_space=pltpu.SMEM)]
        + [grad_spec(2 * unit)] * CHIPS
        + [pl.BlockSpec((1, width, unit), lambda s: (s, 0, 0))] + [grad_spec(half)] * 4 + [band_spec] * 2
        + [pl.BlockSpec((8, width), lambda s: (0, 0))],
        out_specs=[band_spec] * 2 + [wide_spec(width)] * 4 + [wide_spec(2 * ff)] * 2
        + [pl.BlockSpec((unit, width), lambda s: (s, 0))]
        + [pl.BlockSpec((width // CHIPS,), lambda s: (0,))] * 2,
        compiler_params=pltpu.CompilerParams(vmem_limit_bytes=VMEM_BYTES),
    )(lengths, *sums, out_band, x_band, small)
    return (output, g_tokens, g_query, g_key, g_value, g_output, g_gate, g_up, g_down, *gains)


VMEM_BYTES = 65 << 20


def turn_tables(length, head_dim):
    half_dim = head_dim // 2
    steps = np.arange(half_dim, dtype=np.float32) * np.float32(-2.0 * math.log(10000.0) / head_dim)
    angles = np.arange(length, dtype=np.float32)[:, None] * np.exp(steps)[None, :]
    cosine, sine = np.cos(angles), np.sin(angles)
    return (
        np.concatenate([cosine] * 4, axis=1).astype(np.float32),
        np.concatenate([-sine, sine, -sine, sine], axis=1).astype(np.float32),
    )


def solution(mesh):
    layer = item_layer if dict(mesh.shape) == {ITEM: 8, BAND: 4} else band_layer
    placed = (
        P("dp", "blk", None),
        P("dp", "blk", None),
        P("dp"),
        P(),
        P(),
        P(),
        P(),
        P(),
        P(),
        P(),
        P(),
        P(),
    )
    return jax.shard_map(
        layer,
        mesh=mesh,
        in_specs=placed,
        out_specs=(
            P("dp", "blk", None),
            P("dp", "blk", None),
            P("blk", None),
            P("blk", None),
            P("blk", None),
            P("blk", None),
            P("blk", None),
            P("blk", None),
            P("blk", None),
            P("blk"),
            P("blk"),
        ),
        check_vma=False,
    )
```
